128 devices in a mesh: gx: 16 (over z, x_hi, core), gy: 8 (over y, x_lo).
Axes of the slice: x: 4 (x_hi: 2, x_lo: 2; x = x_hi * 2 + x_lo), y: 4, z: 4, core: 2. Of those that a mesh axis runs over, the one named last changes fastest.
Arguments:
- pressure: float32 [256, 128, 512], P('gx', 'gy'), may hold values from -6 to 6
- divergence: float32 [256, 128, 512], P('gx', 'gy'), may hold values from -8 to 8
- inverse_density: float32 [256, 128, 512], P('gx', 'gy'), may hold values from 0.2 to 5
Outputs:
- new_pressure: float32 [256, 128, 512], P('gx', 'gy')
The draws below stay inside these ranges and needn't reach their ends.
All inputs are finite; a program needn't handle non-finite values.
Results may differ from the reference program's by a relative error of at most 0.000021.
Values sent between devices are 32-bit elements; how exact they have to be, the bound alone decides.
A program may use at most 320 MiB of HBM per device.

```python
import math
import jax
import jax.numpy as jnp

NZ = 512
CHEB = 2
COARSE = 4
NX = 256
NY = 128


def draw_divergence(key, part):
    rough = jax.random.normal(key, (NX, NY, NZ), jnp.float32)
    return jnp.clip(rough, -8.0, 8.0)


def levels(stream_key, extent, cuts, low, high):
    def one(axis_at, parts):
        heights = jax.random.uniform(jax.random.fold_in(jax.random.fold_in(stream_key, 6), axis_at), (parts,), jnp.float32, low / len(cuts), high / len(cuts))
        return jnp.repeat(jnp.exp(heights), extent[axis_at] // parts).reshape((-1,) + (1,) * (len(extent) - axis_at - 1))

    level = one(*cuts[0])
    for cut in cuts[1:]:
        level = level * one(*cut)
    return level


def normal_values(stream_key, shape, scale, most, pieces=(), kind=jnp.bfloat16):
    gain = levels(stream_key, shape, pieces, -0.22, 0.18) if pieces else 1.0
    drawn = jax.random.normal(stream_key, shape, jnp.float32) * scale * gain
    return jnp.minimum(jnp.maximum(drawn, -most), most).astype(kind)


def setup_inputs(seed: int = 0) -> dict:
    keys = jax.random.split(jax.random.key(seed), 4)
    return {
        "pressure": normal_values(keys[0], (NX, NY, NZ), 1.0, 6.0, ((0, 16), (1, 8)), jnp.float32),
        "divergence": draw_divergence(jax.random.fold_in(keys[3], 71), 0),
        "inverse_density": jnp.clip(jnp.exp(math.log(5.0) - 3.218876 * jax.random.uniform(keys[2], (NX, NY, NZ), jnp.float32) ** levels(keys[2], (NX, NY, NZ), ((0, 16), (1, 8)), -0.2, 0.2)), 0.2, 5.0),
    }


shift_fine = 0.05
bound_low = 0.3
bound_high = 2.0
jacobi_weight = 0.8
stencil_weights = (0.0, 0.5, 0.125, 0.0625)
weight_total = 5.0
face_offsets = [(1, 0, 0), (-1, 0, 0), (0, 1, 0), (0, -1, 0), (0, 0, 1), (0, 0, -1)]
neighbour_offsets = [(offset_x, offset_y, offset_z) for offset_x in (-1, 0, 1) for offset_y in (-1, 0, 1) for offset_z in (-1, 0, 1) if (offset_x, offset_y, offset_z) != (0, 0, 0)]


def neighbour(values, offsets):
    return jnp.roll(values, (-offsets[0], -offsets[1], -offsets[2]), (0, 1, 2))


def operate_seven(values, mobility, shift_value):
    summed = shift_value * values
    for offsets in face_offsets:
        summed = summed + 0.5 * (mobility + neighbour(mobility, offsets)) * (values - neighbour(values, offsets))
    return summed


def diag_seven(mobility, shift_value):
    summed = shift_value + jnp.zeros_like(mobility)
    for offsets in face_offsets:
        summed = summed + 0.5 * (mobility + neighbour(mobility, offsets))
    return summed


def operate_full(values, mobility, shift_value):
    summed = shift_value * values
    for offsets in neighbour_offsets:
        weight = stencil_weights[abs(offsets[0]) + abs(offsets[1]) + abs(offsets[2])]
        summed = summed + weight * 0.5 * (mobility + neighbour(mobility, offsets)) * (values - neighbour(values, offsets))
    return summed


def diag_full(mobility, shift_value):
    summed = shift_value + jnp.zeros_like(mobility)
    for offsets in neighbour_offsets:
        weight = stencil_weights[abs(offsets[0]) + abs(offsets[1]) + abs(offsets[2])]
        summed = summed + weight * 0.5 * (mobility + neighbour(mobility, offsets))
    return summed


def restrict(values):
    shape = values.shape
    return values.reshape(shape[0] // 2, 2, shape[1] // 2, 2, shape[2] // 2, 2).mean(axis=(1, 3, 5))


def prolong(values):
    return jnp.repeat(jnp.repeat(jnp.repeat(values, 2, 0), 2, 1), 2, 2)


def chebyshev(iterate, source, mobility, shift_value, zero_start, need_residual):
    midpoint = (bound_high + bound_low) / 2
    halfwidth = (bound_high - bound_low) / 2
    sigma_ratio = midpoint / halfwidth
    ratio_prev = 1.0 / sigma_ratio
    inverse = 1.0 / diag_seven(mobility, shift_value)
    if zero_start:
        residual = source
    else:
        residual = source - operate_seven(iterate, mobility, shift_value)
    update = inverse * residual / midpoint
    iterate = update if zero_start else iterate + update
    for repeat in range(1, CHEB):
        residual = residual - operate_seven(update, mobility, shift_value)
        ratio_next = 1.0 / (2.0 * sigma_ratio - ratio_prev)
        update = ratio_next * ratio_prev * update + (2.0 * ratio_next / halfwidth) * inverse * residual
        ratio_prev = ratio_next
        iterate = iterate + update
    if need_residual:
        residual = residual - operate_seven(update, mobility, shift_value)
    return iterate, residual


def reference(pressure, divergence, inverse_density):
    mob_fine = inverse_density
    fine, fine_res = chebyshev(pressure, divergence, mob_fine, shift_fine, False, True)
    mob_mid = restrict(mob_fine)
    source_mid = 4.0 * restrict(fine_res)
    middle_it, middle_res = chebyshev(source_mid, source_mid, mob_mid, 4.0 * shift_fine, True, True)
    mob_low = restrict(mob_mid)
    source_low = 4.0 * restrict(middle_res)
    coarse_shift = 16.0 * shift_fine
    weighted = jacobi_weight / diag_full(mob_low, coarse_shift)
    coarse = weighted * source_low
    for repeat in range(COARSE - 1):
        coarse = coarse + weighted * (source_low - operate_full(coarse, mob_low, coarse_shift))
    mean_src = jnp.mean(source_low)
    mean_cor = jnp.mean(coarse)
    mean_mob = jnp.mean(mob_low)
    coarse = coarse + jacobi_weight * (mean_src - coarse_shift * mean_cor) / (coarse_shift + weight_total * mean_mob)
    middle_it, unused = chebyshev(middle_it + prolong(coarse), source_mid, mob_mid, 4.0 * shift_fine, False, False)
    fine, unused = chebyshev(fine + prolong(middle_it), divergence, mob_fine, shift_fine, False, False)
    return fine
```

```python
import functools

import jax
import jax.numpy as jnp
from jax import lax
from jax.experimental import pallas as pl
from jax.experimental.pallas import tpu as pltpu
from jax.sharding import PartitionSpec as P

MESH = pl.DeviceIdType.MESH
F32 = jnp.float32
BF16 = jnp.bfloat16

S1 = 0.05
S2 = 0.2
S3 = 0.8
MIDPOINT = (2.0 + 0.3) / 2
HALFWIDTH = (2.0 - 0.3) / 2
SIGMA = MIDPOINT / HALFWIDTH
P1 = 1.0 / SIGMA
P2 = 1.0 / (2.0 * SIGMA - P1)
CA = P2 * P1
CB = 2.0 * P2 / HALFWIDTH
NEAR = [(-1, 0), (1, 0), (0, -1), (0, 1), (-1, -1), (-1, 1), (1, -1), (1, 1)]


def thirds(x):
    high = x.astype(BF16)
    rest = x - high.astype(F32)
    middle = rest.astype(BF16)
    low = (rest - middle.astype(F32)).astype(BF16)
    return high, middle, low


def exact_dot(x, matrix):
    total = None
    for part in thirds(x):
        term = jnp.dot(part, matrix, preferred_element_type=F32)
        total = term if total is None else total + term
    return total


def z_next(v):
    half = v.shape[1] // 2
    return jnp.concatenate([v[:, half:], pltpu.roll(v[:, :half], half - 1, 1)], axis=1)


def z_before(v):
    half = v.shape[1] // 2
    return jnp.concatenate([pltpu.roll(v[:, half:], 1, 1), v[:, :half]], axis=1)


def weighted_sum(f):
    q = pltpu.roll(f, 1, 2) + pltpu.roll(f, f.shape[2] - 1, 2)
    face = 0.5 * f + 0.125 * q
    edge = 0.125 * f + 0.0625 * q
    rows = f.shape[1]
    a = 0.5 * q + (pltpu.roll(face, 1, 1) + pltpu.roll(face, rows - 1, 1))
    b = face + (pltpu.roll(edge, 1, 1) + pltpu.roll(edge, rows - 1, 1))
    return a[1:-1] + (b[:-2] + b[2:])


def coarse_operator(v, mob, mob_sum):
    c = v[1:-1]
    m = mob[1:-1]
    return S3 * c + 0.5 * (
        5.0 * m * c - m * weighted_sum(v) + c * mob_sum - weighted_sum(mob * v)
    )


def kernel(
    nx, ny,
    p_hbm, d_hbm, m_hbm, o_hbm,
    px, mf, u, u2, d, r, out, kx, kyl, kyh, kz, w,
    ystage, yrecv, pair, rs, tmat, pmat, pin, pout,
    mid_b, mid_stage, mid_rx, mid_ry, mid_rc, b2, m2, w2, kx2, kyl2, kyh2, kz2,
    va, vb, rr, x2, xk,
    cstage, crecv, cm, cw, cb, ce, t2,
    fstage, frecv, fk,
    ar1, ar2,
    in_sem, out_sem, fs, fr, ms, mr, cs, cr, xs, xr, as1, ar1s, as2, ar2s,
):
    gx = lax.axis_index("gx")
    gy = lax.axis_index("gy")

    def device(ox, oy):
        return (lax.rem(gx + (ox % nx), nx), lax.rem(gy + (oy % ny), ny))

    peers = {(o, 0) for o in range(1, nx)} | {(0, o) for o in range(1, ny)}
    peers |= {(dx % nx, dy % ny) for dx, dy in NEAR}
    peers = sorted(peers - {(0, 0)})

    loads = [
        pltpu.make_async_copy(m_hbm, mf.at[1:17, 8:24, :], in_sem.at[0]),
        pltpu.make_async_copy(p_hbm, px.at[1:17, 8:24, :], in_sem.at[1]),
        pltpu.make_async_copy(d_hbm, d, in_sem.at[2]),
    ]
    for c in loads:
        c.start()
    barrier = pltpu.get_barrier_semaphore()
    for ox, oy in peers:
        pl.semaphore_signal(barrier, inc=1, device_id=device(ox, oy), device_id_type=MESH)

    zi = lax.broadcasted_iota(jnp.int32, tmat.shape, 0)
    ci = lax.broadcasted_iota(jnp.int32, tmat.shape, 1)
    hit = (zi >> 1) == (((ci & 127) << 1) + (ci >> 7))
    tmat[...] = jnp.where(hit, 1.0, 0.0).astype(BF16)
    zi = lax.broadcasted_iota(jnp.int32, pmat.shape, 1)
    ci = lax.broadcasted_iota(jnp.int32, pmat.shape, 0)
    hit = (zi >> 1) == (((ci & 127) << 1) + (ci >> 7))
    pmat[...] = jnp.where(hit, 1.0, 0.0).astype(BF16)
    pl.semaphore_wait(barrier, len(peers))

    def remote(src, dst, ssem, rsem, ox, oy):
        return pltpu.make_async_remote_copy(
            src_ref=src, dst_ref=dst, send_sem=ssem, recv_sem=rsem,
            device_id=device(ox, oy), device_id_type=MESH,
        )

    def fine_send(arr, n):
        for x in range(16):
            ystage[n, 0, x : x + 1, :] = arr[x + 1, 8:9, :]
            ystage[n, 1, x : x + 1, :] = arr[x + 1, 23:24, :]
        copies = [
            remote(arr.at[1, 8:24, :], arr.at[17, 8:24, :], fs.at[n, 0], fr.at[n, 0], -1, 0),
            remote(arr.at[16, 8:24, :], arr.at[0, 8:24, :], fs.at[n, 1], fr.at[n, 1], 1, 0),
            remote(ystage.at[n, 0], yrecv.at[n, 1], fs.at[n, 2], fr.at[n, 2], 0, -1),
            remote(ystage.at[n, 1], yrecv.at[n, 0], fs.at[n, 3], fr.at[n, 3], 0, 1),
        ]
        for c in copies:
            c.start()
        return copies

    def fine_rows(arr, n):
        for x in range(16):
            arr[x + 1, 7:8, :] = yrecv[n, 0, x : x + 1, :]
            arr[x + 1, 24:25, :] = yrecv[n, 1, x : x + 1, :]

    def fine_wait(copies, arr, n):
        for c in copies:
            c.wait()
        fine_rows(arr, n)

    def restrict_fine(get, scale):
        def body(j, carry):
            both = get(2 * j) + get(2 * j + 1)
            for t in range(4):
                lanes = slice(128 * t, 128 * t + 128)
                pair[t] = both[:, lanes]
                rs[j, :, lanes] = pair[t, pl.ds(0, 8, stride=2), :] + pair[t, pl.ds(1, 8, stride=2), :]
            return carry

        lax.fori_loop(0, 8, body, 0)
        got = exact_dot(rs[...].reshape(64, 512), tmat[...]) * scale
        return got.reshape(8, 8, 256)

    def mid_send(n):
        low = lax.broadcasted_iota(jnp.int32, (8, 256), 0) < 4
        for t in range(4):
            a = mid_b[n, 2 * t]
            b = mid_b[n, 2 * t + 1]
            mid_stage[n, 0, t] = jnp.where(low, a, pltpu.roll(b, 4, 0))
            mid_stage[n, 1, t] = jnp.where(low, pltpu.roll(a, 4, 0), b)
        copies = [
            remote(mid_b.at[n, 0:4], mid_rx.at[n, 1], ms.at[n, 0], mr.at[n, 0], -1, 0),
            remote(mid_b.at[n, 4:8], mid_rx.at[n, 0], ms.at[n, 1], mr.at[n, 1], 1, 0),
            remote(mid_stage.at[n, 0], mid_ry.at[n, 1], ms.at[n, 2], mr.at[n, 2], 0, -1),
            remote(mid_stage.at[n, 1], mid_ry.at[n, 0], ms.at[n, 3], mr.at[n, 3], 0, 1),
        ]
        k = 4
        for i, dx in enumerate((-1, 1)):
            for j, dy in enumerate((-1, 1)):
                copies.append(
                    remote(
                        mid_stage.at[n, j, 2 * i : 2 * i + 2], mid_rc.at[n, 1 - i, 1 - j],
                        ms.at[n, k], mr.at[n, k], dx, dy,
                    )
                )
                k += 1
        for c in copies:
            c.start()
        return copies

    def mid_wait(copies, n, ext):
        for x in range(8):
            ext[4 + x, 4:12, :] = mid_b[n, x]
        for c in copies:
            c.wait()
        for i in range(2):
            for x in range(4):
                ext[12 * i + x, 4:12, :] = mid_rx[n, i, x]
            for t in range(4):
                for q in range(2):
                    ext[4 + 2 * t + q, 12 * i : 12 * i + 4, :] = mid_ry[n, i, t, 4 * q : 4 * q + 4, :]
            for j in range(2):
                for t in range(2):
                    for q in range(2):
                        ext[12 * i + 2 * t + q, 12 * j : 12 * j + 4, :] = mid_rc[
                            n, i, j, t, 4 * q : 4 * q + 4, :
                        ]

    def coarse_block(get, n, scale):
        for x in range(4):
            a = get(4 + 2 * x) + get(5 + 2 * x)
            t2[x] = (a[:, :128] + a[:, 128:]) * scale
            cstage[n, 4 * x : 4 * x + 4, :] = (
                t2[x, pl.ds(4, 4, stride=2), :] + t2[x, pl.ds(5, 4, stride=2), :]
            )

    def coarse_send(n):
        copies = []
        for k, (dx, dy) in enumerate(NEAR):
            copies.append(
                remote(cstage.at[n], crecv.at[n, k], cs.at[n, k], cr.at[n, k], dx, dy)
            )
            copies[-1].start()
        return copies

    def coarse_wait(copies, n, ext):
        def place(dx, dy, block):
            for x in range(4):
                ext[4 * dx + 4 + x, 4 * dy + 4 : 4 * dy + 8, :] = block[4 * x : 4 * x + 4, :]

        place(0, 0, cstage.at[n])
        for c in copies:
            c.wait()
        for k, (dx, dy) in enumerate(NEAR):
            place(-dx, -dy, crecv.at[n, k])

    def fine_apply(arr, i, flux):
        c = arr[i + 1, 8:24, :]
        above = kx[i + 1] * (c - arr[i + 2, 8:24, :])
        fz = kz[i] * (c - pltpu.roll(c, 511, 1))
        total = S1 * c + (above - flux)
        total = total + kyl[i] * (c - arr[i + 1, 7:23, :])
        total = total + kyh[i] * (c - arr[i + 1, 9:25, :])
        total = total + (fz - pltpu.roll(fz, 1, 1))
        return c, total, above

    def first_flux(arr):
        return kx[0] * (arr[0, 8:24, :] - arr[1, 8:24, :])

    def mid_apply(arr, i):
        c = arr[i]
        total = S2 * c + kx2[i] * (c - arr[i - 1]) + kx2[i + 1] * (c - arr[i + 1])
        total = total + kyl2[i] * (c - pltpu.roll(c, 1, 0))
        total = total + kyh2[i] * (c - pltpu.roll(c, 15, 0))
        fz = kz2[i] * (c - z_next(c))
        return c, total + (fz - z_before(fz))

    def planes(start, stop, body):
        lax.fori_loop(start, stop, lambda i, carry: (body(i), carry)[1], 0)

    loads[0].wait()
    m_copies = fine_send(mf, 0)
    loads[1].wait()
    p_copies = fine_send(px, 1)
    mid_b[0] = restrict_fine(lambda i: mf[i + 1, 8:24, :], 0.125)
    m2_copies = mid_send(0)
    fine_wait(m_copies, mf, 0)

    def coefficients(i, carry):
        c = mf[i + 1, 8:24, :]
        below = 0.5 * (c + mf[i, 8:24, :])
        above = 0.5 * (c + mf[i + 2, 8:24, :])
        left = 0.5 * (c + mf[i + 1, 7:23, :])
        right = 0.5 * (c + mf[i + 1, 9:25, :])
        nxt = 0.5 * (c + pltpu.roll(c, 511, 1))
        kx[i] = below
        kx[i + 1] = above
        kyl[i] = left
        kyh[i] = right
        kz[i] = nxt
        w[i] = 1.0 / (S1 + below + above + left + right + nxt + pltpu.roll(nxt, 1, 1))
        return carry

    lax.fori_loop(0, 16, coefficients, 0)
    fine_wait(p_copies, px, 1)
    loads[2].wait()

    def pass_one(i, flux):
        c, total, above = fine_apply(px, i, flux)
        res = d[i] - total
        r[i] = res
        u[i + 1, 8:24, :] = w[i] * res * (1.0 / MIDPOINT)
        return above

    lax.fori_loop(0, 16, pass_one, first_flux(px))
    u_copies = fine_send(u, 2)

    mid_wait(m2_copies, 0, m2)
    coarse_block(lambda i: m2[i], 0, 0.125)
    m3_copies = coarse_send(0)

    def mid_coefficients(i):
        c = m2[i]
        below = 0.5 * (c + m2[i - 1])
        above = 0.5 * (c + m2[i + 1])
        left = 0.5 * (c + pltpu.roll(c, 1, 0))
        right = 0.5 * (c + pltpu.roll(c, 15, 0))
        nxt = 0.5 * (c + z_next(c))
        kx2[i] = below
        kx2[i + 1] = above
        kyl2[i] = left
        kyh2[i] = right
        kz2[i] = nxt
        w2[i] = 1.0 / (S2 + below + above + left + right + nxt + z_before(nxt))

    planes(1, 15, mid_coefficients)
    fine_wait(u_copies, u, 2)

    def pass_two(i, flux):
        c, total, above = fine_apply(u, i, flux)
        res = r[i] - total
        r[i] = res
        step = CA * c + CB * w[i] * res
        u2[i + 1, 8:24, :] = step
        px[i + 1, 8:24, :] = px[i + 1, 8:24, :] + c + step
        return above

    lax.fori_loop(0, 16, pass_two, first_flux(u))
    u2_copies = fine_send(u2, 3)

    coarse_wait(m3_copies, 0, cm)
    mob = cm[...]
    mob_sum = weighted_sum(mob)
    cw[1:11] = 0.8 / (S3 + 0.5 * (5.0 * mob[1:-1] + mob_sum))
    for x in range(4):
        cstage[1, 4 * x : 4 * x + 4, :] = cw[4 + x, 4:8, :]
    w3_copies = coarse_send(1)

    def response_one(i):
        vb[i] = (-S2 / MIDPOINT) * w2[i]

    planes(1, 15, response_one)

    def response_two(i):
        c, total = mid_apply(vb, i)
        step = CA * c + CB * w2[i] * (-S2 - total)
        xk[i] = 1.0 + c + step

    planes(2, 14, response_two)
    for x in range(8):
        fk[2, x : x + 1, :] = xk[4 + x, 3:4, :]
        fk[3, x : x + 1, :] = xk[4 + x, 12:13, :]
    fk[0] = xk[3, 4:12, :]
    fk[1] = xk[12, 4:12, :]
    fine_wait(u2_copies, u2, 3)

    def residual_plane(i, flux):
        c, total, above = fine_apply(u2, i, flux)
        r[i] = r[i] - total
        return above

    lax.fori_loop(0, 16, residual_plane, first_flux(u2))
    mid_b[1] = restrict_fine(lambda i: r[i], 0.5)
    b2_copies = mid_send(1)

    coarse_wait(w3_copies, 1, cw)
    weight = cw[...]
    y = jnp.ones_like(weight)
    psi = y
    lap = weighted_sum(mob)
    for k in range(3):
        cut = k + 1
        inner = slice(k, 12 - k)
        y = y[1:-1] - coarse_operator(
            weight[inner] * y, mob[inner], lap[k : 10 - k]
        )
        psi = psi[1:-1] + y
    functional = 1.0 - S3 * (weight[4:8] * psi[1:5])
    ce[0:4] = functional
    for plane in (0, 17):
        px[plane, 8:24, :] = px[plane, 8:24, :] + u[plane, 8:24, :] + u2[plane, 8:24, :]
    yrecv[1] = yrecv[1] + yrecv[2] + yrecv[3]
    mid_wait(b2_copies, 1, b2)

    def mid_one(i):
        va[i] = w2[i] * b2[i] * (1.0 / MIDPOINT)

    planes(1, 15, mid_one)

    def mid_two(i):
        c, total = mid_apply(va, i)
        res = b2[i] - total
        step = CA * c + CB * w2[i] * res
        rr[i] = res
        vb[i] = step
        x2[i] = c + step

    planes(2, 14, mid_two)

    def mid_three(i):
        c, total = mid_apply(vb, i)
        rr[i] = rr[i] - total

    planes(4, 12, mid_three)
    coarse_block(lambda i: rr[i], 2, 0.5)
    b3_copies = coarse_send(2)

    part = jnp.zeros((1, 128), F32)
    partm = jnp.zeros((1, 128), F32)
    for x in range(4):
        part = part + jnp.sum(
            ce[x, 4:8, :] * cstage[2, 4 * x : 4 * x + 4, :], axis=0, keepdims=True
        )
        partm = partm + jnp.sum(cstage[0, 4 * x : 4 * x + 4, :], axis=0, keepdims=True)
    row = lax.broadcasted_iota(jnp.int32, (8, 128), 0)
    ar1[0] = jnp.where(row < 1, part, partm)
    sums = []
    for o in range(1, nx):
        sums.append(remote(ar1.at[0], ar1.at[o], as1.at[o], ar1s.at[o], o, 0))
        sums[-1].start()

    coarse_wait(b3_copies, 2, cb)
    rhs = cb[...]
    e = weight * rhs
    for k in range(3):
        inner = slice(k, 12 - k)
        e = e[1:-1] + weight[k + 1 : 11 - k] * (
            rhs[k + 1 : 11 - k] - coarse_operator(e, mob[inner], lap[k : 10 - k])
        )
    for c in sums:
        c.wait()
    total = ar1[0]
    for o in range(1, nx):
        total = total + ar1[o]
    ar2[0] = total
    sums = []
    for o in range(1, ny):
        sums.append(remote(ar2.at[0], ar2.at[o], as2.at[o], ar2s.at[o], 0, o))
        sums[-1].start()

    ce[3:9] = e
    for x in range(6):
        for t in range(2):
            t2[x, pl.ds(t, 8, stride=2), :] = ce[3 + x, 2:10, :]
    for x in range(6):
        v = t2[x]
        both = jnp.concatenate([v, v], axis=1)
        for q in range(2):
            va[2 + 2 * x + q] = x2[2 + 2 * x + q] + both

    def post_one(i):
        c, tot = mid_apply(va, i)
        res = b2[i] - tot
        rr[i] = res
        vb[i] = w2[i] * res * (1.0 / MIDPOINT)

    planes(3, 13, post_one)

    def post_two(i):
        c, tot = mid_apply(vb, i)
        res = rr[i] - tot
        va[i] = va[i] + c + CA * c + CB * w2[i] * res

    planes(4, 12, post_two)
    for x in range(8):
        pin[8 * x : 8 * x + 8, :] = va[4 + x, 4:12, :]
        fstage[0, x : x + 1, :] = va[4 + x, 4:5, :]
        fstage[1, x : x + 1, :] = va[4 + x, 11:12, :]
    x_copies = [
        remote(pin.at[0:8], frecv.at[1], xs.at[0], xr.at[0], -1, 0),
        remote(pin.at[56:64], frecv.at[0], xs.at[1], xr.at[1], 1, 0),
        remote(fstage.at[0], frecv.at[3], xs.at[2], xr.at[2], 0, -1),
        remote(fstage.at[1], frecv.at[2], xs.at[3], xr.at[3], 0, 1),
    ]
    for c in x_copies:
        c.start()
    for c in sums:
        c.wait()
    total = ar2[0]
    for o in range(1, ny):
        total = total + ar2[o]
    cells = 16.0 * 128.0 * nx * ny
    sum_f = jnp.sum(total[0:1, :], axis=1, keepdims=True)
    sum_m = jnp.sum(total[1:2, :], axis=1, keepdims=True)
    kappa = 0.8 * (sum_f / cells) / (S3 + 5.0 * (sum_m / cells))
    for c in x_copies:
        c.wait()
    for x in range(8):
        pin2 = pin[8 * x : 8 * x + 8, :] + kappa * xk[4 + x, 4:12, :]
        pout[8 * x : 8 * x + 8, 0:256] = pin2
    for f in range(4):
        pout[64 + 8 * f : 72 + 8 * f, 0:256] = frecv[f] + kappa * fk[f]
    grown = exact_dot(pout[:, 0:256], pmat[...])
    pout[...] = grown

    def doubled(rows, t):
        v = pout[rows, 128 * t : 128 * t + 128]
        pair[t, pl.ds(0, 8, stride=2), :] = v
        pair[t, pl.ds(1, 8, stride=2), :] = v
        return pair[t]

    def add_planes(j, carry):
        for t in range(4):
            lanes = slice(128 * t, 128 * t + 128)
            v = doubled(pl.ds(pl.multiple_of(8 * j, 8), 8), t)
            for q in range(2):
                px[2 * j + 1 + q, 8:24, lanes] = px[2 * j + 1 + q, 8:24, lanes] + v
        return carry

    lax.fori_loop(0, 8, add_planes, 0)
    for t in range(4):
        lanes = slice(128 * t, 128 * t + 128)
        for f in range(2):
            v = doubled(slice(64 + 8 * f, 72 + 8 * f), t)
            px[17 * f, 8:24, lanes] = px[17 * f, 8:24, lanes] + v
        for f in range(2):
            v = doubled(slice(80 + 8 * f, 88 + 8 * f), t)
            yrecv[1, f, :, lanes] = yrecv[1, f, :, lanes] + v
    fine_rows(px, 1)

    lax.fori_loop(0, 16, pass_one, first_flux(px))
    copies = fine_send(u, 4)
    fine_wait(copies, u, 4)

    def pass_last(i, flux):
        c, tot, above = fine_apply(u, i, flux)
        res = r[i] - tot
        out[i] = px[i + 1, 8:24, :] + c + CA * c + CB * w[i] * res
        return above

    lax.fori_loop(0, 16, pass_last, first_flux(u))
    store = pltpu.make_async_copy(out, o_hbm, out_sem.at[0])
    store.start()
    store.wait()


def solution(mesh):
    nx, ny = mesh.shape["gx"], mesh.shape["gy"]

    def local(p, d, m):
        vm = lambda *s: pltpu.VMEM(s, F32)
        sem = lambda *s: pltpu.SemaphoreType.DMA(s)
        scratch = [
            vm(18, 32, 512), vm(18, 32, 512), vm(18, 32, 512), vm(18, 32, 512),
            vm(16, 16, 512), vm(16, 16, 512), vm(16, 16, 512),
            vm(17, 16, 512), vm(16, 16, 512), vm(16, 16, 512), vm(16, 16, 512), vm(16, 16, 512),
            vm(5, 2, 16, 512), vm(5, 2, 16, 512), vm(4, 16, 128), vm(8, 8, 512),
            pltpu.VMEM((512, 256), BF16), pltpu.VMEM((256, 512), BF16), vm(64, 256), vm(96, 512),
            vm(2, 8, 8, 256), vm(2, 2, 4, 8, 256), vm(2, 2, 4, 8, 256), vm(2, 2, 4, 8, 256),
            vm(2, 2, 2, 2, 8, 256),
            vm(16, 16, 256), vm(16, 16, 256), vm(16, 16, 256), vm(17, 16, 256),
            vm(16, 16, 256), vm(16, 16, 256), vm(16, 16, 256),
            vm(16, 16, 256), vm(16, 16, 256), vm(16, 16, 256), vm(16, 16, 256), vm(16, 16, 256),
            vm(3, 16, 128), vm(3, 8, 16, 128), vm(12, 16, 128), vm(12, 16, 128), vm(12, 16, 128),
            vm(12, 16, 128), vm(6, 16, 128),
            vm(2, 8, 256), vm(4, 8, 256), vm(4, 8, 256),
            vm(nx, 8, 128), vm(ny, 8, 128),
            sem(3), sem(1), sem(5, 4), sem(5, 4), sem(2, 8), sem(2, 8), sem(3, 8), sem(3, 8),
            sem(4), sem(4), sem(nx), sem(nx), sem(ny), sem(ny),
        ]
        return pl.pallas_call(
            functools.partial(kernel, nx, ny),
            out_shape=jax.ShapeDtypeStruct((16, 16, 512), F32),
            in_specs=[pl.BlockSpec(memory_space=pl.ANY)] * 3,
            out_specs=pl.BlockSpec(memory_space=pl.ANY),
            scratch_shapes=scratch,
            compiler_params=pltpu.CompilerParams(collective_id=0, has_side_effects=True),
        )(p, d, m)

    spec = P("gx", "gy", None)
    return jax.shard_map(
        local, mesh=mesh, in_specs=(spec, spec, spec), out_specs=spec, check_vma=False
    )
```

```python
import functools

import jax
import jax.numpy as jnp
from jax import lax
from jax.experimental import pallas as pl
from jax.experimental.pallas import tpu as pltpu
from jax.sharding import PartitionSpec as P

MESH = pl.DeviceIdType.MESH
F32 = jnp.float32
BF16 = jnp.bfloat16

S1 = 0.05
S2 = 0.2
S3 = 0.8
MIDPOINT = (2.0 + 0.3) / 2
HALFWIDTH = (2.0 - 0.3) / 2
SIGMA = MIDPOINT / HALFWIDTH
P1 = 1.0 / SIGMA
P2 = 1.0 / (2.0 * SIGMA - P1)
CA = P2 * P1
CB = 2.0 * P2 / HALFWIDTH
INV = 1.0 / MIDPOINT
ALPHA = CA + CB * (MIDPOINT - 1.0)
STEP = CB * MIDPOINT
BETA = 1.0 / CB - 1.0
GAMMA = CA / CB
NEAR = [(-1, 0), (1, 0), (0, -1), (0, 1), (-1, -1), (-1, 1), (1, -1), (1, 1)]


def thirds(x):
    high = x.astype(BF16)
    rest = x - high.astype(F32)
    middle = rest.astype(BF16)
    low = (rest - middle.astype(F32)).astype(BF16)
    return high, middle, low


def exact_dot(x, matrix):
    total = None
    for part in thirds(x):
        term = jnp.dot(part, matrix, preferred_element_type=F32)
        total = term if total is None else total + term
    return total


def weighted_sum(f):
    q = pltpu.roll(f, 1, 2) + pltpu.roll(f, f.shape[2] - 1, 2)
    face = 0.5 * f + 0.125 * q
    edge = 0.125 * f + 0.0625 * q
    rows = f.shape[1]
    a = 0.5 * q + (pltpu.roll(face, 1, 1) + pltpu.roll(face, rows - 1, 1))
    b = face + (pltpu.roll(edge, 1, 1) + pltpu.roll(edge, rows - 1, 1))
    return a[1:-1] + (b[:-2] + b[2:])


def coarse_operator(v, mob, mob_sum):
    c = v[1:-1]
    m = mob[1:-1]
    return S3 * c + 0.5 * (
        5.0 * m * c - m * weighted_sum(v) + c * mob_sum - weighted_sum(mob * v)
    )


def fine_next(v):
    turned = pltpu.roll(v, 127, 2)
    lane = lax.broadcasted_iota(jnp.int32, v.shape, 2)
    return jnp.where(lane == 127, jnp.concatenate([turned[1:], turned[:1]], axis=0), turned)


def fine_before(v):
    turned = pltpu.roll(v, 1, 2)
    lane = lax.broadcasted_iota(jnp.int32, v.shape, 2)
    return jnp.where(lane == 0, jnp.concatenate([turned[3:], turned[:3]], axis=0), turned)


def mid_next(v):
    return jnp.concatenate([v[1:], pltpu.roll(v[:1], 127, 2)], axis=0)


def mid_before(v):
    return jnp.concatenate([pltpu.roll(v[1:], 1, 2), v[:1]], axis=0)


def kernel(
    nx, ny,
    p_hbm, d_hbm, m_hbm, out,
    px, mf, u, u2, d, g, dg, w, kx, ky, kz,
    xr, ys, yr, kyf, gyf, gxf, dl, rs, tmat, pmat, pout,
    mid_b, mid_stage, mid_rx, mid_ry, mid_rc, b2, m2, w2, d2, kx2, ky2, kz2,
    va, vb, rr, x2, xk,
    cstage, crecv, cm, cw, cb, ce, t2,
    base, fstage, frecv, fk,
    ar1, ar2,
    in_sem, fs, fr, ms, mr, cs, cr, xs, xrs, as1, ar1s, as2, ar2s,
):
    gx = lax.axis_index("gx")
    gy = lax.axis_index("gy")
    IN = slice(8, 24)
    LO = slice(7, 23)
    HI = slice(9, 25)

    def device(ox, oy):
        return (lax.rem(gx + (ox % nx), nx), lax.rem(gy + (oy % ny), ny))

    peers = {(o, 0) for o in range(1, nx)} | {(0, o) for o in range(1, ny)}
    peers |= {(dx % nx, dy % ny) for dx, dy in NEAR}
    peers = sorted(peers - {(0, 0)})

    loads = []
    for n, (src, dst) in enumerate(
        ((m_hbm, mf.at[1:17, :, IN, :]), (p_hbm, px.at[1:17, :, IN, :]), (d_hbm, d))
    ):
        loads.append(
            [
                pltpu.make_async_copy(
                    src.at[:, :, 128 * t : 128 * t + 128], dst.at[:, t], in_sem.at[n, t]
                )
                for t in range(4)
            ]
        )
        for c in loads[-1]:
            c.start()
    barrier = pltpu.get_barrier_semaphore()
    for ox, oy in peers:
        pl.semaphore_signal(barrier, inc=1, device_id=device(ox, oy), device_id_type=MESH)

    def remote(src, dst, ssem, rsem, ox, oy):
        return pltpu.make_async_remote_copy(
            src_ref=src, dst_ref=dst, send_sem=ssem, recv_sem=rsem,
            device_id=device(ox, oy), device_id_type=MESH,
        )

    def planes(start, stop, width, body):
        def several(j, carry):
            for q in range(width):
                body(start + width * j + q)
            return carry

        lax.fori_loop(0, (stop - start) // width, several, 0)

    zeros = jnp.zeros((4, 8, 128), F32)
    rims = (mf, px, u, u2)
    for a in rims:
        for plane in (0, 17):
            a[plane, :, 8:16, :] = zeros
            a[plane, :, 16:24, :] = zeros

    def clear(i):
        for a in rims:
            a[i + 1, :, 0:8, :] = zeros
            a[i + 1, :, 24:32, :] = zeros
        ky[i, :, 0:8, :] = zeros

    planes(0, 16, 2, clear)

    zi = lax.broadcasted_iota(jnp.int32, tmat.shape, 0)
    ci = lax.broadcasted_iota(jnp.int32, tmat.shape, 1)
    hit = (zi >> 1) == (((ci & 127) << 1) + (ci >> 7))
    tmat[...] = jnp.where(hit, 1.0, 0.0).astype(BF16)
    zi = lax.broadcasted_iota(jnp.int32, pmat.shape, 1)
    ci = lax.broadcasted_iota(jnp.int32, pmat.shape, 0)
    hit = (zi >> 1) == (((ci & 127) << 1) + (ci >> 7))
    pmat[...] = jnp.where(hit, 1.0, 0.0).astype(BF16)

    def pack_rows(arr, n):
        for x in range(16):
            ys[n, 0, :, x : x + 1, :] = arr[x + 1, :, 8:9, :]
            ys[n, 1, :, x : x + 1, :] = arr[x + 1, :, 23:24, :]

    def fine_send(arr, n):
        copies = [
            remote(arr.at[1, :, IN, :], xr.at[n, 1], fs.at[n, 0], fr.at[n, 0], -1, 0),
            remote(arr.at[16, :, IN, :], xr.at[n, 0], fs.at[n, 1], fr.at[n, 1], 1, 0),
            remote(ys.at[n, 0], yr.at[n, 1], fs.at[n, 2], fr.at[n, 2], 0, -1),
            remote(ys.at[n, 1], yr.at[n, 0], fs.at[n, 3], fr.at[n, 3], 0, 1),
        ]
        for c in copies:
            c.start()
        return copies

    def wait(copies):
        for c in copies:
            c.wait()

    def restrict_fine(arr, off, row, scale):
        for j in range(8):
            for t in range(4):
                total = None
                for q in range(2):
                    for h in range(2):
                        part = arr[2 * j + q + off, t, pl.ds(row + h, 8, stride=2), :]
                        total = part if total is None else total + part
                rs[8 * j : 8 * j + 8, 128 * t : 128 * t + 128] = total * scale
        return exact_dot(rs[...], tmat[...])

    def mid_put(n, got):
        low = lax.broadcasted_iota(jnp.int32, (2, 8, 128), 1) < 4
        blocks = []
        for x in range(8):
            rows = got[8 * x : 8 * x + 8]
            v = jnp.stack([rows[:, :128], rows[:, 128:]], axis=0)
            mid_b[n, x] = v
            blocks.append(v)
        for t in range(4):
            a, b = blocks[2 * t], blocks[2 * t + 1]
            mid_stage[n, 0, t] = jnp.where(low, a, pltpu.roll(b, 4, 1))
            mid_stage[n, 1, t] = jnp.where(low, pltpu.roll(a, 4, 1), b)

    def mid_send(n):
        copies = [
            remote(mid_b.at[n, 0:4], mid_rx.at[n, 1], ms.at[n, 0], mr.at[n, 0], -1, 0),
            remote(mid_b.at[n, 4:8], mid_rx.at[n, 0], ms.at[n, 1], mr.at[n, 1], 1, 0),
            remote(mid_stage.at[n, 0], mid_ry.at[n, 1], ms.at[n, 2], mr.at[n, 2], 0, -1),
            remote(mid_stage.at[n, 1], mid_ry.at[n, 0], ms.at[n, 3], mr.at[n, 3], 0, 1),
        ]
        k = 4
        for i, dx in enumerate((-1, 1)):
            for j, dy in enumerate((-1, 1)):
                copies.append(
                    remote(
                        mid_stage.at[n, j, 2 * i : 2 * i + 2], mid_rc.at[n, 1 - i, 1 - j],
                        ms.at[n, k], mr.at[n, k], dx, dy,
                    )
                )
                k += 1
        for c in copies:
            c.start()
        return copies

    def mid_place(n, ext):
        for i in range(2):
            for x in range(4):
                ext[12 * i + x, :, 12:20, :] = mid_rx[n, i, x]
            for t in range(4):
                for q in range(2):
                    ext[4 + 2 * t + q, :, 8 + 12 * i : 12 + 12 * i, :] = mid_ry[
                        n, i, t, :, 4 * q : 4 * q + 4, :
                    ]
            for j in range(2):
                for t in range(2):
                    for q in range(2):
                        ext[12 * i + 2 * t + q, :, 8 + 12 * j : 12 + 12 * j, :] = mid_rc[
                            n, i, j, t, :, 4 * q : 4 * q + 4, :
                        ]

    def mid_own(n, ext):
        for x in range(8):
            ext[4 + x, :, 12:20, :] = mid_b[n, x]

    def coarse_block(arr, n, row, scale):
        for x in range(4):
            total = None
            for q in range(2):
                for t in range(2):
                    for h in range(2):
                        part = arr[4 + 2 * x + q, t, pl.ds(row + h, 4, stride=2), :]
                        total = part if total is None else total + part
            cstage[n, 4 * x : 4 * x + 4, :] = total * scale

    def coarse_send(n):
        copies = []
        for k, (dx, dy) in enumerate(NEAR):
            copies.append(
                remote(cstage.at[n], crecv.at[n, k], cs.at[n, k], cr.at[n, k], dx, dy)
            )
            copies[-1].start()
        return copies

    def coarse_wait(copies, n, ext):
        def place(dx, dy, block):
            for x in range(4):
                ext[4 * dx + 4 + x, 4 * dy + 4 : 4 * dy + 8, :] = block[4 * x : 4 * x + 4, :]

        place(0, 0, cstage.at[n])
        wait(copies)
        for k, (dx, dy) in enumerate(NEAR):
            place(-dx, -dy, crecv.at[n, k])

    def fine_sum(arr, i):
        c = arr[i + 1, :, IN, :]
        z = kz[i]
        total = kx[i] * arr[i, :, IN, :] + kx[i + 1] * arr[i + 2, :, IN, :]
        total = total + ky[i, :, LO, :] * arr[i + 1, :, LO, :]
        total = total + ky[i, :, IN, :] * arr[i + 1, :, HI, :]
        return c, total + z * fine_next(c) + fine_before(z * c)

    def mid_sum(arr, i):
        c = arr[i, :, IN, :]
        z = kz2[i]
        total = kx2[i] * arr[i - 1, :, IN, :] + kx2[i + 1] * arr[i + 1, :, IN, :]
        total = total + ky2[i, :, LO, :] * arr[i, :, LO, :]
        total = total + ky2[i, :, IN, :] * arr[i, :, HI, :]
        return c, total + z * mid_next(c) + mid_before(z * c)

    def add_rows(arr, off, row):
        for x in range(16):
            for f in range(2):
                k = row + 15 * f
                arr[x + off, :, k : k + 1, :] = (
                    arr[x + off, :, k : k + 1, :] + dl[f, :, x : x + 1, :]
                )

    wait(loads[0])
    pack_rows(mf, 0)
    mid_put(0, restrict_fine(mf, 1, 8, 0.125))
    wait(loads[1])
    pack_rows(px, 1)
    wait(loads[2])
    pl.semaphore_wait(barrier, len(peers))
    m_copies = fine_send(mf, 0)
    p_copies = fine_send(px, 1)
    m2_copies = mid_send(0)

    def coefficients(i):
        c = mf[i + 1, :, IN, :]
        below = 0.5 * (c + mf[i, :, IN, :])
        above = c + mf[i + 2, :, IN, :]
        left = c + mf[i + 1, :, LO, :]
        right = 0.5 * (c + mf[i + 1, :, HI, :])
        after = 0.5 * (c + fine_next(c))
        before = c + fine_before(c)
        kx[i] = below
        ky[i, :, IN, :] = right
        kz[i] = after
        dg[i] = (S1 + below + right + after) + 0.5 * (above + left + before)

    planes(0, 16, 4, coefficients)
    kx[16] = 0.5 * mf[16, :, IN, :]

    def first_sum(i):
        c, total = fine_sum(px, i)
        g[i] = d[i] + total

    planes(0, 16, 4, first_sum)

    wait(m_copies)
    for f in range(2):
        face = 0.5 * xr[0, f]
        kx[16 * f] = kx[16 * f] + face
        dg[15 * f] = dg[15 * f] + face
        face = 0.5 * yr[0, f]
        kyf[f] = 0.5 * ys[0, f] + face
        dl[f] = face
    add_rows(dg, 0, 0)
    wait(p_copies)
    for f in range(2):
        g[15 * f] = g[15 * f] + kx[16 * f] * xr[1, f]
        dl[f] = kyf[f] * yr[1, f]
    add_rows(g, 0, 0)

    def first_step(i):
        weight = INV / dg[i]
        w[i] = weight
        u[i + 1, :, IN, :] = weight * g[i] - INV * px[i + 1, :, IN, :]

    planes(0, 16, 4, first_step)
    pack_rows(u, 2)
    u_copies = fine_send(u, 2)

    def second_sum(i):
        c, total = fine_sum(u, i)
        u2[i + 1, :, IN, :] = ALPHA * c + STEP * (w[i] * total)

    planes(0, 16, 4, second_sum)
    for x in range(16):
        for f in range(2):
            gyf[f, :, x : x + 1, :] = w[x, :, 15 * f : 15 * f + 1, :]
    for f in range(2):
        gyf[f] = STEP * (gyf[f] * kyf[f])
        gxf[f] = STEP * (w[15 * f] * kx[16 * f])
    mid_own(0, m2)
    wait(m2_copies)
    mid_place(0, m2)
    coarse_block(m2, 0, 12, 0.125)
    m3_copies = coarse_send(0)

    wait(u_copies)
    for f in range(2):
        k = 1 + 15 * f
        u2[k, :, IN, :] = u2[k, :, IN, :] + gxf[f] * xr[2, f]
        dl[f] = gyf[f] * yr[2, f]
    add_rows(u2, 1, 8)
    pack_rows(u2, 3)
    u2_copies = fine_send(u2, 3)

    def third_sum(i):
        c, total = fine_sum(u2, i)
        before = u[i + 1, :, IN, :]
        g[i] = dg[i] * (BETA * c - GAMMA * before) + total
        px[i + 1, :, IN, :] = px[i + 1, :, IN, :] + before + c

    planes(0, 16, 4, third_sum)

    def mid_coefficients(i):
        c = m2[i, :, IN, :]
        below = 0.5 * (c + m2[i - 1, :, IN, :])
        above = 0.5 * (c + m2[i + 1, :, IN, :])
        left = c + m2[i, :, LO, :]
        right = 0.5 * (c + m2[i, :, HI, :])
        after = 0.5 * (c + mid_next(c))
        before = c + mid_before(c)
        kx2[i] = below
        kx2[i + 1] = above
        ky2[i, :, IN, :] = right
        kz2[i] = after
        diagonal = (S2 + below + above + right + after) + 0.5 * (left + before)
        d2[i] = diagonal
        w2[i] = INV / diagonal

    planes(1, 15, 7, mid_coefficients)
    coarse_wait(m3_copies, 0, cm)
    mob = cm[...]
    lap = weighted_sum(mob)
    cw[1:11] = 0.8 / (S3 + 0.5 * (5.0 * mob[1:-1] + lap))
    for x in range(4):
        cstage[1, 4 * x : 4 * x + 4, :] = cw[4 + x, 4:8, :]
    w3_copies = coarse_send(1)

    wait(u2_copies)
    for f in range(2):
        g[15 * f] = g[15 * f] + kx[16 * f] * xr[3, f]
        dl[f] = kyf[f] * yr[3, f]
    add_rows(g, 0, 0)
    mid_put(1, restrict_fine(g, 0, 0, 0.5))
    b2_copies = mid_send(1)

    def response_one(i):
        vb[i, :, IN, :] = (-S2) * w2[i]

    planes(1, 15, 7, response_one)

    def response_two(i):
        c, total = mid_sum(vb, i)
        xk[i] = 1.0 + (1.0 + ALPHA) * c + STEP * (w2[i] * total)

    planes(2, 14, 6, response_two)
    for x in range(8):
        fk[2, :, x : x + 1, :] = xk[4 + x, :, 3:4, :]
        fk[3, :, x : x + 1, :] = xk[4 + x, :, 12:13, :]
    fk[0] = xk[3, :, 4:12, :]
    fk[1] = xk[12, :, 4:12, :]
    coarse_wait(w3_copies, 1, cw)
    weight = cw[...]
    y = jnp.ones_like(weight)
    psi = y
    for k in range(3):
        inner = slice(k, 12 - k)
        y = y[1:-1] - coarse_operator(weight[inner] * y, mob[inner], lap[k : 10 - k])
        psi = psi[1:-1] + y
    ce[0:4] = 1.0 - S3 * (weight[4:8] * psi[1:5])
    for f in range(2):
        xr[1, f] = xr[1, f] + xr[2, f] + xr[3, f]
        yr[1, f] = yr[1, f] + yr[2, f] + yr[3, f]
    mid_own(1, b2)
    wait(b2_copies)
    mid_place(1, b2)

    def mid_one(i):
        va[i, :, IN, :] = w2[i] * b2[i, :, IN, :]

    planes(1, 15, 7, mid_one)

    def mid_two(i):
        c, total = mid_sum(va, i)
        step = ALPHA * c + STEP * (w2[i] * total)
        vb[i, :, IN, :] = step
        x2[i] = c + step

    planes(2, 14, 6, mid_two)

    def mid_three(i):
        c, total = mid_sum(vb, i)
        rr[i] = d2[i] * (BETA * c - GAMMA * va[i, :, IN, :]) + total

    planes(4, 12, 4, mid_three)
    coarse_block(rr, 2, 4, 0.5)
    b3_copies = coarse_send(2)

    part = jnp.zeros((1, 128), F32)
    partm = jnp.zeros((1, 128), F32)
    for x in range(4):
        part = part + jnp.sum(
            ce[x, 4:8, :] * cstage[2, 4 * x : 4 * x + 4, :], axis=0, keepdims=True
        )
        partm = partm + jnp.sum(cstage[0, 4 * x : 4 * x + 4, :], axis=0, keepdims=True)
    row = lax.broadcasted_iota(jnp.int32, (8, 128), 0)
    ar1[0] = jnp.where(row < 1, part, partm)
    sums = []
    for o in range(1, nx):
        sums.append(remote(ar1.at[0], ar1.at[o], as1.at[o], ar1s.at[o], o, 0))
        sums[-1].start()

    coarse_wait(b3_copies, 2, cb)
    rhs = cb[...]
    e = weight * rhs
    for k in range(3):
        inner = slice(k, 12 - k)
        e = e[1:-1] + weight[k + 1 : 11 - k] * (
            rhs[k + 1 : 11 - k] - coarse_operator(e, mob[inner], lap[k : 10 - k])
        )
    wait(sums)
    total = ar1[0]
    for o in range(1, nx):
        total = total + ar1[o]
    ar2[0] = total
    sums = []
    for o in range(1, ny):
        sums.append(remote(ar2.at[0], ar2.at[o], as2.at[o], ar2s.at[o], 0, o))
        sums[-1].start()

    ce[3:9] = e
    for x in range(6):
        for h in range(2):
            t2[x, pl.ds(h, 8, stride=2), :] = ce[3 + x, 2:10, :]
    for x in range(6):
        v = t2[x]
        both = jnp.stack([v, v], axis=0)
        for q in range(2):
            va[2 + 2 * x + q, :, IN, :] = x2[2 + 2 * x + q] + both

    def post_one(i):
        c, total = mid_sum(va, i)
        vb[i, :, IN, :] = w2[i] * (b2[i, :, IN, :] + total) - INV * c

    planes(3, 13, 5, post_one)

    def post_two(i):
        c, total = mid_sum(vb, i)
        done = va[i, :, IN, :] + (1.0 + ALPHA) * c + STEP * (w2[i] * total)
        base[i - 4] = done[:, 4:12, :]

    planes(4, 12, 4, post_two)
    for x in range(8):
        fstage[0, :, x : x + 1, :] = base[x, :, 0:1, :]
        fstage[1, :, x : x + 1, :] = base[x, :, 7:8, :]
    x_copies = [
        remote(base.at[0], frecv.at[1], xs.at[0], xrs.at[0], -1, 0),
        remote(base.at[7], frecv.at[0], xs.at[1], xrs.at[1], 1, 0),
        remote(fstage.at[0], frecv.at[3], xs.at[2], xrs.at[2], 0, -1),
        remote(fstage.at[1], frecv.at[2], xs.at[3], xrs.at[3], 0, 1),
    ]
    for c in x_copies:
        c.start()
    wait(sums)
    total = ar2[0]
    for o in range(1, ny):
        total = total + ar2[o]
    cells = 16.0 * 128.0 * nx * ny
    sum_f = jnp.sum(total[0:1, :], axis=1, keepdims=True)
    sum_m = jnp.sum(total[1:2, :], axis=1, keepdims=True)
    kappa = 0.8 * (sum_f / cells) / (S3 + 5.0 * (sum_m / cells))

    for x in range(8):
        v = base[x] + kappa * xk[4 + x, :, 4:12, :]
        pout[8 * x : 8 * x + 8, 0:128] = v[0]
        pout[8 * x : 8 * x + 8, 128:256] = v[1]
    wait(x_copies)
    for f in range(4):
        v = frecv[f] + kappa * fk[f]
        pout[64 + 8 * f : 72 + 8 * f, 0:128] = v[0]
        pout[64 + 8 * f : 72 + 8 * f, 128:256] = v[1]
    pout[...] = exact_dot(pout[:, 0:256], pmat[...])

    for j in range(8):
        for t in range(4):
            v = pout[8 * j : 8 * j + 8, 128 * t : 128 * t + 128]
            for q in range(2):
                for h in range(2):
                    rows = pl.ds(8 + h, 8, stride=2)
                    px[2 * j + 1 + q, t, rows, :] = px[2 * j + 1 + q, t, rows, :] + v
    for t in range(4):
        lanes = slice(128 * t, 128 * t + 128)
        for f in range(2):
            for h in range(2):
                rows = pl.ds(h, 8, stride=2)
                xr[1, f, t, rows, :] = xr[1, f, t, rows, :] + pout[64 + 8 * f : 72 + 8 * f, lanes]
                yr[1, f, t, rows, :] = yr[1, f, t, rows, :] + pout[80 + 8 * f : 88 + 8 * f, lanes]
    for f in range(2):
        d[15 * f] = d[15 * f] + kx[16 * f] * xr[1, f]
        dl[f] = kyf[f] * yr[1, f]
    add_rows(d, 0, 0)

    def fourth_sum(i):
        c, total = fine_sum(px, i)
        u[i + 1, :, IN, :] = w[i] * (d[i] + total) - INV * c

    planes(0, 16, 4, fourth_sum)
    pack_rows(u, 4)
    copies = fine_send(u, 4)

    def last_sum(i):
        c, total = fine_sum(u, i)
        g[i] = px[i + 1, :, IN, :] + (1.0 + ALPHA) * c + STEP * (w[i] * total)

    planes(0, 16, 4, last_sum)
    wait(copies)
    for f in range(2):
        g[15 * f] = g[15 * f] + gxf[f] * xr[4, f]
        dl[f] = gyf[f] * yr[4, f]
    add_rows(g, 0, 0)
    for i in range(16):
        for t in range(4):
            out[i, :, 128 * t : 128 * t + 128] = g[i, t]


def solution(mesh):
    nx, ny = mesh.shape["gx"], mesh.shape["gy"]

    def local(p, d, m):
        vm = lambda *s: pltpu.VMEM(s, F32)
        sem = lambda *s: pltpu.SemaphoreType.DMA(s)
        plane = (16, 4, 16, 128)
        face = (4, 16, 128)
        scratch = [
            vm(18, 4, 32, 128), vm(18, 4, 32, 128), vm(18, 4, 32, 128), vm(18, 4, 32, 128),
            vm(*plane), vm(*plane), vm(*plane), vm(*plane),
            vm(17, 4, 16, 128), vm(16, 4, 32, 128), vm(*plane),
            vm(5, 2, *face), vm(5, 2, *face), vm(5, 2, *face),
            vm(2, *face), vm(2, *face), vm(2, *face), vm(2, *face), vm(64, 512),
            pltpu.VMEM((512, 256), BF16), pltpu.VMEM((256, 512), BF16), vm(96, 512),
            vm(2, 8, 2, 8, 128), vm(2, 2, 4, 2, 8, 128), vm(2, 2, 4, 2, 8, 128),
            vm(2, 2, 4, 2, 8, 128), vm(2, 2, 2, 2, 2, 8, 128),
            vm(16, 2, 32, 128), vm(16, 2, 32, 128), vm(16, 2, 16, 128), vm(16, 2, 16, 128),
            vm(17, 2, 16, 128), vm(16, 2, 32, 128), vm(16, 2, 16, 128),
            vm(16, 2, 32, 128), vm(16, 2, 32, 128), vm(16, 2, 16, 128), vm(16, 2, 16, 128),
            vm(16, 2, 16, 128),
            vm(3, 16, 128), vm(3, 8, 16, 128), vm(12, 16, 128), vm(12, 16, 128), vm(12, 16, 128),
            vm(12, 16, 128), vm(6, 16, 128),
            vm(8, 2, 8, 128), vm(2, 2, 8, 128), vm(4, 2, 8, 128), vm(4, 2, 8, 128),
            vm(nx, 8, 128), vm(ny, 8, 128),
            sem(3, 4), sem(5, 4), sem(5, 4), sem(2, 8), sem(2, 8), sem(3, 8), sem(3, 8),
            sem(4), sem(4), sem(nx), sem(nx), sem(ny), sem(ny),
        ]
        return pl.pallas_call(
            functools.partial(kernel, nx, ny),
            out_shape=jax.ShapeDtypeStruct((16, 16, 512), F32),
            in_specs=[pl.BlockSpec(memory_space=pl.ANY)] * 3,
            out_specs=pl.BlockSpec(memory_space=pltpu.VMEM),
            scratch_shapes=scratch,
            compiler_params=pltpu.CompilerParams(
                collective_id=0, has_side_effects=True, vmem_limit_bytes=30 * 1024 * 1024
            ),
        )(*[pltpu.with_memory_space_constraint(a, pltpu.HBM) for a in (p, d, m)])

    spec = P("gx", "gy", None)
    return jax.shard_map(
        local, mesh=mesh, in_specs=(spec, spec, spec), out_specs=spec, check_vma=False
    )
```

```python
import functools

import jax
import jax.numpy as jnp
from jax import lax
from jax.experimental import pallas as pl
from jax.experimental.pallas import tpu as pltpu
from jax.sharding import PartitionSpec as P

MESH = pl.DeviceIdType.MESH
F32 = jnp.float32
BF16 = jnp.bfloat16

S1 = 0.05
S2 = 0.2
S3 = 0.8
MIDPOINT = (2.0 + 0.3) / 2
HALFWIDTH = (2.0 - 0.3) / 2
SIGMA = MIDPOINT / HALFWIDTH
P1 = 1.0 / SIGMA
P2 = 1.0 / (2.0 * SIGMA - P1)
CA = P2 * P1
CB = 2.0 * P2 / HALFWIDTH
INV = 1.0 / MIDPOINT
ALPHA = CA + CB * (MIDPOINT - 1.0)
STEP = CB * MIDPOINT
BETA = 1.0 / CB - 1.0
GAMMA = CA / CB
NEAR = [(-1, 0), (1, 0), (0, -1), (0, 1), (-1, -1), (-1, 1), (1, -1), (1, 1)]


def thirds(x):
    high = x.astype(BF16)
    rest = x - high.astype(F32)
    middle = rest.astype(BF16)
    low = (rest - middle.astype(F32)).astype(BF16)
    return high, middle, low


def exact_dot(x, matrix):
    total = None
    for part in thirds(x):
        term = jnp.dot(part, matrix, preferred_element_type=F32)
        total = term if total is None else total + term
    return total


def weighted_sum(f):
    q = pltpu.roll(f, 1, 2) + pltpu.roll(f, f.shape[2] - 1, 2)
    face = 0.5 * f + 0.125 * q
    edge = 0.125 * f + 0.0625 * q
    rows = f.shape[1]
    a = 0.5 * q + (pltpu.roll(face, 1, 1) + pltpu.roll(face, rows - 1, 1))
    b = face + (pltpu.roll(edge, 1, 1) + pltpu.roll(edge, rows - 1, 1))
    return a[1:-1] + (b[:-2] + b[2:])


def coarse_operator(v, mob, mob_sum):
    c = v[1:-1]
    m = mob[1:-1]
    return S3 * c + 0.5 * (
        5.0 * m * c - m * weighted_sum(v) + c * mob_sum - weighted_sum(mob * v)
    )


def fine_next(v):
    turned = pltpu.roll(v, 127, 2)
    lane = lax.broadcasted_iota(jnp.int32, v.shape, 2)
    return jnp.where(lane == 127, jnp.concatenate([turned[1:], turned[:1]], axis=0), turned)


def fine_before(v):
    turned = pltpu.roll(v, 1, 2)
    lane = lax.broadcasted_iota(jnp.int32, v.shape, 2)
    return jnp.where(lane == 0, jnp.concatenate([turned[3:], turned[:3]], axis=0), turned)


def mid_next(v):
    return jnp.concatenate([v[1:], pltpu.roll(v[:1], 127, 2)], axis=0)


def mid_before(v):
    return jnp.concatenate([pltpu.roll(v[1:], 1, 2), v[:1]], axis=0)


def kernel(
    nx, ny,
    p_hbm, d_hbm, m_hbm, out,
    px, mf, u, u2, d, g, dg, w, kx, ky, kz,
    xr, ys, yr, kyf, gyf, gxf, dl, rs, tmat, pmat, pout,
    mid_b, mid_stage, mid_rx, mid_ry, mid_rc, b2, m2, w2, d2, kx2, ky2, kz2,
    va, vb, rr, x2, xk,
    cstage, crecv, cm, cw, cb, ce, t2,
    base, fstage, frecv, fk,
    ar1, ar2,
    cst, crn, vf, v2f, ktf, k12f, kzf, wf, uf, bcs, bcr,
    in_sem, fs, fr, ms, mr, cs, cr, xs, xrs, as1, ar1s, as2, ar2s,
):
    gx = lax.axis_index("gx")
    gy = lax.axis_index("gy")
    IN = slice(8, 24)
    LO = slice(7, 23)
    HI = slice(9, 25)

    def device(ox, oy):
        return (lax.rem(gx + (ox % nx), nx), lax.rem(gy + (oy % ny), ny))

    peers = {(o, 0) for o in range(1, nx)} | {(0, o) for o in range(1, ny)}
    peers |= {(dx % nx, dy % ny) for dx, dy in NEAR}
    peers = sorted(peers - {(0, 0)})

    loads = []
    for n, (src, dst) in enumerate(
        ((m_hbm, mf.at[1:17, :, IN, :]), (p_hbm, px.at[1:17, :, IN, :]), (d_hbm, d))
    ):
        loads.append(
            [
                pltpu.make_async_copy(
                    src.at[:, :, 128 * t : 128 * t + 128], dst.at[:, t], in_sem.at[n, t]
                )
                for t in range(4)
            ]
        )
        for c in loads[-1]:
            c.start()
    barrier = pltpu.get_barrier_semaphore()
    for ox, oy in peers:
        pl.semaphore_signal(barrier, inc=1, device_id=device(ox, oy), device_id_type=MESH)

    def remote(src, dst, ssem, rsem, ox, oy):
        return pltpu.make_async_remote_copy(
            src_ref=src, dst_ref=dst, send_sem=ssem, recv_sem=rsem,
            device_id=device(ox, oy), device_id_type=MESH,
        )

    def planes(start, stop, width, body):
        def several(j, carry):
            for q in range(width):
                body(start + width * j + q)
            return carry

        lax.fori_loop(0, (stop - start) // width, several, 0)

    zeros = jnp.zeros((4, 8, 128), F32)
    rims = (mf, px, u, u2)
    for a in rims:
        for plane in (0, 17):
            a[plane, :, 8:16, :] = zeros
            a[plane, :, 16:24, :] = zeros

    def clear(i):
        for a in rims:
            a[i + 1, :, 0:8, :] = zeros
            a[i + 1, :, 24:32, :] = zeros
        ky[i, :, 0:8, :] = zeros

    planes(0, 16, 2, clear)

    zi = lax.broadcasted_iota(jnp.int32, tmat.shape, 0)
    ci = lax.broadcasted_iota(jnp.int32, tmat.shape, 1)
    hit = (zi >> 1) == (((ci & 127) << 1) + (ci >> 7))
    tmat[...] = jnp.where(hit, 1.0, 0.0).astype(BF16)
    zi = lax.broadcasted_iota(jnp.int32, pmat.shape, 1)
    ci = lax.broadcasted_iota(jnp.int32, pmat.shape, 0)
    hit = (zi >> 1) == (((ci & 127) << 1) + (ci >> 7))
    pmat[...] = jnp.where(hit, 1.0, 0.0).astype(BF16)

    def pack_rows(arr, n, layer=0, off=1, row=8):
        low, high = row + layer, row + 15 - layer
        for x in range(16):
            ys[n, 0, :, x : x + 1, :] = arr[x + off, :, low : low + 1, :]
            ys[n, 1, :, x : x + 1, :] = arr[x + off, :, high : high + 1, :]

    def fine_send(arr, n, layer=0, off=1, row=8):
        rows = slice(row, row + 16)
        low, high = arr.at[off + layer, :, rows, :], arr.at[off + 15 - layer, :, rows, :]
        copies = [
            remote(low, xr.at[n, 1], fs.at[n, 0], fr.at[n, 0], -1, 0),
            remote(high, xr.at[n, 0], fs.at[n, 1], fr.at[n, 1], 1, 0),
            remote(ys.at[n, 0], yr.at[n, 1], fs.at[n, 2], fr.at[n, 2], 0, -1),
            remote(ys.at[n, 1], yr.at[n, 0], fs.at[n, 3], fr.at[n, 3], 0, 1),
        ]
        for c in copies:
            c.start()
        return copies

    def wait(copies):
        for c in copies:
            c.wait()

    def wait_sent(copies):
        for c in copies:
            c.wait_send()

    def wait_arrived(copies):
        for c in copies:
            c.wait_recv()

    def corner_send(arr, n):
        copies = []
        for k, (dx, dy) in enumerate(NEAR[4:]):
            x, y = 1 + 15 * (k // 2), 8 + 15 * (k % 2)
            for t in range(4):
                cst[n, k, t : t + 1, :] = arr[x, t, y : y + 1, :]
            copies.append(
                remote(cst.at[n, k], crn.at[n, 3 - k], fs.at[7 + n, k], fr.at[7 + n, k], dx, dy)
            )
            copies[-1].start()
        return copies

    def restrict_fine(arr, off, row, scale):
        for j in range(8):
            for t in range(4):
                total = None
                for q in range(2):
                    for h in range(2):
                        part = arr[2 * j + q + off, t, pl.ds(row + h, 8, stride=2), :]
                        total = part if total is None else total + part
                rs[8 * j : 8 * j + 8, 128 * t : 128 * t + 128] = total * scale
        return exact_dot(rs[...], tmat[...])

    def mid_put(n, got):
        low = lax.broadcasted_iota(jnp.int32, (2, 8, 128), 1) < 4
        blocks = []
        for x in range(8):
            rows = got[8 * x : 8 * x + 8]
            v = jnp.stack([rows[:, :128], rows[:, 128:]], axis=0)
            mid_b[n, x] = v
            blocks.append(v)
        for t in range(4):
            a, b = blocks[2 * t], blocks[2 * t + 1]
            mid_stage[n, 0, t] = jnp.where(low, a, pltpu.roll(b, 4, 1))
            mid_stage[n, 1, t] = jnp.where(low, pltpu.roll(a, 4, 1), b)

    def mid_send(n):
        copies = [
            remote(mid_b.at[n, 0:4], mid_rx.at[n, 1], ms.at[n, 0], mr.at[n, 0], -1, 0),
            remote(mid_b.at[n, 4:8], mid_rx.at[n, 0], ms.at[n, 1], mr.at[n, 1], 1, 0),
            remote(mid_stage.at[n, 0], mid_ry.at[n, 1], ms.at[n, 2], mr.at[n, 2], 0, -1),
            remote(mid_stage.at[n, 1], mid_ry.at[n, 0], ms.at[n, 3], mr.at[n, 3], 0, 1),
        ]
        k = 4
        for i, dx in enumerate((-1, 1)):
            for j, dy in enumerate((-1, 1)):
                copies.append(
                    remote(
                        mid_stage.at[n, j, 2 * i : 2 * i + 2], mid_rc.at[n, 1 - i, 1 - j],
                        ms.at[n, k], mr.at[n, k], dx, dy,
                    )
                )
                k += 1
        for c in copies:
            c.start()
        return copies

    def mid_place(n, ext):
        for i in range(2):
            for x in range(4):
                ext[12 * i + x, :, 12:20, :] = mid_rx[n, i, x]
            for t in range(4):
                for q in range(2):
                    ext[4 + 2 * t + q, :, 8 + 12 * i : 12 + 12 * i, :] = mid_ry[
                        n, i, t, :, 4 * q : 4 * q + 4, :
                    ]
            for j in range(2):
                for t in range(2):
                    for q in range(2):
                        ext[12 * i + 2 * t + q, :, 8 + 12 * j : 12 + 12 * j, :] = mid_rc[
                            n, i, j, t, :, 4 * q : 4 * q + 4, :
                        ]

    def mid_own(n, ext):
        for x in range(8):
            ext[4 + x, :, 12:20, :] = mid_b[n, x]

    def coarse_block(arr, n, row, scale):
        for x in range(4):
            total = None
            for q in range(2):
                for t in range(2):
                    for h in range(2):
                        part = arr[4 + 2 * x + q, t, pl.ds(row + h, 4, stride=2), :]
                        total = part if total is None else total + part
            cstage[n, 4 * x : 4 * x + 4, :] = total * scale

    def coarse_send(n):
        copies = []
        for k, (dx, dy) in enumerate(NEAR):
            copies.append(
                remote(cstage.at[n], crecv.at[n, k], cs.at[n, k], cr.at[n, k], dx, dy)
            )
            copies[-1].start()
        return copies

    def coarse_wait(copies, n, ext):
        def place(dx, dy, block):
            for x in range(4):
                ext[4 * dx + 4 + x, 4 * dy + 4 : 4 * dy + 8, :] = block[4 * x : 4 * x + 4, :]

        place(0, 0, cstage.at[n])
        wait(copies)
        for k, (dx, dy) in enumerate(NEAR):
            place(-dx, -dy, crecv.at[n, k])

    def fine_sum(arr, i):
        c = arr[i + 1, :, IN, :]
        z = kz[i]
        total = kx[i] * arr[i, :, IN, :] + kx[i + 1] * arr[i + 2, :, IN, :]
        total = total + ky[i, :, LO, :] * arr[i + 1, :, LO, :]
        total = total + ky[i, :, IN, :] * arr[i + 1, :, HI, :]
        return c, total + z * fine_next(c) + fine_before(z * c)

    def mid_sum(arr, i):
        c = arr[i, :, IN, :]
        z = kz2[i]
        total = kx2[i] * arr[i - 1, :, IN, :] + kx2[i + 1] * arr[i + 1, :, IN, :]
        total = total + ky2[i, :, LO, :] * arr[i, :, LO, :]
        total = total + ky2[i, :, IN, :] * arr[i, :, HI, :]
        return c, total + z * mid_next(c) + mid_before(z * c)

    def add_rows(arr, off, row):
        for x in range(16):
            for f in range(2):
                k = row + 15 * f
                arr[x + off, :, k : k + 1, :] = (
                    arr[x + off, :, k : k + 1, :] + dl[f, :, x : x + 1, :]
                )

    wait(loads[0])
    pack_rows(mf, 0)
    mid_put(0, restrict_fine(mf, 1, 8, 0.125))
    wait(loads[1])
    pack_rows(px, 1)
    wait(loads[2])
    pl.semaphore_wait(barrier, len(peers))
    m_copies = fine_send(mf, 0)
    p_copies = fine_send(px, 1)

    def coefficients(i):
        c = mf[i + 1, :, IN, :]
        below = 0.5 * (c + mf[i, :, IN, :])
        above = c + mf[i + 2, :, IN, :]
        left = c + mf[i + 1, :, LO, :]
        right = 0.5 * (c + mf[i + 1, :, HI, :])
        after = 0.5 * (c + fine_next(c))
        before = c + fine_before(c)
        kx[i] = below
        ky[i, :, IN, :] = right
        kz[i] = after
        dg[i] = (S1 + below + right + after) + 0.5 * (above + left + before)

    planes(0, 16, 4, coefficients)
    kx[16] = 0.5 * mf[16, :, IN, :]

    def first_sum(i):
        c, total = fine_sum(px, i)
        g[i] = d[i] + total

    planes(0, 16, 4, first_sum)
    pack_rows(d, 4, 0, 0, 0)
    pack_rows(mf, 5, 1)
    wait_sent(m_copies)
    wait_sent(p_copies)
    m2_copies = mid_send(0)

    wait_arrived(m_copies)
    for f in range(2):
        face = 0.5 * xr[0, f]
        kx[16 * f] = kx[16 * f] + face
        dg[15 * f] = dg[15 * f] + face
        face = 0.5 * yr[0, f]
        kyf[f] = 0.5 * ys[0, f] + face
        dl[f] = face
    add_rows(dg, 0, 0)
    wait_arrived(p_copies)
    for f in range(2):
        g[15 * f] = g[15 * f] + kx[16 * f] * xr[1, f]
        dl[f] = kyf[f] * yr[1, f]
    add_rows(g, 0, 0)

    def first_step(i):
        weight = INV / dg[i]
        w[i] = weight
        u[i + 1, :, IN, :] = weight * g[i] - INV * px[i + 1, :, IN, :]

    planes(0, 16, 4, first_step)
    pack_rows(u, 2)
    u_copies = fine_send(u, 2)

    def second_sum(i):
        c, total = fine_sum(u, i)
        u2[i + 1, :, IN, :] = ALPHA * c + STEP * (w[i] * total)

    planes(0, 16, 4, second_sum)
    for x in range(16):
        for f in range(2):
            gyf[f, :, x : x + 1, :] = w[x, :, 15 * f : 15 * f + 1, :]
    for f in range(2):
        gyf[f] = STEP * (gyf[f] * kyf[f])
        gxf[f] = STEP * (w[15 * f] * kx[16 * f])
    mid_own(0, m2)
    wait(m2_copies)
    mid_place(0, m2)
    coarse_block(m2, 0, 12, 0.125)
    m3_copies = coarse_send(0)
    wait_sent(u_copies)
    d_copies = fine_send(d, 4, 0, 0, 0)

    wait_arrived(u_copies)
    for f in range(2):
        k = 1 + 15 * f
        u2[k, :, IN, :] = u2[k, :, IN, :] + gxf[f] * xr[2, f]
        dl[f] = gyf[f] * yr[2, f]
    add_rows(u2, 1, 8)
    pack_rows(u2, 3)
    u2_copies = fine_send(u2, 3)

    def third_sum(i):
        c, total = fine_sum(u2, i)
        before = u[i + 1, :, IN, :]
        g[i] = dg[i] * (BETA * c - GAMMA * before) + total
        px[i + 1, :, IN, :] = px[i + 1, :, IN, :] + before + c

    planes(0, 16, 4, third_sum)

    def mid_coefficients(i):
        c = m2[i, :, IN, :]
        below = 0.5 * (c + m2[i - 1, :, IN, :])
        above = 0.5 * (c + m2[i + 1, :, IN, :])
        left = c + m2[i, :, LO, :]
        right = 0.5 * (c + m2[i, :, HI, :])
        after = 0.5 * (c + mid_next(c))
        before = c + mid_before(c)
        kx2[i] = below
        kx2[i + 1] = above
        ky2[i, :, IN, :] = right
        kz2[i] = after
        diagonal = (S2 + below + above + right + after) + 0.5 * (left + before)
        d2[i] = diagonal
        w2[i] = INV / diagonal

    planes(1, 15, 7, mid_coefficients)
    coarse_wait(m3_copies, 0, cm)
    mob = cm[...]
    lap = weighted_sum(mob)
    cw[1:11] = 0.8 / (S3 + 0.5 * (5.0 * mob[1:-1] + lap))
    for x in range(4):
        cstage[1, 4 * x : 4 * x + 4, :] = cw[4 + x, 4:8, :]
    w3_copies = coarse_send(1)
    wait_sent(u2_copies)
    far_copies = fine_send(mf, 5, 1) + corner_send(mf, 0)

    wait_arrived(u2_copies)
    for f in range(2):
        g[15 * f] = g[15 * f] + kx[16 * f] * xr[3, f]
        dl[f] = kyf[f] * yr[3, f]
    add_rows(g, 0, 0)
    mid_put(1, restrict_fine(g, 0, 0, 0.5))
    b2_copies = mid_send(1)

    pack_rows(px, 6, 1)
    def response_one(i):
        vb[i, :, IN, :] = (-S2) * w2[i]

    planes(1, 15, 7, response_one)

    def response_two(i):
        c, total = mid_sum(vb, i)
        xk[i] = 1.0 + (1.0 + ALPHA) * c + STEP * (w2[i] * total)

    planes(2, 14, 6, response_two)
    for x in range(8):
        fk[2, :, x : x + 1, :] = xk[4 + x, :, 3:4, :]
        fk[3, :, x : x + 1, :] = xk[4 + x, :, 12:13, :]
    fk[0] = xk[3, :, 4:12, :]
    fk[1] = xk[12, :, 4:12, :]
    coarse_wait(w3_copies, 1, cw)
    weight = cw[...]
    y = jnp.ones_like(weight)
    psi = y
    for k in range(3):
        inner = slice(k, 12 - k)
        y = y[1:-1] - coarse_operator(weight[inner] * y, mob[inner], lap[k : 10 - k])
        psi = psi[1:-1] + y
    ce[0:4] = 1.0 - S3 * (weight[4:8] * psi[1:5])
    for f in range(2):
        xr[1, f] = xr[1, f] + xr[2, f] + xr[3, f]
        yr[1, f] = yr[1, f] + yr[2, f] + yr[3, f]
    mid_own(1, b2)
    wait_sent(b2_copies)
    x1_copies = fine_send(px, 6, 1) + corner_send(px, 1)
    wait_arrived(b2_copies)
    mid_place(1, b2)

    def mid_one(i):
        va[i, :, IN, :] = w2[i] * b2[i, :, IN, :]

    planes(1, 15, 7, mid_one)

    def mid_two(i):
        c, total = mid_sum(va, i)
        step = ALPHA * c + STEP * (w2[i] * total)
        vb[i, :, IN, :] = step
        x2[i] = c + step

    planes(2, 14, 6, mid_two)

    def mid_three(i):
        c, total = mid_sum(vb, i)
        rr[i] = d2[i] * (BETA * c - GAMMA * va[i, :, IN, :]) + total

    planes(4, 12, 4, mid_three)
    coarse_block(rr, 2, 4, 0.5)
    b3_copies = coarse_send(2)

    part = jnp.zeros((1, 128), F32)
    partm = jnp.zeros((1, 128), F32)
    for x in range(4):
        part = part + jnp.sum(
            ce[x, 4:8, :] * cstage[2, 4 * x : 4 * x + 4, :], axis=0, keepdims=True
        )
        partm = partm + jnp.sum(cstage[0, 4 * x : 4 * x + 4, :], axis=0, keepdims=True)
    ar1[0, 0:1, :] = part
    ar1[0, 1:2, :] = partm
    sums = []
    for o in range(1, nx):
        sums.append(remote(ar1.at[0], ar1.at[o], as1.at[o], ar1s.at[o], o, 0))
        sums[-1].start()

    wait(d_copies)
    wait(far_copies)

    def corners(f):
        return ((0, 1), (2, 3), (0, 2), (1, 3))[f]

    for f in range(4):
        first, second = (xr.at[0, f], xr.at[5, f]) if f < 2 else (yr.at[0, f - 2], yr.at[5, f - 2])
        k01 = kx[16 * f] if f < 2 else kyf[f - 2]
        c = first[...]
        vf[f, :, IN, :] = c
        for row, k in zip((7, 24), corners(f)):
            for t in range(4):
                vf[f, t, row : row + 1, :] = crn[0, k, t : t + 1, :]
        ktf[f, :, IN, :] = 0.5 * (c + vf[f, :, HI, :])
        ktf[f, :, 7:8, :] = 0.5 * (vf[f, :, 7:8, :] + vf[f, :, 8:9, :])
        k12 = 0.5 * (c + second[...])
        after = 0.5 * (c + fine_next(c))
        k12f[f] = k12
        kzf[f] = after
        wf[f] = INV / (
            S1 + k01 + k12 + ktf[f, :, IN, :] + ktf[f, :, LO, :] + after + fine_before(after)
        )

    coarse_wait(b3_copies, 2, cb)
    rhs = cb[...]
    e = weight * rhs
    for k in range(3):
        inner = slice(k, 12 - k)
        e = e[1:-1] + weight[k + 1 : 11 - k] * (
            rhs[k + 1 : 11 - k] - coarse_operator(e, mob[inner], lap[k : 10 - k])
        )
    wait(sums)
    total = ar1[0]
    for o in range(1, nx):
        total = total + ar1[o]
    ar2[0] = total
    sums = []
    for o in range(1, ny):
        sums.append(remote(ar2.at[0], ar2.at[o], as2.at[o], ar2s.at[o], 0, o))
        sums[-1].start()

    ce[3:9] = e
    for x in range(6):
        for h in range(2):
            t2[x, pl.ds(h, 8, stride=2), :] = ce[3 + x, 2:10, :]
    for x in range(6):
        v = t2[x]
        both = jnp.stack([v, v], axis=0)
        for q in range(2):
            va[2 + 2 * x + q, :, IN, :] = x2[2 + 2 * x + q] + both

    def post_one(i):
        c, total = mid_sum(va, i)
        vb[i, :, IN, :] = w2[i] * (b2[i, :, IN, :] + total) - INV * c

    planes(3, 13, 5, post_one)

    def post_two(i):
        c, total = mid_sum(vb, i)
        done = va[i, :, IN, :] + (1.0 + ALPHA) * c + STEP * (w2[i] * total)
        base[i - 4] = done[:, 4:12, :]

    planes(4, 12, 4, post_two)
    for x in range(8):
        fstage[0, :, x : x + 1, :] = base[x, :, 0:1, :]
        fstage[1, :, x : x + 1, :] = base[x, :, 7:8, :]
    x_copies = [
        remote(base.at[0], frecv.at[1], xs.at[0], xrs.at[0], -1, 0),
        remote(base.at[7], frecv.at[0], xs.at[1], xrs.at[1], 1, 0),
        remote(fstage.at[0], frecv.at[3], xs.at[2], xrs.at[2], 0, -1),
        remote(fstage.at[1], frecv.at[2], xs.at[3], xrs.at[3], 0, 1),
    ]
    for k, (dx, dy) in enumerate(NEAR[4:]):
        x, y = 7 * (k // 2), 7 * (k % 2)
        for t in range(2):
            bcs[k, t : t + 1, :] = base[x, t, y : y + 1, :]
        x_copies.append(
            remote(bcs.at[k], bcr.at[3 - k], xs.at[4 + k], xrs.at[4 + k], dx, dy)
        )
    for c in x_copies:
        c.start()
    wait(x1_copies)
    wait(sums)
    total = ar2[0]
    for o in range(1, ny):
        total = total + ar2[o]
    cells = 16.0 * 128.0 * nx * ny
    sum_f = jnp.sum(total[0:1, :], axis=1, keepdims=True)
    sum_m = jnp.sum(total[1:2, :], axis=1, keepdims=True)
    kappa = 0.8 * (sum_f / cells) / (S3 + 5.0 * (sum_m / cells))

    for x in range(8):
        v = base[x] + kappa * xk[4 + x, :, 4:12, :]
        pout[8 * x : 8 * x + 8, 0:128] = v[0]
        pout[8 * x : 8 * x + 8, 128:256] = v[1]
    wait(x_copies)
    for f in range(4):
        v = frecv[f] + kappa * fk[f]
        pout[64 + 8 * f : 72 + 8 * f, 0:128] = v[0]
        pout[64 + 8 * f : 72 + 8 * f, 128:256] = v[1]
    for k in range(4):
        x, y = 3 + 9 * (k // 2), 3 + 9 * (k % 2)
        for t in range(2):
            pout[96 + k : 97 + k, 128 * t : 128 * t + 128] = (
                bcr[k, t : t + 1, :] + kappa * xk[x, t, y : y + 1, :]
            )
    pout[...] = exact_dot(pout[:, 0:256], pmat[...])

    for j in range(8):
        for t in range(4):
            v = pout[8 * j : 8 * j + 8, 128 * t : 128 * t + 128]
            for q in range(2):
                for h in range(2):
                    rows = pl.ds(8 + h, 8, stride=2)
                    px[2 * j + 1 + q, t, rows, :] = px[2 * j + 1 + q, t, rows, :] + v
    for f in range(4):
        first, second = (xr.at[1, f], xr.at[6, f]) if f < 2 else (yr.at[1, f - 2], yr.at[6, f - 2])
        for t in range(4):
            lanes = slice(128 * t, 128 * t + 128)
            v = pout[64 + 8 * f : 72 + 8 * f, lanes]
            for h in range(2):
                rows = pl.ds(h, 8, stride=2)
                vf[f, t, pl.ds(8 + h, 8, stride=2), :] = first[t, rows, :] + v
                v2f[f, t, rows, :] = second[t, rows, :] + v
            for row, k in zip((7, 24), corners(f)):
                vf[f, t, row : row + 1, :] = crn[1, k, t : t + 1, :] + pout[96 + k : 97 + k, lanes]
    pack_rows(px, 1)
    for f in range(2):
        d[15 * f] = d[15 * f] + kx[16 * f] * vf[f, :, IN, :]
        dl[f] = kyf[f] * vf[2 + f, :, IN, :]
    add_rows(d, 0, 0)

    for f in range(4):
        if f < 2:
            k01, inside, rhs_f = kx[16 * f], px[1 + 15 * f, :, IN, :], xr[4, f]
        else:
            k01, inside, rhs_f = kyf[f - 2], ys[1, f - 2], yr[4, f - 2]
        c = vf[f, :, IN, :]
        z = kzf[f]
        total = k01 * inside + k12f[f] * v2f[f]
        total = total + ktf[f, :, LO, :] * vf[f, :, LO, :] + ktf[f, :, IN, :] * vf[f, :, HI, :]
        total = total + z * fine_next(c) + fine_before(z * c)
        uf[f] = wf[f] * (rhs_f + total) - INV * c

    def fourth_sum(i):
        c, total = fine_sum(px, i)
        u[i + 1, :, IN, :] = w[i] * (d[i] + total) - INV * c

    planes(0, 16, 4, fourth_sum)

    def last_sum(i):
        c, total = fine_sum(u, i)
        g[i] = px[i + 1, :, IN, :] + (1.0 + ALPHA) * c + STEP * (w[i] * total)

    planes(0, 16, 4, last_sum)
    for f in range(2):
        g[15 * f] = g[15 * f] + gxf[f] * uf[f]
        dl[f] = gyf[f] * uf[2 + f]
    add_rows(g, 0, 0)
    for i in range(16):
        for t in range(4):
            out[i, :, 128 * t : 128 * t + 128] = g[i, t]


def solution(mesh):
    nx, ny = mesh.shape["gx"], mesh.shape["gy"]

    def local(p, d, m):
        vm = lambda *s: pltpu.VMEM(s, F32)
        sem = lambda *s: pltpu.SemaphoreType.DMA(s)
        plane = (16, 4, 16, 128)
        face = (4, 16, 128)
        scratch = [
            vm(18, 4, 32, 128), vm(18, 4, 32, 128), vm(18, 4, 32, 128), vm(18, 4, 32, 128),
            vm(*plane), vm(*plane), vm(*plane), vm(*plane),
            vm(17, 4, 16, 128), vm(16, 4, 32, 128), vm(*plane),
            vm(7, 2, *face), vm(7, 2, *face), vm(7, 2, *face),
            vm(2, *face), vm(2, *face), vm(2, *face), vm(2, *face), vm(64, 512),
            pltpu.VMEM((512, 256), BF16), pltpu.VMEM((256, 512), BF16), vm(104, 512),
            vm(2, 8, 2, 8, 128), vm(2, 2, 4, 2, 8, 128), vm(2, 2, 4, 2, 8, 128),
            vm(2, 2, 4, 2, 8, 128), vm(2, 2, 2, 2, 2, 8, 128),
            vm(16, 2, 32, 128), vm(16, 2, 32, 128), vm(16, 2, 16, 128), vm(16, 2, 16, 128),
            vm(17, 2, 16, 128), vm(16, 2, 32, 128), vm(16, 2, 16, 128),
            vm(16, 2, 32, 128), vm(16, 2, 32, 128), vm(16, 2, 16, 128), vm(16, 2, 16, 128),
            vm(16, 2, 16, 128),
            vm(3, 16, 128), vm(3, 8, 16, 128), vm(12, 16, 128), vm(12, 16, 128), vm(12, 16, 128),
            vm(12, 16, 128), vm(6, 16, 128),
            vm(8, 2, 8, 128), vm(2, 2, 8, 128), vm(4, 2, 8, 128), vm(4, 2, 8, 128),
            vm(nx, 2, 128), vm(ny, 2, 128),
            vm(2, 4, 4, 128), vm(2, 4, 4, 128), vm(4, 4, 32, 128), vm(4, *face), vm(4, 4, 32, 128),
            vm(4, *face), vm(4, *face), vm(4, *face), vm(4, *face), vm(4, 2, 128), vm(4, 2, 128),
            sem(3, 4), sem(9, 4), sem(9, 4), sem(2, 8), sem(2, 8), sem(3, 8), sem(3, 8),
            sem(8), sem(8), sem(nx), sem(nx), sem(ny), sem(ny),
        ]
        return pl.pallas_call(
            functools.partial(kernel, nx, ny),
            out_shape=jax.ShapeDtypeStruct((16, 16, 512), F32),
            in_specs=[pl.BlockSpec(memory_space=pl.ANY)] * 3,
            out_specs=pl.BlockSpec(memory_space=pltpu.VMEM),
            scratch_shapes=scratch,
            compiler_params=pltpu.CompilerParams(
                collective_id=0, has_side_effects=True, vmem_limit_bytes=30 * 1024 * 1024
            ),
        )(*[pltpu.with_memory_space_constraint(a, pltpu.HBM) for a in (p, d, m)])

    spec = P("gx", "gy", None)
    return jax.shard_map(
        local, mesh=mesh, in_specs=(spec, spec, spec), out_specs=spec, check_vma=False
    )
```

```python
import functools

import jax
import jax.numpy as jnp
from jax import lax
from jax.experimental import pallas as pl
from jax.experimental.pallas import tpu as pltpu
from jax.sharding import PartitionSpec as P

MESH = pl.DeviceIdType.MESH
F32 = jnp.float32
BF16 = jnp.bfloat16

S1 = 0.05
S2 = 0.2
S3 = 0.8
MIDPOINT = (2.0 + 0.3) / 2
HALFWIDTH = (2.0 - 0.3) / 2
SIGMA = MIDPOINT / HALFWIDTH
P1 = 1.0 / SIGMA
P2 = 1.0 / (2.0 * SIGMA - P1)
CA = P2 * P1
CB = 2.0 * P2 / HALFWIDTH
INV = 1.0 / MIDPOINT
ALPHA = CA + CB * (MIDPOINT - 1.0)
STEP = CB * MIDPOINT
BETA = 1.0 / CB - 1.0
GAMMA = CA / CB
FAR = [(x, y) for x in range(-2, 3) for y in range(-2, 3) if max(abs(x), abs(y)) == 2]
NEAR = [(-1, 0), (1, 0), (0, -1), (0, 1), (-1, -1), (-1, 1), (1, -1), (1, 1)]


def thirds(x):
    high = x.astype(BF16)
    rest = x - high.astype(F32)
    middle = rest.astype(BF16)
    low = (rest - middle.astype(F32)).astype(BF16)
    return high, middle, low


def exact_dot(x, matrix):
    total = None
    for part in thirds(x):
        term = jnp.dot(part, matrix, preferred_element_type=F32)
        total = term if total is None else total + term
    return total


def weighted_sum(f):
    q = pltpu.roll(f, 1, 2) + pltpu.roll(f, f.shape[2] - 1, 2)
    face = 0.5 * f + 0.125 * q
    edge = 0.125 * f + 0.0625 * q
    rows = f.shape[1]
    a = 0.5 * q + (pltpu.roll(face, 1, 1) + pltpu.roll(face, rows - 1, 1))
    b = face + (pltpu.roll(edge, 1, 1) + pltpu.roll(edge, rows - 1, 1))
    return a[1:-1] + (b[:-2] + b[2:])


def coarse_operator(v, mob, mob_sum):
    c = v[1:-1]
    m = mob[1:-1]
    return S3 * c + 0.5 * (
        5.0 * m * c - m * weighted_sum(v) + c * mob_sum - weighted_sum(mob * v)
    )


def fine_next(v):
    turned = pltpu.roll(v, 127, 2)
    lane = lax.broadcasted_iota(jnp.int32, v.shape, 2)
    return jnp.where(lane == 127, jnp.concatenate([turned[1:], turned[:1]], axis=0), turned)


def fine_before(v):
    turned = pltpu.roll(v, 1, 2)
    lane = lax.broadcasted_iota(jnp.int32, v.shape, 2)
    return jnp.where(lane == 0, jnp.concatenate([turned[3:], turned[:3]], axis=0), turned)


def mid_next(v):
    return jnp.concatenate([v[1:], pltpu.roll(v[:1], 127, 2)], axis=0)


def mid_before(v):
    return jnp.concatenate([pltpu.roll(v[1:], 1, 2), v[:1]], axis=0)


def kernel(
    nx, ny,
    p_hbm, d_hbm, m_hbm, out,
    px, mf, u, u2, d, g, dg, w, kx, ky, kz,
    xr, ys, yr, kyf, gyf, gxf, dl, rs, tmat, pmat, pout,
    mid_b, mid_stage, mid_rx, mid_ry, mid_rc, b2, m2, w2, d2, kx2, ky2, kz2,
    va, vb, rr, x2,
    cstage, crecv, cm, cw, cb, ce, t2,
    base, cedge, cfar,
    ar1, ar2,
    cst, crn, vf, v2f, ktf, k12f, kzf, wf, uf,
    in_sem, fs, fr, ms, mr, cs, cr, as1, ar1s, as2, ar2s,
):
    gx = lax.axis_index("gx")
    gy = lax.axis_index("gy")
    IN = slice(8, 24)
    LO = slice(7, 23)
    HI = slice(9, 25)

    def device(ox, oy):
        return (lax.rem(gx + (ox % nx), nx), lax.rem(gy + (oy % ny), ny))

    peers = {(o, 0) for o in range(1, nx)} | {(0, o) for o in range(1, ny)}
    peers |= {(dx % nx, dy % ny) for dx, dy in NEAR + FAR}
    peers = sorted(peers - {(0, 0)})

    loads = []
    for n, (src, dst) in enumerate(
        ((m_hbm, mf.at[1:17, :, IN, :]), (p_hbm, px.at[1:17, :, IN, :]), (d_hbm, d))
    ):
        loads.append(
            [
                pltpu.make_async_copy(
                    src.at[:, :, 128 * t : 128 * t + 128], dst.at[:, t], in_sem.at[n, t]
                )
                for t in range(4)
            ]
        )
        for c in loads[-1]:
            c.start()
    barrier = pltpu.get_barrier_semaphore()
    for ox, oy in peers:
        pl.semaphore_signal(barrier, inc=1, device_id=device(ox, oy), device_id_type=MESH)

    def remote(src, dst, ssem, rsem, ox, oy):
        return pltpu.make_async_remote_copy(
            src_ref=src, dst_ref=dst, send_sem=ssem, recv_sem=rsem,
            device_id=device(ox, oy), device_id_type=MESH,
        )

    def planes(start, stop, width, body):
        def several(j, carry):
            for q in range(width):
                body(start + width * j + q)
            return carry

        lax.fori_loop(0, (stop - start) // width, several, 0)

    zeros = jnp.zeros((4, 8, 128), F32)
    rims = (mf, px, u, u2)
    for a in rims:
        for plane in (0, 17):
            a[plane, :, 8:16, :] = zeros
            a[plane, :, 16:24, :] = zeros

    def clear(i):
        for a in rims:
            a[i + 1, :, 0:8, :] = zeros
            a[i + 1, :, 24:32, :] = zeros
        ky[i, :, 0:8, :] = zeros

    planes(0, 16, 2, clear)

    zi = lax.broadcasted_iota(jnp.int32, tmat.shape, 0)
    ci = lax.broadcasted_iota(jnp.int32, tmat.shape, 1)
    hit = (zi >> 1) == (((ci & 127) << 1) + (ci >> 7))
    tmat[...] = jnp.where(hit, 1.0, 0.0).astype(BF16)
    zi = lax.broadcasted_iota(jnp.int32, pmat.shape, 1)
    ci = lax.broadcasted_iota(jnp.int32, pmat.shape, 0)
    hit = (zi >> 1) == (((ci & 127) << 1) + (ci >> 7))
    pmat[...] = jnp.where(hit, 1.0, 0.0).astype(BF16)

    def pack_rows(arr, n, layer=0, off=1, row=8):
        low, high = row + layer, row + 15 - layer
        for x in range(16):
            ys[n, 0, :, x : x + 1, :] = arr[x + off, :, low : low + 1, :]
            ys[n, 1, :, x : x + 1, :] = arr[x + off, :, high : high + 1, :]

    def fine_send(arr, n, layer=0, off=1, row=8):
        rows = slice(row, row + 16)
        low, high = arr.at[off + layer, :, rows, :], arr.at[off + 15 - layer, :, rows, :]
        copies = [
            remote(low, xr.at[n, 1], fs.at[n, 0], fr.at[n, 0], -1, 0),
            remote(high, xr.at[n, 0], fs.at[n, 1], fr.at[n, 1], 1, 0),
            remote(ys.at[n, 0], yr.at[n, 1], fs.at[n, 2], fr.at[n, 2], 0, -1),
            remote(ys.at[n, 1], yr.at[n, 0], fs.at[n, 3], fr.at[n, 3], 0, 1),
        ]
        for c in copies:
            c.start()
        return copies

    def wait(copies):
        for c in copies:
            c.wait()

    def wait_sent(copies):
        for c in copies:
            c.wait_send()

    def wait_arrived(copies):
        for c in copies:
            c.wait_recv()

    def corner_send(arr, n):
        copies = []
        for k, (dx, dy) in enumerate(NEAR[4:]):
            x, y = 1 + 15 * (k // 2), 8 + 15 * (k % 2)
            for t in range(4):
                cst[n, k, t : t + 1, :] = arr[x, t, y : y + 1, :]
            copies.append(
                remote(cst.at[n, k], crn.at[n, 3 - k], fs.at[7 + n, k], fr.at[7 + n, k], dx, dy)
            )
            copies[-1].start()
        return copies

    def restrict_fine(arr, off, row, scale):
        for j in range(8):
            for t in range(4):
                total = None
                for q in range(2):
                    for h in range(2):
                        part = arr[2 * j + q + off, t, pl.ds(row + h, 8, stride=2), :]
                        total = part if total is None else total + part
                rs[8 * j : 8 * j + 8, 128 * t : 128 * t + 128] = total * scale
        return exact_dot(rs[...], tmat[...])

    def mid_put(n, got):
        blocks = []
        for x in range(8):
            rows = got[8 * x : 8 * x + 8]
            v = jnp.stack([rows[:, :128], rows[:, 128:]], axis=0)
            mid_b[n, x] = v
            blocks.append(v)
        mid_fold(n, blocks)

    def mid_fold(n, blocks):
        low = lax.broadcasted_iota(jnp.int32, (2, 8, 128), 1) < 4
        for t in range(4):
            a, b = blocks[2 * t], blocks[2 * t + 1]
            mid_stage[n, 0, t] = jnp.where(low, a, pltpu.roll(b, 4, 1))
            mid_stage[n, 1, t] = jnp.where(low, pltpu.roll(a, 4, 1), b)

    def mid_send(n):
        copies = [
            remote(mid_b.at[n, 0:4], mid_rx.at[n, 1], ms.at[n, 0], mr.at[n, 0], -1, 0),
            remote(mid_b.at[n, 4:8], mid_rx.at[n, 0], ms.at[n, 1], mr.at[n, 1], 1, 0),
            remote(mid_stage.at[n, 0], mid_ry.at[n, 1], ms.at[n, 2], mr.at[n, 2], 0, -1),
            remote(mid_stage.at[n, 1], mid_ry.at[n, 0], ms.at[n, 3], mr.at[n, 3], 0, 1),
        ]
        k = 4
        for i, dx in enumerate((-1, 1)):
            for j, dy in enumerate((-1, 1)):
                copies.append(
                    remote(
                        mid_stage.at[n, j, 2 * i : 2 * i + 2], mid_rc.at[n, 1 - i, 1 - j],
                        ms.at[n, k], mr.at[n, k], dx, dy,
                    )
                )
                k += 1
        for c in copies:
            c.start()
        return copies

    def mid_place(n, ext):
        for i in range(2):
            for x in range(4):
                ext[12 * i + x, :, 12:20, :] = mid_rx[n, i, x]
            for t in range(4):
                for q in range(2):
                    ext[4 + 2 * t + q, :, 8 + 12 * i : 12 + 12 * i, :] = mid_ry[
                        n, i, t, :, 4 * q : 4 * q + 4, :
                    ]
            for j in range(2):
                for t in range(2):
                    for q in range(2):
                        ext[12 * i + 2 * t + q, :, 8 + 12 * j : 12 + 12 * j, :] = mid_rc[
                            n, i, j, t, :, 4 * q : 4 * q + 4, :
                        ]

    def mid_own(n, ext):
        for x in range(8):
            ext[4 + x, :, 12:20, :] = mid_b[n, x]

    def coarse_block(arr, n, row, scale):
        for x in range(4):
            total = None
            for q in range(2):
                for t in range(2):
                    for h in range(2):
                        part = arr[4 + 2 * x + q, t, pl.ds(row + h, 4, stride=2), :]
                        total = part if total is None else total + part
            cstage[n, 4 * x : 4 * x + 4, :] = total * scale

    def coarse_send(n):
        cedge[n, 0] = cstage[n, 0:4, :]
        cedge[n, 1] = cstage[n, 12:16, :]
        for x in range(4):
            for k in range(2):
                cedge[n, 2 + k, x : x + 1, :] = cstage[n, 4 * x + 3 * k : 4 * x + 3 * k + 1, :]
        copies = []
        for k, (dx, dy) in enumerate(NEAR):
            copies.append(
                remote(cstage.at[n], crecv.at[n, k], cs.at[n, k], cr.at[n, k], dx, dy)
            )
            copies[-1].start()
        for k, (dx, dy) in enumerate(FAR):
            side = (dx == 2) if abs(dx) == 2 else 2 + (dy == 2)
            copies.append(
                remote(
                    cedge.at[n, int(side)], cfar.at[n, k],
                    cs.at[n, 8 + k], cr.at[n, 8 + k], dx, dy,
                )
            )
            copies[-1].start()
        return copies

    def coarse_wait(copies, n, ext, sent=True):
        def place(dx, dy, block):
            for x in range(4):
                ext[4 * dx + 5 + x, 4 * dy + 5 : 4 * dy + 9, :] = block[4 * x : 4 * x + 4, :]

        place(0, 0, cstage.at[n])
        if sent:
            wait_sent(copies)
        wait_arrived(copies)
        for k, (dx, dy) in enumerate(NEAR):
            place(-dx, -dy, crecv.at[n, k])
        for k, (dx, dy) in enumerate(FAR):
            far = cfar.at[n, k]
            if abs(dx) == 2:
                plane = 0 if dx == 2 else 13
                if abs(dy) == 2:
                    row, at = (0, 3) if dy == 2 else (13, 0)
                    ext[plane, row : row + 1, :] = far[at : at + 1, :]
                else:
                    ext[plane, 5 - 4 * dy : 9 - 4 * dy, :] = far[...]
            else:
                row = 0 if dy == 2 else 13
                for x in range(4):
                    ext[5 - 4 * dx + x, row : row + 1, :] = far[x : x + 1, :]

    def fine_sum(arr, i):
        c = arr[i + 1, :, IN, :]
        z = kz[i]
        total = kx[i] * arr[i, :, IN, :] + kx[i + 1] * arr[i + 2, :, IN, :]
        total = total + ky[i, :, LO, :] * arr[i + 1, :, LO, :]
        total = total + ky[i, :, IN, :] * arr[i + 1, :, HI, :]
        return c, total + z * fine_next(c) + fine_before(z * c)

    def mid_sum(arr, i):
        c = arr[i, :, IN, :]
        z = kz2[i]
        total = kx2[i] * arr[i - 1, :, IN, :] + kx2[i + 1] * arr[i + 1, :, IN, :]
        total = total + ky2[i, :, LO, :] * arr[i, :, LO, :]
        total = total + ky2[i, :, IN, :] * arr[i, :, HI, :]
        return c, total + z * mid_next(c) + mid_before(z * c)

    def add_rows(arr, off, row):
        for x in range(16):
            for f in range(2):
                k = row + 15 * f
                arr[x + off, :, k : k + 1, :] = (
                    arr[x + off, :, k : k + 1, :] + dl[f, :, x : x + 1, :]
                )

    wait(loads[0])
    pack_rows(mf, 0)
    mid_put(0, restrict_fine(mf, 1, 8, 0.125))
    wait(loads[1])
    pack_rows(px, 1)
    wait(loads[2])
    pl.semaphore_wait(barrier, len(peers))
    m_copies = fine_send(mf, 0)
    p_copies = fine_send(px, 1)

    def coefficients(i):
        c = mf[i + 1, :, IN, :]
        below = 0.5 * (c + mf[i, :, IN, :])
        above = c + mf[i + 2, :, IN, :]
        left = c + mf[i + 1, :, LO, :]
        right = 0.5 * (c + mf[i + 1, :, HI, :])
        after = 0.5 * (c + fine_next(c))
        before = c + fine_before(c)
        kx[i] = below
        ky[i, :, IN, :] = right
        kz[i] = after
        dg[i] = (S1 + below + right + after) + 0.5 * (above + left + before)

    planes(0, 16, 4, coefficients)
    kx[16] = 0.5 * mf[16, :, IN, :]

    def first_sum(i):
        c, total = fine_sum(px, i)
        g[i] = d[i] + total

    planes(0, 16, 4, first_sum)
    pack_rows(d, 4, 0, 0, 0)
    pack_rows(mf, 5, 1)
    wait_sent(m_copies)
    wait_sent(p_copies)
    m2_copies = mid_send(0)

    wait_arrived(m_copies)
    for f in range(2):
        face = 0.5 * xr[0, f]
        kx[16 * f] = kx[16 * f] + face
        dg[15 * f] = dg[15 * f] + face
        face = 0.5 * yr[0, f]
        kyf[f] = 0.5 * ys[0, f] + face
        dl[f] = face
    add_rows(dg, 0, 0)
    wait_arrived(p_copies)
    for f in range(2):
        g[15 * f] = g[15 * f] + kx[16 * f] * xr[1, f]
        dl[f] = kyf[f] * yr[1, f]
    add_rows(g, 0, 0)

    def first_step(i):
        weight = INV / dg[i]
        w[i] = weight
        u[i + 1, :, IN, :] = weight * g[i] - INV * px[i + 1, :, IN, :]

    planes(0, 16, 4, first_step)
    pack_rows(u, 2)
    u_copies = fine_send(u, 2)

    def second_sum(i):
        c, total = fine_sum(u, i)
        u2[i + 1, :, IN, :] = ALPHA * c + STEP * (w[i] * total)

    planes(0, 16, 4, second_sum)
    for x in range(16):
        for f in range(2):
            gyf[f, :, x : x + 1, :] = w[x, :, 15 * f : 15 * f + 1, :]
    for f in range(2):
        gyf[f] = STEP * (gyf[f] * kyf[f])
        gxf[f] = STEP * (w[15 * f] * kx[16 * f])
    mid_own(0, m2)
    wait(m2_copies)
    mid_place(0, m2)
    coarse_block(m2, 0, 12, 0.125)
    m3_copies = coarse_send(0)
    wait_sent(u_copies)
    d_copies = fine_send(d, 4, 0, 0, 0)

    wait_arrived(u_copies)
    for f in range(2):
        k = 1 + 15 * f
        u2[k, :, IN, :] = u2[k, :, IN, :] + gxf[f] * xr[2, f]
        dl[f] = gyf[f] * yr[2, f]
    add_rows(u2, 1, 8)
    pack_rows(u2, 3)
    u2_copies = fine_send(u2, 3)

    def third_sum(i):
        c, total = fine_sum(u2, i)
        before = u[i + 1, :, IN, :]
        g[i] = dg[i] * (BETA * c - GAMMA * before) + total
        px[i + 1, :, IN, :] = px[i + 1, :, IN, :] + before + c

    planes(0, 16, 4, third_sum)

    def mid_coefficients(i):
        c = m2[i, :, IN, :]
        below = 0.5 * (c + m2[i - 1, :, IN, :])
        above = 0.5 * (c + m2[i + 1, :, IN, :])
        left = c + m2[i, :, LO, :]
        right = 0.5 * (c + m2[i, :, HI, :])
        after = 0.5 * (c + mid_next(c))
        before = c + mid_before(c)
        kx2[i] = below
        kx2[i + 1] = above
        ky2[i, :, IN, :] = right
        kz2[i] = after
        diagonal = (S2 + below + above + right + after) + 0.5 * (left + before)
        d2[i] = diagonal
        w2[i, :, IN, :] = INV / diagonal

    planes(1, 15, 7, mid_coefficients)
    coarse_wait(m3_copies, 0, cm)
    mob = cm[...]
    lap = weighted_sum(mob)
    cw[1:13] = 0.8 / (S3 + 0.5 * (5.0 * mob[1:-1] + lap))
    for x in range(4):
        cstage[1, 4 * x : 4 * x + 4, :] = cw[5 + x, 5:9, :]
    w3_copies = coarse_send(1)
    for x in range(8):
        mid_b[2, x] = w2[4 + x, :, 12:20, :]
    mid_fold(2, [mid_b[2, x] for x in range(8)])
    wait_sent(u2_copies)
    w2_copies = mid_send(2)

    wait_arrived(u2_copies)
    for f in range(2):
        g[15 * f] = g[15 * f] + kx[16 * f] * xr[3, f]
        dl[f] = kyf[f] * yr[3, f]
    add_rows(g, 0, 0)
    mid_put(1, restrict_fine(g, 0, 0, 0.5))
    b2_copies = mid_send(1)

    pack_rows(px, 6, 1)
    coarse_wait(w3_copies, 1, cw)
    weight = cw[...]
    y = jnp.ones_like(weight)
    psi = y
    for k in range(3):
        inner = slice(k, 14 - k)
        y = y[1:-1] - coarse_operator(weight[inner] * y, mob[inner], lap[k : 12 - k])
        psi = psi[1:-1] + y
    ce[3:11] = 0.5 - (0.5 * S3) * (weight[3:11] * psi)

    def double_rows():
        for x in range(8):
            for h in range(2):
                t2[x, pl.ds(h, 8, stride=2), :] = ce[3 + x, 3:11, :]

    def double(x):
        v = t2[x]
        return jnp.stack([v, v], axis=0)

    double_rows()
    for x in range(8):
        v = double(x)
        for q in range(2):
            va[2 * x + q, :, IN, :] = v

    def adjoint_one(i):
        c, total = mid_sum(va, i)
        vb[i, :, IN, :] = w2[i, :, IN, :] * (d2[i] * c - total)

    planes(3, 13, 5, adjoint_one)

    def adjoint_two(i):
        c, total = mid_sum(vb, i)
        x2[i] = va[i, :, IN, :] - (1.0 + ALPHA) * c - STEP * (w2[i, :, IN, :] * total)

    planes(4, 12, 4, adjoint_two)
    part = jnp.zeros((2, 8, 128), F32)
    for x in range(8):
        part = part + x2[4 + x, :, 4:12, :] * mid_b[1, x]
    partm = jnp.zeros((4, 128), F32)
    for x in range(4):
        partm = partm + cstage[0, 4 * x : 4 * x + 4, :]
    ar1[0, 0:1, :] = jnp.sum(part[0] + part[1], axis=0, keepdims=True)
    ar1[0, 1:2, :] = jnp.sum(partm, axis=0, keepdims=True)
    wait_sent(b2_copies)
    sums = []
    for o in range(1, nx):
        sums.append(remote(ar1.at[0], ar1.at[o], as1.at[o], ar1s.at[o], o, 0))
        sums[-1].start()
    far_copies = fine_send(mf, 5, 1) + corner_send(mf, 0)
    wait(w2_copies)
    mid_place(2, w2)
    for f in range(2):
        xr[1, f] = xr[1, f] + xr[2, f] + xr[3, f]
        yr[1, f] = yr[1, f] + yr[2, f] + yr[3, f]
    mid_own(1, b2)
    wait_arrived(b2_copies)
    mid_place(1, b2)

    def mid_one(i):
        va[i, :, IN, :] = w2[i, :, IN, :] * b2[i, :, IN, :]

    planes(0, 16, 8, mid_one)

    def mid_two(i):
        c, total = mid_sum(va, i)
        step = ALPHA * c + STEP * (w2[i, :, IN, :] * total)
        vb[i, :, IN, :] = step
        x2[i] = c + step

    planes(1, 15, 7, mid_two)

    def mid_three(i):
        c, total = mid_sum(vb, i)
        rr[i] = d2[i] * (BETA * c - GAMMA * va[i, :, IN, :]) + total

    planes(4, 12, 4, mid_three)
    coarse_block(rr, 2, 4, 0.5)
    b3_copies = coarse_send(2)

    wait(sums)
    total = ar1[0]
    for o in range(1, nx):
        total = total + ar1[o]
    ar2[0] = total
    sums = []
    for o in range(1, ny):
        sums.append(remote(ar2.at[0], ar2.at[o], as2.at[o], ar2s.at[o], 0, o))
        sums[-1].start()
    wait_sent(b3_copies)
    x1_copies = fine_send(px, 6, 1) + corner_send(px, 1)

    wait(d_copies)
    wait(far_copies)

    def corners(f):
        return ((0, 1), (2, 3), (0, 2), (1, 3))[f]

    for f in range(4):
        first, second = (xr.at[0, f], xr.at[5, f]) if f < 2 else (yr.at[0, f - 2], yr.at[5, f - 2])
        k01 = kx[16 * f] if f < 2 else kyf[f - 2]
        c = first[...]
        vf[f, :, IN, :] = c
        for row, k in zip((7, 24), corners(f)):
            for t in range(4):
                vf[f, t, row : row + 1, :] = crn[0, k, t : t + 1, :]
        ktf[f, :, IN, :] = 0.5 * (c + vf[f, :, HI, :])
        ktf[f, :, 7:8, :] = 0.5 * (vf[f, :, 7:8, :] + vf[f, :, 8:9, :])
        k12 = 0.5 * (c + second[...])
        after = 0.5 * (c + fine_next(c))
        k12f[f] = k12
        kzf[f] = after
        wf[f] = INV / (
            S1 + k01 + k12 + ktf[f, :, IN, :] + ktf[f, :, LO, :] + after + fine_before(after)
        )

    coarse_wait(b3_copies, 2, cb, False)
    rhs = cb[...]
    e = weight * rhs
    for k in range(3):
        inner = slice(k, 14 - k)
        e = e[1:-1] + weight[k + 1 : 13 - k] * (
            rhs[k + 1 : 13 - k] - coarse_operator(e, mob[inner], lap[k : 12 - k])
        )
    wait(sums)
    total = ar2[0]
    for o in range(1, ny):
        total = total + ar2[o]
    cells = 16.0 * 128.0 * nx * ny
    sum_f = jnp.sum(total[0:1, :], axis=1, keepdims=True)
    sum_m = jnp.sum(total[1:2, :], axis=1, keepdims=True)
    kappa = 0.8 * (sum_f / cells) / (S3 + 5.0 * (sum_m / cells))

    ce[3:11] = e + kappa
    double_rows()
    for x in range(8):
        v = double(x)
        for q in range(2):
            if 0 < 2 * x + q < 15:
                va[2 * x + q, :, IN, :] = x2[2 * x + q] + v

    def post_one(i):
        c, total = mid_sum(va, i)
        vb[i, :, IN, :] = w2[i, :, IN, :] * (b2[i, :, IN, :] + total) - INV * c

    planes(2, 14, 6, post_one)

    def post_two(i):
        c, total = mid_sum(vb, i)
        base[i - 3] = (
            va[i, :, IN, :] + (1.0 + ALPHA) * c + STEP * (w2[i, :, IN, :] * total)
        )

    planes(3, 13, 5, post_two)
    for t in range(2):
        lanes = slice(128 * t, 128 * t + 128)
        for x in range(8):
            pout[8 * x : 8 * x + 8, lanes] = base[1 + x, t, 4:12, :]
            for f in range(2):
                row = 3 + 9 * f
                pout[80 + 8 * f + x : 81 + 8 * f + x, lanes] = base[1 + x, t, row : row + 1, :]
        for f in range(2):
            pout[64 + 8 * f : 72 + 8 * f, lanes] = base[9 * f, t, 4:12, :]
        for k in range(4):
            row = 3 + 9 * (k % 2)
            pout[96 + k : 97 + k, lanes] = base[9 * (k // 2), t, row : row + 1, :]
    pout[...] = exact_dot(pout[:, 0:256], pmat[...])
    wait(x1_copies)

    for j in range(8):
        for t in range(4):
            v = pout[8 * j : 8 * j + 8, 128 * t : 128 * t + 128]
            for q in range(2):
                for h in range(2):
                    rows = pl.ds(8 + h, 8, stride=2)
                    px[2 * j + 1 + q, t, rows, :] = px[2 * j + 1 + q, t, rows, :] + v
    for f in range(4):
        first, second = (xr.at[1, f], xr.at[6, f]) if f < 2 else (yr.at[1, f - 2], yr.at[6, f - 2])
        for t in range(4):
            lanes = slice(128 * t, 128 * t + 128)
            v = pout[64 + 8 * f : 72 + 8 * f, lanes]
            for h in range(2):
                rows = pl.ds(h, 8, stride=2)
                vf[f, t, pl.ds(8 + h, 8, stride=2), :] = first[t, rows, :] + v
                v2f[f, t, rows, :] = second[t, rows, :] + v
            for row, k in zip((7, 24), corners(f)):
                vf[f, t, row : row + 1, :] = crn[1, k, t : t + 1, :] + pout[96 + k : 97 + k, lanes]
    pack_rows(px, 1)
    for f in range(2):
        d[15 * f] = d[15 * f] + kx[16 * f] * vf[f, :, IN, :]
        dl[f] = kyf[f] * vf[2 + f, :, IN, :]
    add_rows(d, 0, 0)

    for f in range(4):
        if f < 2:
            k01, inside, rhs_f = kx[16 * f], px[1 + 15 * f, :, IN, :], xr[4, f]
        else:
            k01, inside, rhs_f = kyf[f - 2], ys[1, f - 2], yr[4, f - 2]
        c = vf[f, :, IN, :]
        z = kzf[f]
        total = k01 * inside + k12f[f] * v2f[f]
        total = total + ktf[f, :, LO, :] * vf[f, :, LO, :] + ktf[f, :, IN, :] * vf[f, :, HI, :]
        total = total + z * fine_next(c) + fine_before(z * c)
        uf[f] = wf[f] * (rhs_f + total) - INV * c

    def fourth_sum(i):
        c, total = fine_sum(px, i)
        u[i + 1, :, IN, :] = w[i] * (d[i] + total) - INV * c

    planes(0, 16, 4, fourth_sum)

    def last_sum(i):
        c, total = fine_sum(u, i)
        g[i] = px[i + 1, :, IN, :] + (1.0 + ALPHA) * c + STEP * (w[i] * total)

    planes(0, 16, 4, last_sum)
    for f in range(2):
        g[15 * f] = g[15 * f] + gxf[f] * uf[f]
        dl[f] = gyf[f] * uf[2 + f]
    add_rows(g, 0, 0)
    for i in range(16):
        for t in range(4):
            out[i, :, 128 * t : 128 * t + 128] = g[i, t]


def solution(mesh):
    nx, ny = mesh.shape["gx"], mesh.shape["gy"]

    def local(p, d, m):
        vm = lambda *s: pltpu.VMEM(s, F32)
        sem = lambda *s: pltpu.SemaphoreType.DMA(s)
        plane = (16, 4, 16, 128)
        face = (4, 16, 128)
        scratch = [
            vm(18, 4, 32, 128), vm(18, 4, 32, 128), vm(18, 4, 32, 128), vm(18, 4, 32, 128),
            vm(*plane), vm(*plane), vm(*plane), vm(*plane),
            vm(17, 4, 16, 128), vm(16, 4, 32, 128), vm(*plane),
            vm(7, 2, *face), vm(7, 2, *face), vm(7, 2, *face),
            vm(2, *face), vm(2, *face), vm(2, *face), vm(2, *face), vm(64, 512),
            pltpu.VMEM((512, 256), BF16), pltpu.VMEM((256, 512), BF16), vm(104, 512),
            vm(3, 8, 2, 8, 128), vm(3, 2, 4, 2, 8, 128), vm(3, 2, 4, 2, 8, 128),
            vm(3, 2, 4, 2, 8, 128), vm(3, 2, 2, 2, 2, 8, 128),
            vm(16, 2, 32, 128), vm(16, 2, 32, 128), vm(16, 2, 32, 128), vm(16, 2, 16, 128),
            vm(17, 2, 16, 128), vm(16, 2, 32, 128), vm(16, 2, 16, 128),
            vm(16, 2, 32, 128), vm(16, 2, 32, 128), vm(16, 2, 16, 128), vm(16, 2, 16, 128),
            vm(3, 16, 128), vm(3, 8, 16, 128), vm(14, 16, 128), vm(14, 16, 128), vm(14, 16, 128),
            vm(14, 16, 128), vm(8, 16, 128),
            vm(10, 2, 16, 128), vm(3, 4, 4, 128), vm(3, 16, 4, 128),
            vm(nx, 2, 128), vm(ny, 2, 128),
            vm(2, 4, 4, 128), vm(2, 4, 4, 128), vm(4, 4, 32, 128), vm(4, *face), vm(4, 4, 32, 128),
            vm(4, *face), vm(4, *face), vm(4, *face), vm(4, *face),
            sem(3, 4), sem(9, 4), sem(9, 4), sem(3, 8), sem(3, 8), sem(3, 24), sem(3, 24),
            sem(nx), sem(nx), sem(ny), sem(ny),
        ]
        return pl.pallas_call(
            functools.partial(kernel, nx, ny),
            out_shape=jax.ShapeDtypeStruct((16, 16, 512), F32),
            in_specs=[pl.BlockSpec(memory_space=pl.ANY)] * 3,
            out_specs=pl.BlockSpec(memory_space=pltpu.VMEM),
            scratch_shapes=scratch,
            compiler_params=pltpu.CompilerParams(
                collective_id=0, has_side_effects=True, vmem_limit_bytes=30 * 1024 * 1024
            ),
        )(*[pltpu.with_memory_space_constraint(a, pltpu.HBM) for a in (p, d, m)])

    spec = P("gx", "gy", None)
    return jax.shard_map(
        local, mesh=mesh, in_specs=(spec, spec, spec), out_specs=spec, check_vma=False
    )
```

```python
import functools

import jax
import jax.numpy as jnp
from jax import lax
from jax.experimental import pallas as pl
from jax.experimental.pallas import tpu as pltpu
from jax.sharding import PartitionSpec as P

MESH = pl.DeviceIdType.MESH
F32 = jnp.float32
BF16 = jnp.bfloat16

S1 = 0.05
S2 = 0.2
S3 = 0.8
MIDPOINT = (2.0 + 0.3) / 2
HALFWIDTH = (2.0 - 0.3) / 2
SIGMA = MIDPOINT / HALFWIDTH
P1 = 1.0 / SIGMA
P2 = 1.0 / (2.0 * SIGMA - P1)
CA = P2 * P1
CB = 2.0 * P2 / HALFWIDTH
INV = 1.0 / MIDPOINT
ALPHA = CA + CB * (MIDPOINT - 1.0)
STEP = CB * MIDPOINT
BETA = 1.0 / CB - 1.0
GAMMA = CA / CB
FAR = [(x, y) for x in range(-2, 3) for y in range(-2, 3) if max(abs(x), abs(y)) == 2]
NEAR = [(-1, 0), (1, 0), (0, -1), (0, 1), (-1, -1), (-1, 1), (1, -1), (1, 1)]


def thirds(x):
    high = x.astype(BF16)
    rest = x - high.astype(F32)
    middle = rest.astype(BF16)
    low = (rest - middle.astype(F32)).astype(BF16)
    return high, middle, low


def exact_dot(x, matrix):
    total = None
    for part in thirds(x):
        term = jnp.dot(part, matrix, preferred_element_type=F32)
        total = term if total is None else total + term
    return total


def weighted_sum(f):
    q = pltpu.roll(f, 1, 2) + pltpu.roll(f, f.shape[2] - 1, 2)
    face = 0.5 * f + 0.125 * q
    edge = 0.125 * f + 0.0625 * q
    rows = f.shape[1]
    a = 0.5 * q + (pltpu.roll(face, 1, 1) + pltpu.roll(face, rows - 1, 1))
    b = face + (pltpu.roll(edge, 1, 1) + pltpu.roll(edge, rows - 1, 1))
    return a[1:-1] + (b[:-2] + b[2:])


def coarse_operator(v, mob, mob_sum):
    c = v[1:-1]
    m = mob[1:-1]
    return S3 * c + 0.5 * (
        5.0 * m * c - m * weighted_sum(v) + c * mob_sum - weighted_sum(mob * v)
    )


def fine_next(v):
    turned = pltpu.roll(v, 127, 2)
    lane = lax.broadcasted_iota(jnp.int32, v.shape, 2)
    return jnp.where(lane == 127, jnp.concatenate([turned[1:], turned[:1]], axis=0), turned)


def fine_before(v):
    turned = pltpu.roll(v, 1, 2)
    lane = lax.broadcasted_iota(jnp.int32, v.shape, 2)
    return jnp.where(lane == 0, jnp.concatenate([turned[3:], turned[:3]], axis=0), turned)


def mid_next(v):
    return jnp.concatenate([v[1:], pltpu.roll(v[:1], 127, 2)], axis=0)


def mid_before(v):
    return jnp.concatenate([pltpu.roll(v[1:], 1, 2), v[:1]], axis=0)


def kernel(
    nx, ny,
    p_hbm, d_hbm, m_hbm, out,
    px, mf, u, u2, d, g, dg, w, kx, ky, kz,
    xr, ys, yr, kyf, gyf, gxf, dl, rs, tmat, pmat, pout,
    mid_b, mid_stage, mid_rx, mid_ry, mid_rc, b2, m2, w2, d2, kx2, ky2, kz2,
    va, vb, rr, x2,
    cstage, crecv, cm, cw, cb, ce, t2,
    base, cedge, cfar,
    ar1, ar2,
    cst, crn, vf, v2f, ktf, k12f, kzf, wf, uf,
    in_sem, fs, fr, ms, mr, cs, cr, as1, ar1s, as2, ar2s,
):
    gx = lax.axis_index("gx")
    gy = lax.axis_index("gy")
    IN = slice(8, 24)
    LO = slice(7, 23)
    HI = slice(9, 25)

    def device(ox, oy):
        return (lax.rem(gx + (ox % nx), nx), lax.rem(gy + (oy % ny), ny))

    peers = {(o, 0) for o in range(1, nx)} | {(0, o) for o in range(1, ny)}
    peers |= {(dx % nx, dy % ny) for dx, dy in NEAR + FAR}
    peers = sorted(peers - {(0, 0)})

    loads = []
    for n, (src, dst) in enumerate(
        ((m_hbm, mf.at[1:17, :, IN, :]), (p_hbm, px.at[1:17, :, IN, :]), (d_hbm, d))
    ):
        loads.append(
            [
                pltpu.make_async_copy(
                    src.at[:, :, 128 * t : 128 * t + 128], dst.at[:, t], in_sem.at[n, t]
                )
                for t in range(4)
            ]
        )
        for c in loads[-1]:
            c.start()
    barrier = pltpu.get_barrier_semaphore()
    for ox, oy in peers:
        pl.semaphore_signal(barrier, inc=1, device_id=device(ox, oy), device_id_type=MESH)

    def remote(src, dst, ssem, rsem, ox, oy):
        return pltpu.make_async_remote_copy(
            src_ref=src, dst_ref=dst, send_sem=ssem, recv_sem=rsem,
            device_id=device(ox, oy), device_id_type=MESH,
        )

    def planes(start, stop, width, body):
        def several(j, carry):
            for q in range(width):
                body(start + width * j + q)
            return carry

        lax.fori_loop(0, (stop - start) // width, several, 0)

    zeros = jnp.zeros((4, 8, 128), F32)
    rims = (mf, px, u, u2)
    for a in rims:
        for plane in (0, 17):
            a[plane, :, 8:16, :] = zeros
            a[plane, :, 16:24, :] = zeros

    def clear(i):
        for a in rims:
            a[i + 1, :, 0:8, :] = zeros
            a[i + 1, :, 24:32, :] = zeros
        ky[i, :, 0:8, :] = zeros

    planes(0, 16, 2, clear)

    zi = lax.broadcasted_iota(jnp.int32, tmat.shape, 0)
    ci = lax.broadcasted_iota(jnp.int32, tmat.shape, 1)
    hit = (zi >> 1) == (((ci & 127) << 1) + (ci >> 7))
    tmat[...] = jnp.where(hit, 1.0, 0.0).astype(BF16)
    zi = lax.broadcasted_iota(jnp.int32, pmat.shape, 1)
    ci = lax.broadcasted_iota(jnp.int32, pmat.shape, 0)
    hit = (zi >> 1) == (((ci & 127) << 1) + (ci >> 7))
    pmat[...] = jnp.where(hit, 1.0, 0.0).astype(BF16)

    def pack_rows(arr, n, layer=0, off=1, row=8):
        low, high = row + layer, row + 15 - layer
        for x in range(16):
            ys[n, 0, :, x : x + 1, :] = arr[x + off, :, low : low + 1, :]
            ys[n, 1, :, x : x + 1, :] = arr[x + off, :, high : high + 1, :]

    def fine_send(arr, n, layer=0, off=1, row=8):
        rows = slice(row, row + 16)
        low, high = arr.at[off + layer, :, rows, :], arr.at[off + 15 - layer, :, rows, :]
        copies = [
            remote(low, xr.at[n, 1], fs.at[n, 0], fr.at[n, 0], -1, 0),
            remote(high, xr.at[n, 0], fs.at[n, 1], fr.at[n, 1], 1, 0),
            remote(ys.at[n, 0], yr.at[n, 1], fs.at[n, 2], fr.at[n, 2], 0, -1),
            remote(ys.at[n, 1], yr.at[n, 0], fs.at[n, 3], fr.at[n, 3], 0, 1),
        ]
        for c in copies:
            c.start()
        return copies

    def wait(copies):
        for c in copies:
            c.wait()

    def wait_sent(copies):
        for c in copies:
            c.wait_send()

    def wait_arrived(copies):
        for c in copies:
            c.wait_recv()

    def corner_send(arr, n):
        copies = []
        for k, (dx, dy) in enumerate(NEAR[4:]):
            x, y = 1 + 15 * (k // 2), 8 + 15 * (k % 2)
            for t in range(4):
                cst[n, k, t : t + 1, :] = arr[x, t, y : y + 1, :]
            copies.append(
                remote(cst.at[n, k], crn.at[n, 3 - k], fs.at[7 + n, k], fr.at[7 + n, k], dx, dy)
            )
            copies[-1].start()
        return copies

    def restrict_fine(arr, off, row, scale):
        for j in range(8):
            for t in range(4):
                total = None
                for q in range(2):
                    for h in range(2):
                        part = arr[2 * j + q + off, t, pl.ds(row + h, 8, stride=2), :]
                        total = part if total is None else total + part
                rs[8 * j : 8 * j + 8, 128 * t : 128 * t + 128] = total * scale
        return exact_dot(rs[...], tmat[...])

    def mid_put(n, got):
        blocks = []
        for x in range(8):
            rows = got[8 * x : 8 * x + 8]
            v = jnp.stack([rows[:, :128], rows[:, 128:]], axis=0)
            mid_b[n, x] = v
            blocks.append(v)
        mid_fold(n, blocks)

    def mid_fold(n, blocks):
        low = lax.broadcasted_iota(jnp.int32, (2, 8, 128), 1) < 4
        for t in range(4):
            a, b = blocks[2 * t], blocks[2 * t + 1]
            mid_stage[n, 0, t] = jnp.where(low, a, pltpu.roll(b, 4, 1))
            mid_stage[n, 1, t] = jnp.where(low, pltpu.roll(a, 4, 1), b)

    def mid_send(n):
        copies = [
            remote(mid_b.at[n, 0:4], mid_rx.at[n, 1], ms.at[n, 0], mr.at[n, 0], -1, 0),
            remote(mid_b.at[n, 4:8], mid_rx.at[n, 0], ms.at[n, 1], mr.at[n, 1], 1, 0),
            remote(mid_stage.at[n, 0], mid_ry.at[n, 1], ms.at[n, 2], mr.at[n, 2], 0, -1),
            remote(mid_stage.at[n, 1], mid_ry.at[n, 0], ms.at[n, 3], mr.at[n, 3], 0, 1),
        ]
        k = 4
        for i, dx in enumerate((-1, 1)):
            for j, dy in enumerate((-1, 1)):
                copies.append(
                    remote(
                        mid_stage.at[n, j, 2 * i : 2 * i + 2], mid_rc.at[n, 1 - i, 1 - j],
                        ms.at[n, k], mr.at[n, k], dx, dy,
                    )
                )
                k += 1
        for c in copies:
            c.start()
        return copies

    def mid_place(n, ext):
        for i in range(2):
            for x in range(4):
                ext[12 * i + x, :, 12:20, :] = mid_rx[n, i, x]
            for t in range(4):
                for q in range(2):
                    ext[4 + 2 * t + q, :, 8 + 12 * i : 12 + 12 * i, :] = mid_ry[
                        n, i, t, :, 4 * q : 4 * q + 4, :
                    ]
            for j in range(2):
                for t in range(2):
                    for q in range(2):
                        ext[12 * i + 2 * t + q, :, 8 + 12 * j : 12 + 12 * j, :] = mid_rc[
                            n, i, j, t, :, 4 * q : 4 * q + 4, :
                        ]

    def mid_own(n, ext):
        for x in range(8):
            ext[4 + x, :, 12:20, :] = mid_b[n, x]

    def coarse_block(arr, n, first, row, scale):
        for x in range(4):
            total = None
            for q in range(2):
                for t in range(2):
                    for h in range(2):
                        part = arr[first + 2 * x + q, t, pl.ds(row + h, 4, stride=2), :]
                        total = part if total is None else total + part
            cstage[n, 4 * x : 4 * x + 4, :] = total * scale

    def coarse_send(n):
        copies = []
        for k, (dx, dy) in enumerate(NEAR):
            copies.append(
                remote(cstage.at[n], crecv.at[n, k], cs.at[n, k], cr.at[n, k], dx, dy)
            )
            copies[-1].start()
        cedge[n, 0] = cstage[n, 0:4, :]
        cedge[n, 1] = cstage[n, 12:16, :]
        for x in range(4):
            for k in range(2):
                cedge[n, 2 + k, x : x + 1, :] = cstage[n, 4 * x + 3 * k : 4 * x + 3 * k + 1, :]
        for k, (dx, dy) in enumerate(FAR):
            side = (dx == 2) if abs(dx) == 2 else 2 + (dy == 2)
            copies.append(
                remote(
                    cedge.at[n, int(side)], cfar.at[n, k],
                    cs.at[n, 8 + k], cr.at[n, 8 + k], dx, dy,
                )
            )
            copies[-1].start()
        return copies

    def coarse_wait(copies, n, ext, sent=True):
        def place(dx, dy, block):
            for x in range(4):
                ext[4 * dx + 5 + x, 4 * dy + 5 : 4 * dy + 9, :] = block[4 * x : 4 * x + 4, :]

        place(0, 0, cstage.at[n])
        if sent:
            wait_sent(copies)
        wait_arrived(copies)
        for k, (dx, dy) in enumerate(NEAR):
            place(-dx, -dy, crecv.at[n, k])
        for k, (dx, dy) in enumerate(FAR):
            far = cfar.at[n, k]
            if abs(dx) == 2:
                plane = 0 if dx == 2 else 13
                if abs(dy) == 2:
                    row, at = (0, 3) if dy == 2 else (13, 0)
                    ext[plane, row : row + 1, :] = far[at : at + 1, :]
                else:
                    ext[plane, 5 - 4 * dy : 9 - 4 * dy, :] = far[...]
            else:
                row = 0 if dy == 2 else 13
                for x in range(4):
                    ext[5 - 4 * dx + x, row : row + 1, :] = far[x : x + 1, :]

    def fine_sum(arr, i):
        c = arr[i + 1, :, IN, :]
        z = kz[i]
        total = kx[i] * arr[i, :, IN, :] + kx[i + 1] * arr[i + 2, :, IN, :]
        total = total + ky[i, :, LO, :] * arr[i + 1, :, LO, :]
        total = total + ky[i, :, IN, :] * arr[i + 1, :, HI, :]
        return c, total + z * fine_next(c) + fine_before(z * c)

    def mid_sum(arr, i):
        c = arr[i, :, IN, :]
        z = kz2[i]
        total = kx2[i] * arr[i - 1, :, IN, :] + kx2[i + 1] * arr[i + 1, :, IN, :]
        total = total + ky2[i, :, LO, :] * arr[i, :, LO, :]
        total = total + ky2[i, :, IN, :] * arr[i, :, HI, :]
        return c, total + z * mid_next(c) + mid_before(z * c)

    def add_rows(arr, off, row):
        for x in range(16):
            for f in range(2):
                k = row + 15 * f
                arr[x + off, :, k : k + 1, :] = (
                    arr[x + off, :, k : k + 1, :] + dl[f, :, x : x + 1, :]
                )

    wait(loads[0])
    pack_rows(mf, 0)
    mid_put(0, restrict_fine(mf, 1, 8, 0.125))
    coarse_block(mid_b.at[0], 0, 0, 0, 0.125)
    wait(loads[1])
    pack_rows(px, 1)
    wait(loads[2])
    pl.semaphore_wait(barrier, len(peers))
    m_copies = fine_send(mf, 0)
    p_copies = fine_send(px, 1)

    def coefficients(i):
        c = mf[i + 1, :, IN, :]
        below = 0.5 * (c + mf[i, :, IN, :])
        above = c + mf[i + 2, :, IN, :]
        left = c + mf[i + 1, :, LO, :]
        right = 0.5 * (c + mf[i + 1, :, HI, :])
        after = 0.5 * (c + fine_next(c))
        before = c + fine_before(c)
        kx[i] = below
        ky[i, :, IN, :] = right
        kz[i] = after
        dg[i] = (S1 + below + right + after) + 0.5 * (above + left + before)

    planes(0, 16, 4, coefficients)
    kx[16] = 0.5 * mf[16, :, IN, :]

    def first_sum(i):
        c, total = fine_sum(px, i)
        g[i] = d[i] + total

    planes(0, 16, 4, first_sum)
    pack_rows(d, 4, 0, 0, 0)
    pack_rows(mf, 5, 1)
    wait_sent(m_copies)
    wait_sent(p_copies)
    m3_copies = coarse_send(0)
    m2_copies = mid_send(0)

    wait_arrived(m_copies)
    for f in range(2):
        face = 0.5 * xr[0, f]
        kx[16 * f] = kx[16 * f] + face
        dg[15 * f] = dg[15 * f] + face
        face = 0.5 * yr[0, f]
        kyf[f] = 0.5 * ys[0, f] + face
        dl[f] = face
    add_rows(dg, 0, 0)
    wait_arrived(p_copies)
    for f in range(2):
        g[15 * f] = g[15 * f] + kx[16 * f] * xr[1, f]
        dl[f] = kyf[f] * yr[1, f]
    add_rows(g, 0, 0)

    def first_step(i):
        weight = INV / dg[i]
        w[i] = weight
        u[i + 1, :, IN, :] = weight * g[i] - INV * px[i + 1, :, IN, :]

    planes(0, 16, 4, first_step)
    pack_rows(u, 2)
    u_copies = fine_send(u, 2)

    def second_sum(i):
        c, total = fine_sum(u, i)
        u2[i + 1, :, IN, :] = ALPHA * c + STEP * (w[i] * total)

    planes(0, 16, 4, second_sum)
    for x in range(16):
        for f in range(2):
            gyf[f, :, x : x + 1, :] = w[x, :, 15 * f : 15 * f + 1, :]
    for f in range(2):
        gyf[f] = STEP * (gyf[f] * kyf[f])
        gxf[f] = STEP * (w[15 * f] * kx[16 * f])
    mid_own(0, m2)
    wait(m2_copies)
    mid_place(0, m2)
    def mid_coefficients(i):
        c = m2[i, :, IN, :]
        below = 0.5 * (c + m2[i - 1, :, IN, :])
        above = 0.5 * (c + m2[i + 1, :, IN, :])
        left = c + m2[i, :, LO, :]
        right = 0.5 * (c + m2[i, :, HI, :])
        after = 0.5 * (c + mid_next(c))
        before = c + mid_before(c)
        kx2[i] = below
        kx2[i + 1] = above
        ky2[i, :, IN, :] = right
        kz2[i] = after
        diagonal = (S2 + below + above + right + after) + 0.5 * (left + before)
        d2[i] = diagonal
        w2[i, :, IN, :] = INV / diagonal

    planes(1, 15, 7, mid_coefficients)
    coarse_wait(m3_copies, 0, cm)
    mob = cm[...]
    lap = weighted_sum(mob)
    cw[1:13] = 0.8 / (S3 + 0.5 * (5.0 * mob[1:-1] + lap))
    for x in range(4):
        cstage[1, 4 * x : 4 * x + 4, :] = cw[5 + x, 5:9, :]
    for x in range(8):
        mid_b[2, x] = w2[4 + x, :, 12:20, :]
    mid_fold(2, [mid_b[2, x] for x in range(8)])
    wait_sent(u_copies)
    w3_copies = coarse_send(1)
    w2_copies = mid_send(2)

    wait_arrived(u_copies)
    for f in range(2):
        k = 1 + 15 * f
        u2[k, :, IN, :] = u2[k, :, IN, :] + gxf[f] * xr[2, f]
        dl[f] = gyf[f] * yr[2, f]
    add_rows(u2, 1, 8)
    pack_rows(u2, 3)
    u2_copies = fine_send(u2, 3)

    def third_sum(i):
        c, total = fine_sum(u2, i)
        before = u[i + 1, :, IN, :]
        g[i] = dg[i] * (BETA * c - GAMMA * before) + total
        px[i + 1, :, IN, :] = px[i + 1, :, IN, :] + before + c

    planes(0, 16, 4, third_sum)
    wait_sent(u2_copies)
    d_copies = fine_send(d, 4, 0, 0, 0)
    coarse_wait(w3_copies, 1, cw)
    weight = cw[...]
    y = jnp.ones_like(weight)
    psi = y
    for k in range(3):
        inner = slice(k, 14 - k)
        y = y[1:-1] - coarse_operator(weight[inner] * y, mob[inner], lap[k : 12 - k])
        psi = psi[1:-1] + y
    ce[3:11] = 0.5 - (0.5 * S3) * (weight[3:11] * psi)

    def double_rows():
        for x in range(8):
            for h in range(2):
                t2[x, pl.ds(h, 8, stride=2), :] = ce[3 + x, 3:11, :]

    def double(x):
        v = t2[x]
        return jnp.stack([v, v], axis=0)

    double_rows()
    for x in range(8):
        v = double(x)
        for q in range(2):
            va[2 * x + q, :, IN, :] = v

    def adjoint_one(i):
        c, total = mid_sum(va, i)
        vb[i, :, IN, :] = w2[i, :, IN, :] * (d2[i] * c - total)

    planes(3, 13, 5, adjoint_one)

    def adjoint_two(i):
        c, total = mid_sum(vb, i)
        x2[i] = va[i, :, IN, :] - (1.0 + ALPHA) * c - STEP * (w2[i, :, IN, :] * total)

    planes(4, 12, 4, adjoint_two)
    wait(w2_copies)
    mid_place(2, w2)

    wait_arrived(u2_copies)
    for f in range(2):
        g[15 * f] = g[15 * f] + kx[16 * f] * xr[3, f]
        dl[f] = kyf[f] * yr[3, f]
    add_rows(g, 0, 0)
    mid_put(1, restrict_fine(g, 0, 0, 0.5))
    b2_copies = mid_send(1)

    pack_rows(px, 6, 1)
    part = jnp.zeros((2, 8, 128), F32)
    for x in range(8):
        part = part + x2[4 + x, :, 4:12, :] * mid_b[1, x]
    partm = jnp.zeros((4, 128), F32)
    for x in range(4):
        partm = partm + cstage[0, 4 * x : 4 * x + 4, :]
    ar1[0, 0:1, :] = jnp.sum(part[0] + part[1], axis=0, keepdims=True)
    ar1[0, 1:2, :] = jnp.sum(partm, axis=0, keepdims=True)
    wait_sent(b2_copies)
    sums = []
    for o in range(1, nx):
        sums.append(remote(ar1.at[0], ar1.at[o], as1.at[o], ar1s.at[o], o, 0))
        sums[-1].start()
    far_copies = fine_send(mf, 5, 1) + corner_send(mf, 0)
    for f in range(2):
        xr[1, f] = xr[1, f] + xr[2, f] + xr[3, f]
        yr[1, f] = yr[1, f] + yr[2, f] + yr[3, f]
    mid_own(1, b2)
    wait_arrived(b2_copies)
    mid_place(1, b2)

    def mid_one(i):
        va[i, :, IN, :] = w2[i, :, IN, :] * b2[i, :, IN, :]

    planes(0, 16, 8, mid_one)

    def mid_two(i):
        c, total = mid_sum(va, i)
        step = ALPHA * c + STEP * (w2[i, :, IN, :] * total)
        vb[i, :, IN, :] = step
        x2[i] = c + step

    planes(1, 15, 7, mid_two)

    def mid_three(i):
        c, total = mid_sum(vb, i)
        rr[i] = d2[i] * (BETA * c - GAMMA * va[i, :, IN, :]) + total

    planes(4, 12, 4, mid_three)
    coarse_block(rr, 2, 4, 4, 0.5)
    b3_copies = coarse_send(2)

    wait(sums)
    total = ar1[0]
    for o in range(1, nx):
        total = total + ar1[o]
    ar2[0] = total
    sums = []
    for o in range(1, ny):
        sums.append(remote(ar2.at[0], ar2.at[o], as2.at[o], ar2s.at[o], 0, o))
        sums[-1].start()
    wait_sent(b3_copies)
    x1_copies = fine_send(px, 6, 1) + corner_send(px, 1)

    wait(d_copies)
    wait(far_copies)

    def corners(f):
        return ((0, 1), (2, 3), (0, 2), (1, 3))[f]

    for f in range(4):
        first, second = (xr.at[0, f], xr.at[5, f]) if f < 2 else (yr.at[0, f - 2], yr.at[5, f - 2])
        k01 = kx[16 * f] if f < 2 else kyf[f - 2]
        c = first[...]
        vf[f, :, IN, :] = c
        for row, k in zip((7, 24), corners(f)):
            for t in range(4):
                vf[f, t, row : row + 1, :] = crn[0, k, t : t + 1, :]
        ktf[f, :, IN, :] = 0.5 * (c + vf[f, :, HI, :])
        ktf[f, :, 7:8, :] = 0.5 * (vf[f, :, 7:8, :] + vf[f, :, 8:9, :])
        k12 = 0.5 * (c + second[...])
        after = 0.5 * (c + fine_next(c))
        k12f[f] = k12
        kzf[f] = after
        wf[f] = INV / (
            S1 + k01 + k12 + ktf[f, :, IN, :] + ktf[f, :, LO, :] + after + fine_before(after)
        )

    coarse_wait(b3_copies, 2, cb, False)
    rhs = cb[...]
    e = weight * rhs
    for k in range(3):
        inner = slice(k, 14 - k)
        e = e[1:-1] + weight[k + 1 : 13 - k] * (
            rhs[k + 1 : 13 - k] - coarse_operator(e, mob[inner], lap[k : 12 - k])
        )
    wait(sums)
    total = ar2[0]
    for o in range(1, ny):
        total = total + ar2[o]
    cells = 16.0 * 128.0 * nx * ny
    sum_f = jnp.sum(total[0:1, :], axis=1, keepdims=True)
    sum_m = jnp.sum(total[1:2, :], axis=1, keepdims=True)
    kappa = 0.8 * (sum_f / cells) / (S3 + 5.0 * (sum_m / cells))

    ce[3:11] = e + kappa
    double_rows()
    for x in range(8):
        v = double(x)
        for q in range(2):
            if 0 < 2 * x + q < 15:
                va[2 * x + q, :, IN, :] = x2[2 * x + q] + v

    def post_one(i):
        c, total = mid_sum(va, i)
        vb[i, :, IN, :] = w2[i, :, IN, :] * (b2[i, :, IN, :] + total) - INV * c

    planes(2, 14, 6, post_one)

    def post_two(i):
        c, total = mid_sum(vb, i)
        base[i - 3] = (
            va[i, :, IN, :] + (1.0 + ALPHA) * c + STEP * (w2[i, :, IN, :] * total)
        )

    planes(3, 13, 5, post_two)
    for t in range(2):
        lanes = slice(128 * t, 128 * t + 128)
        for x in range(8):
            pout[8 * x : 8 * x + 8, lanes] = base[1 + x, t, 4:12, :]
            for f in range(2):
                row = 3 + 9 * f
                pout[80 + 8 * f + x : 81 + 8 * f + x, lanes] = base[1 + x, t, row : row + 1, :]
        for f in range(2):
            pout[64 + 8 * f : 72 + 8 * f, lanes] = base[9 * f, t, 4:12, :]
        for k in range(4):
            row = 3 + 9 * (k % 2)
            pout[96 + k : 97 + k, lanes] = base[9 * (k // 2), t, row : row + 1, :]
    pout[...] = exact_dot(pout[:, 0:256], pmat[...])
    wait(x1_copies)

    for j in range(8):
        for t in range(4):
            v = pout[8 * j : 8 * j + 8, 128 * t : 128 * t + 128]
            for q in range(2):
                for h in range(2):
                    rows = pl.ds(8 + h, 8, stride=2)
                    px[2 * j + 1 + q, t, rows, :] = px[2 * j + 1 + q, t, rows, :] + v
    for f in range(4):
        first, second = (xr.at[1, f], xr.at[6, f]) if f < 2 else (yr.at[1, f - 2], yr.at[6, f - 2])
        for t in range(4):
            lanes = slice(128 * t, 128 * t + 128)
            v = pout[64 + 8 * f : 72 + 8 * f, lanes]
            for h in range(2):
                rows = pl.ds(h, 8, stride=2)
                vf[f, t, pl.ds(8 + h, 8, stride=2), :] = first[t, rows, :] + v
                v2f[f, t, rows, :] = second[t, rows, :] + v
            for row, k in zip((7, 24), corners(f)):
                vf[f, t, row : row + 1, :] = crn[1, k, t : t + 1, :] + pout[96 + k : 97 + k, lanes]
    pack_rows(px, 1)
    for f in range(2):
        d[15 * f] = d[15 * f] + kx[16 * f] * vf[f, :, IN, :]
        dl[f] = kyf[f] * vf[2 + f, :, IN, :]
    add_rows(d, 0, 0)

    for f in range(4):
        if f < 2:
            k01, inside, rhs_f = kx[16 * f], px[1 + 15 * f, :, IN, :], xr[4, f]
        else:
            k01, inside, rhs_f = kyf[f - 2], ys[1, f - 2], yr[4, f - 2]
        c = vf[f, :, IN, :]
        z = kzf[f]
        total = k01 * inside + k12f[f] * v2f[f]
        total = total + ktf[f, :, LO, :] * vf[f, :, LO, :] + ktf[f, :, IN, :] * vf[f, :, HI, :]
        total = total + z * fine_next(c) + fine_before(z * c)
        uf[f] = wf[f] * (rhs_f + total) - INV * c

    def fourth_sum(i):
        c, total = fine_sum(px, i)
        u[i + 1, :, IN, :] = w[i] * (d[i] + total) - INV * c

    planes(0, 16, 4, fourth_sum)

    def last_sum(i):
        c, total = fine_sum(u, i)
        g[i] = px[i + 1, :, IN, :] + (1.0 + ALPHA) * c + STEP * (w[i] * total)

    planes(0, 16, 4, last_sum)
    for f in range(2):
        g[15 * f] = g[15 * f] + gxf[f] * uf[f]
        dl[f] = gyf[f] * uf[2 + f]
    add_rows(g, 0, 0)
    for i in range(16):
        for t in range(4):
            out[i, :, 128 * t : 128 * t + 128] = g[i, t]


def solution(mesh):
    nx, ny = mesh.shape["gx"], mesh.shape["gy"]

    def local(p, d, m):
        vm = lambda *s: pltpu.VMEM(s, F32)
        sem = lambda *s: pltpu.SemaphoreType.DMA(s)
        plane = (16, 4, 16, 128)
        face = (4, 16, 128)
        scratch = [
            vm(18, 4, 32, 128), vm(18, 4, 32, 128), vm(18, 4, 32, 128), vm(18, 4, 32, 128),
            vm(*plane), vm(*plane), vm(*plane), vm(*plane),
            vm(17, 4, 16, 128), vm(16, 4, 32, 128), vm(*plane),
            vm(7, 2, *face), vm(7, 2, *face), vm(7, 2, *face),
            vm(2, *face), vm(2, *face), vm(2, *face), vm(2, *face), vm(64, 512),
            pltpu.VMEM((512, 256), BF16), pltpu.VMEM((256, 512), BF16), vm(104, 512),
            vm(3, 8, 2, 8, 128), vm(3, 2, 4, 2, 8, 128), vm(3, 2, 4, 2, 8, 128),
            vm(3, 2, 4, 2, 8, 128), vm(3, 2, 2, 2, 2, 8, 128),
            vm(16, 2, 32, 128), vm(16, 2, 32, 128), vm(16, 2, 32, 128), vm(16, 2, 16, 128),
            vm(17, 2, 16, 128), vm(16, 2, 32, 128), vm(16, 2, 16, 128),
            vm(16, 2, 32, 128), vm(16, 2, 32, 128), vm(16, 2, 16, 128), vm(16, 2, 16, 128),
            vm(3, 16, 128), vm(3, 8, 16, 128), vm(14, 16, 128), vm(14, 16, 128), vm(14, 16, 128),
            vm(14, 16, 128), vm(8, 16, 128),
            vm(10, 2, 16, 128), vm(3, 4, 4, 128), vm(3, 16, 4, 128),
            vm(nx, 2, 128), vm(ny, 2, 128),
            vm(2, 4, 4, 128), vm(2, 4, 4, 128), vm(4, 4, 32, 128), vm(4, *face), vm(4, 4, 32, 128),
            vm(4, *face), vm(4, *face), vm(4, *face), vm(4, *face),
            sem(3, 4), sem(9, 4), sem(9, 4), sem(3, 8), sem(3, 8), sem(3, 24), sem(3, 24),
            sem(nx), sem(nx), sem(ny), sem(ny),
        ]
        return pl.pallas_call(
            functools.partial(kernel, nx, ny),
            out_shape=jax.ShapeDtypeStruct((16, 16, 512), F32),
            in_specs=[pl.BlockSpec(memory_space=pl.ANY)] * 3,
            out_specs=pl.BlockSpec(memory_space=pltpu.VMEM),
            scratch_shapes=scratch,
            compiler_params=pltpu.CompilerParams(
                collective_id=0, has_side_effects=True, vmem_limit_bytes=30 * 1024 * 1024
            ),
        )(*[pltpu.with_memory_space_constraint(a, pltpu.HBM) for a in (p, d, m)])

    spec = P("gx", "gy", None)
    return jax.shard_map(
        local, mesh=mesh, in_specs=(spec, spec, spec), out_specs=spec, check_vma=False
    )
```

```python
import functools

import jax
import jax.numpy as jnp
from jax import lax
from jax.experimental import pallas as pl
from jax.experimental.pallas import tpu as pltpu
from jax.sharding import PartitionSpec as P

MESH = pl.DeviceIdType.MESH
F32 = jnp.float32
BF16 = jnp.bfloat16

S1 = 0.05
S2 = 0.2
S3 = 0.8
MIDPOINT = (2.0 + 0.3) / 2
HALFWIDTH = (2.0 - 0.3) / 2
SIGMA = MIDPOINT / HALFWIDTH
P1 = 1.0 / SIGMA
P2 = 1.0 / (2.0 * SIGMA - P1)
CA = P2 * P1
CB = 2.0 * P2 / HALFWIDTH
INV = 1.0 / MIDPOINT
ALPHA = CA + CB * (MIDPOINT - 1.0)
STEP = CB * MIDPOINT
BETA = 1.0 / CB - 1.0
GAMMA = CA / CB
NEAR = [(-1, 0), (1, 0), (0, -1), (0, 1), (-1, -1), (-1, 1), (1, -1), (1, 1)]


def thirds(x):
    high = x.astype(BF16)
    rest = x - high.astype(F32)
    middle = rest.astype(BF16)
    low = (rest - middle.astype(F32)).astype(BF16)
    return high, middle, low


def exact_dot(x, matrix):
    total = None
    for part in thirds(x):
        term = jnp.dot(part, matrix, preferred_element_type=F32)
        total = term if total is None else total + term
    return total


def weighted_sum(f):
    q = pltpu.roll(f, 1, 2) + pltpu.roll(f, f.shape[2] - 1, 2)
    face = 0.5 * f + 0.125 * q
    edge = 0.125 * f + 0.0625 * q
    rows = f.shape[1]
    a = 0.5 * q + (pltpu.roll(face, 1, 1) + pltpu.roll(face, rows - 1, 1))
    b = face + (pltpu.roll(edge, 1, 1) + pltpu.roll(edge, rows - 1, 1))
    return a[1:-1] + (b[:-2] + b[2:])


def coarse_operator(v, mob, mob_sum):
    c = v[1:-1]
    m = mob[1:-1]
    return S3 * c + 0.5 * (
        5.0 * m * c - m * weighted_sum(v) + c * mob_sum - weighted_sum(mob * v)
    )


def fine_next(v):
    turned = pltpu.roll(v, 127, 2)
    lane = lax.broadcasted_iota(jnp.int32, v.shape, 2)
    return jnp.where(lane == 127, jnp.concatenate([turned[1:], turned[:1]], axis=0), turned)


def fine_before(v):
    turned = pltpu.roll(v, 1, 2)
    lane = lax.broadcasted_iota(jnp.int32, v.shape, 2)
    return jnp.where(lane == 0, jnp.concatenate([turned[3:], turned[:3]], axis=0), turned)


def mid_next(v):
    return jnp.concatenate([v[1:], pltpu.roll(v[:1], 127, 2)], axis=0)


def mid_before(v):
    return jnp.concatenate([pltpu.roll(v[1:], 1, 2), v[:1]], axis=0)


def kernel(
    nx, ny,
    p_hbm, d_hbm, m_hbm, out,
    px, mf, u, u2, d, g, dg, w, kx, ky, kz,
    xr, ys, yr, kyf, gyf, gxf, dl, rs, tmat, pmat, pout,
    mid_b, mid_stage, mid_rx, mid_ry, mid_rc, b2, m2, w2, d2, kx2, ky2, kz2,
    va, vb, rr, x2, xk,
    cstage, crecv, cm, cw, cb, ce, t2,
    base, fstage, frecv, fk,
    ar1, ar2,
    cst, crn, vf, v2f, ktf, k12f, kzf, wf, uf, bcs, bcr,
    nst, nrx, nry, nrc, ring, ringr, pcor,
    in_sem, fs, fr, ms, mr, cs, cr, xs, xrs, as1, ar1s, as2, ar2s,
):
    gx = lax.axis_index("gx")
    gy = lax.axis_index("gy")
    IN = slice(8, 24)
    LO = slice(7, 23)
    HI = slice(9, 25)

    def device(ox, oy):
        return (lax.rem(gx + (ox % nx), nx), lax.rem(gy + (oy % ny), ny))

    peers = {(o, 0) for o in range(1, nx)} | {(0, o) for o in range(1, ny)}
    peers |= {(dx % nx, dy % ny) for dx, dy in NEAR}
    peers = sorted(peers - {(0, 0)})

    loads = []
    for n, (src, dst) in enumerate(
        ((m_hbm, mf.at[1:17, :, IN, :]), (p_hbm, px.at[1:17, :, IN, :]), (d_hbm, d))
    ):
        loads.append(
            [
                pltpu.make_async_copy(
                    src.at[:, :, 128 * t : 128 * t + 128], dst.at[:, t], in_sem.at[n, t]
                )
                for t in range(4)
            ]
        )
        for c in loads[-1]:
            c.start()
    barrier = pltpu.get_barrier_semaphore()
    for ox, oy in peers:
        pl.semaphore_signal(barrier, inc=1, device_id=device(ox, oy), device_id_type=MESH)

    def remote(src, dst, ssem, rsem, ox, oy):
        return pltpu.make_async_remote_copy(
            src_ref=src, dst_ref=dst, send_sem=ssem, recv_sem=rsem,
            device_id=device(ox, oy), device_id_type=MESH,
        )

    def planes(start, stop, width, body):
        def several(j, carry):
            for q in range(width):
                body(start + width * j + q)
            return carry

        lax.fori_loop(0, (stop - start) // width, several, 0)

    zeros = jnp.zeros((4, 8, 128), F32)
    rims = (mf, px, u, u2)
    for a in rims:
        for plane in (0, 17):
            a[plane, :, 8:16, :] = zeros
            a[plane, :, 16:24, :] = zeros

    def clear(i):
        for a in rims:
            a[i + 1, :, 0:8, :] = zeros
            a[i + 1, :, 24:32, :] = zeros
        ky[i, :, 0:8, :] = zeros

    planes(0, 16, 2, clear)

    zi = lax.broadcasted_iota(jnp.int32, tmat.shape, 0)
    ci = lax.broadcasted_iota(jnp.int32, tmat.shape, 1)
    hit = (zi >> 1) == (((ci & 127) << 1) + (ci >> 7))
    tmat[...] = jnp.where(hit, 1.0, 0.0).astype(BF16)
    zi = lax.broadcasted_iota(jnp.int32, pmat.shape, 1)
    ci = lax.broadcasted_iota(jnp.int32, pmat.shape, 0)
    hit = (zi >> 1) == (((ci & 127) << 1) + (ci >> 7))
    pmat[...] = jnp.where(hit, 1.0, 0.0).astype(BF16)

    def pack_rows(arr, n, layer=0, off=1, row=8):
        low, high = row + layer, row + 15 - layer
        for x in range(16):
            ys[n, 0, :, x : x + 1, :] = arr[x + off, :, low : low + 1, :]
            ys[n, 1, :, x : x + 1, :] = arr[x + off, :, high : high + 1, :]

    def fine_send(arr, n, layer=0, off=1, row=8):
        rows = slice(row, row + 16)
        low, high = arr.at[off + layer, :, rows, :], arr.at[off + 15 - layer, :, rows, :]
        copies = [
            remote(low, xr.at[n, 1], fs.at[n, 0], fr.at[n, 0], -1, 0),
            remote(high, xr.at[n, 0], fs.at[n, 1], fr.at[n, 1], 1, 0),
            remote(ys.at[n, 0], yr.at[n, 1], fs.at[n, 2], fr.at[n, 2], 0, -1),
            remote(ys.at[n, 1], yr.at[n, 0], fs.at[n, 3], fr.at[n, 3], 0, 1),
        ]
        for c in copies:
            c.start()
        return copies

    def wait(copies):
        for c in copies:
            c.wait()

    def wait_sent(copies):
        for c in copies:
            c.wait_send()

    def wait_arrived(copies):
        for c in copies:
            c.wait_recv()

    def corner_send(arr, n):
        copies = []
        for k, (dx, dy) in enumerate(NEAR[4:]):
            x, y = 1 + 15 * (k // 2), 8 + 15 * (k % 2)
            for t in range(4):
                cst[n, k, t : t + 1, :] = arr[x, t, y : y + 1, :]
            copies.append(
                remote(cst.at[n, k], crn.at[n, 3 - k], fs.at[7 + n, k], fr.at[7 + n, k], dx, dy)
            )
            copies[-1].start()
        return copies

    def restrict_fine(arr, off, row, scale):
        for j in range(8):
            for t in range(4):
                total = None
                for q in range(2):
                    for h in range(2):
                        part = arr[2 * j + q + off, t, pl.ds(row + h, 8, stride=2), :]
                        total = part if total is None else total + part
                rs[8 * j : 8 * j + 8, 128 * t : 128 * t + 128] = total * scale
        return exact_dot(rs[...], tmat[...])

    def mid_put(n, got):
        blocks = []
        for x in range(8):
            rows = got[8 * x : 8 * x + 8]
            v = jnp.stack([rows[:, :128], rows[:, 128:]], axis=0)
            mid_b[n, x] = v
            blocks.append(v)
        return blocks

    def mid_fold(n, blocks):
        low = lax.broadcasted_iota(jnp.int32, (2, 8, 128), 1) < 4
        for t in range(4):
            a, b = blocks[2 * t], blocks[2 * t + 1]
            mid_stage[n, 0, t] = jnp.where(low, a, pltpu.roll(b, 4, 1))
            mid_stage[n, 1, t] = jnp.where(low, pltpu.roll(a, 4, 1), b)

    def rhs_send():
        for q in range(2):
            for k in range(4):
                for j in range(2):
                    nst[j, q, :, 2 * k : 2 * k + 2, :] = mid_b[
                        1, 4 * q + k, :, 6 * j : 6 * j + 2, :
                    ]
        copies = [
            remote(mid_b.at[1, 0:2], nrx.at[1], ms.at[1, 0], mr.at[1, 0], -1, 0),
            remote(mid_b.at[1, 6:8], nrx.at[0], ms.at[1, 1], mr.at[1, 1], 1, 0),
            remote(nst.at[0], nry.at[1], ms.at[1, 2], mr.at[1, 2], 0, -1),
            remote(nst.at[1], nry.at[0], ms.at[1, 3], mr.at[1, 3], 0, 1),
        ]
        k = 4
        for i, dx in enumerate((-1, 1)):
            for j, dy in enumerate((-1, 1)):
                copies.append(
                    remote(
                        nst.at[j, i], nrc.at[1 - i, 1 - j], ms.at[1, k], mr.at[1, k], dx, dy
                    )
                )
                k += 1
        for c in copies:
            c.start()
        return copies

    def rhs_place():
        for i in range(2):
            for x in range(2):
                plane = 2 + 10 * i + x
                b2[plane, :, 12:20, :] = nrx[i, x]
                at = 4 - 4 * i + 2 * x
                for j in range(2):
                    row = 10 + 10 * j
                    b2[plane, :, row : row + 2, :] = nrc[i, j, :, at : at + 2, :]
        for j in range(2):
            row = 10 + 10 * j
            for q in range(2):
                for k in range(4):
                    b2[4 + 4 * q + k, :, row : row + 2, :] = nry[j, q, :, 2 * k : 2 * k + 2, :]

    def mid_send(n):
        copies = [
            remote(mid_b.at[n, 0:4], mid_rx.at[n, 1], ms.at[n, 0], mr.at[n, 0], -1, 0),
            remote(mid_b.at[n, 4:8], mid_rx.at[n, 0], ms.at[n, 1], mr.at[n, 1], 1, 0),
            remote(mid_stage.at[n, 0], mid_ry.at[n, 1], ms.at[n, 2], mr.at[n, 2], 0, -1),
            remote(mid_stage.at[n, 1], mid_ry.at[n, 0], ms.at[n, 3], mr.at[n, 3], 0, 1),
        ]
        k = 4
        for i, dx in enumerate((-1, 1)):
            for j, dy in enumerate((-1, 1)):
                copies.append(
                    remote(
                        mid_stage.at[n, j, 2 * i : 2 * i + 2], mid_rc.at[n, 1 - i, 1 - j],
                        ms.at[n, k], mr.at[n, k], dx, dy,
                    )
                )
                k += 1
        for c in copies:
            c.start()
        return copies

    def mid_place(n, ext):
        for i in range(2):
            for x in range(4):
                ext[12 * i + x, :, 12:20, :] = mid_rx[n, i, x]
            for t in range(4):
                for q in range(2):
                    ext[4 + 2 * t + q, :, 8 + 12 * i : 12 + 12 * i, :] = mid_ry[
                        n, i, t, :, 4 * q : 4 * q + 4, :
                    ]
            for j in range(2):
                for t in range(2):
                    for q in range(2):
                        ext[12 * i + 2 * t + q, :, 8 + 12 * j : 12 + 12 * j, :] = mid_rc[
                            n, i, j, t, :, 4 * q : 4 * q + 4, :
                        ]

    def mid_own(n, ext):
        for x in range(8):
            ext[4 + x, :, 12:20, :] = mid_b[n, x]

    def coarse_block(arr, n, row, scale):
        for x in range(4):
            total = None
            for q in range(2):
                for t in range(2):
                    for h in range(2):
                        part = arr[4 + 2 * x + q, t, pl.ds(row + h, 4, stride=2), :]
                        total = part if total is None else total + part
            cstage[n, 4 * x : 4 * x + 4, :] = total * scale

    def coarse_send(n):
        copies = []
        for k, (dx, dy) in enumerate(NEAR):
            copies.append(
                remote(cstage.at[n], crecv.at[n, k], cs.at[n, k], cr.at[n, k], dx, dy)
            )
            copies[-1].start()
        return copies

    def coarse_wait(copies, n, ext):
        def place(dx, dy, block):
            for x in range(4):
                ext[4 * dx + 4 + x, 4 * dy + 4 : 4 * dy + 8, :] = block[4 * x : 4 * x + 4, :]

        place(0, 0, cstage.at[n])
        wait(copies)
        for k, (dx, dy) in enumerate(NEAR):
            place(-dx, -dy, crecv.at[n, k])

    def fine_sum(arr, i):
        c = arr[i + 1, :, IN, :]
        z = kz[i]
        total = kx[i] * arr[i, :, IN, :] + kx[i + 1] * arr[i + 2, :, IN, :]
        total = total + ky[i, :, LO, :] * arr[i + 1, :, LO, :]
        total = total + ky[i, :, IN, :] * arr[i + 1, :, HI, :]
        return c, total + z * fine_next(c) + fine_before(z * c)

    def mid_sum(arr, i):
        c = arr[i, :, IN, :]
        z = kz2[i]
        total = kx2[i] * arr[i - 1, :, IN, :] + kx2[i + 1] * arr[i + 1, :, IN, :]
        total = total + ky2[i, :, LO, :] * arr[i, :, LO, :]
        total = total + ky2[i, :, IN, :] * arr[i, :, HI, :]
        return c, total + z * mid_next(c) + mid_before(z * c)

    def add_rows(arr, off, row):
        for x in range(16):
            for f in range(2):
                k = row + 15 * f
                arr[x + off, :, k : k + 1, :] = (
                    arr[x + off, :, k : k + 1, :] + dl[f, :, x : x + 1, :]
                )

    wait(loads[0])
    pack_rows(mf, 0)
    mid_fold(0, mid_put(0, restrict_fine(mf, 1, 8, 0.125)))
    wait(loads[1])
    pack_rows(px, 1)
    wait(loads[2])
    pl.semaphore_wait(barrier, len(peers))
    m_copies = fine_send(mf, 0)
    p_copies = fine_send(px, 1)

    def coefficients(i):
        c = mf[i + 1, :, IN, :]
        below = 0.5 * (c + mf[i, :, IN, :])
        above = c + mf[i + 2, :, IN, :]
        left = c + mf[i + 1, :, LO, :]
        right = 0.5 * (c + mf[i + 1, :, HI, :])
        after = 0.5 * (c + fine_next(c))
        before = c + fine_before(c)
        kx[i] = below
        ky[i, :, IN, :] = right
        kz[i] = after
        dg[i] = (S1 + below + right + after) + 0.5 * (above + left + before)

    planes(0, 16, 4, coefficients)
    kx[16] = 0.5 * mf[16, :, IN, :]

    def first_sum(i):
        c, total = fine_sum(px, i)
        g[i] = d[i] + total

    planes(0, 16, 4, first_sum)
    pack_rows(d, 4, 0, 0, 0)
    pack_rows(mf, 5, 1)
    wait_sent(m_copies)
    wait_sent(p_copies)
    m2_copies = mid_send(0)

    wait_arrived(m_copies)
    for f in range(2):
        face = 0.5 * xr[0, f]
        kx[16 * f] = kx[16 * f] + face
        dg[15 * f] = dg[15 * f] + face
        face = 0.5 * yr[0, f]
        kyf[f] = 0.5 * ys[0, f] + face
        dl[f] = face
    add_rows(dg, 0, 0)
    wait_arrived(p_copies)
    for f in range(2):
        g[15 * f] = g[15 * f] + kx[16 * f] * xr[1, f]
        dl[f] = kyf[f] * yr[1, f]
    add_rows(g, 0, 0)

    def first_step(i):
        weight = INV / dg[i]
        w[i] = weight
        u[i + 1, :, IN, :] = weight * g[i] - INV * px[i + 1, :, IN, :]

    planes(0, 16, 4, first_step)
    pack_rows(u, 2)
    u_copies = fine_send(u, 2)

    def second_sum(i):
        c, total = fine_sum(u, i)
        u2[i + 1, :, IN, :] = ALPHA * c + STEP * (w[i] * total)

    planes(0, 16, 4, second_sum)
    for x in range(16):
        for f in range(2):
            gyf[f, :, x : x + 1, :] = w[x, :, 15 * f : 15 * f + 1, :]
    for f in range(2):
        gyf[f] = STEP * (gyf[f] * kyf[f])
        gxf[f] = STEP * (w[15 * f] * kx[16 * f])
    mid_own(0, m2)
    wait(m2_copies)
    mid_place(0, m2)
    coarse_block(m2, 0, 12, 0.125)
    m3_copies = coarse_send(0)
    wait_sent(u_copies)

    wait_arrived(u_copies)
    for f in range(2):
        k = 1 + 15 * f
        u2[k, :, IN, :] = u2[k, :, IN, :] + gxf[f] * xr[2, f]
        dl[f] = gyf[f] * yr[2, f]
    add_rows(u2, 1, 8)
    pack_rows(u2, 3)
    u2_copies = fine_send(u2, 3)

    def third_sum(i):
        c, total = fine_sum(u2, i)
        before = u[i + 1, :, IN, :]
        g[i] = dg[i] * (BETA * c - GAMMA * before) + total
        px[i + 1, :, IN, :] = px[i + 1, :, IN, :] + before + c

    planes(0, 16, 4, third_sum)

    def mid_coefficients(i):
        c = m2[i, :, IN, :]
        below = 0.5 * (c + m2[i - 1, :, IN, :])
        above = 0.5 * (c + m2[i + 1, :, IN, :])
        left = c + m2[i, :, LO, :]
        right = 0.5 * (c + m2[i, :, HI, :])
        after = 0.5 * (c + mid_next(c))
        before = c + mid_before(c)
        kx2[i] = below
        kx2[i + 1] = above
        ky2[i, :, IN, :] = right
        kz2[i] = after
        diagonal = (S2 + below + above + right + after) + 0.5 * (left + before)
        d2[i] = diagonal
        w2[i] = INV / diagonal

    planes(1, 15, 7, mid_coefficients)
    coarse_wait(m3_copies, 0, cm)
    mob = cm[...]
    lap = weighted_sum(mob)
    cw[1:11] = 0.8 / (S3 + 0.5 * (5.0 * mob[1:-1] + lap))
    for x in range(4):
        cstage[1, 4 * x : 4 * x + 4, :] = cw[4 + x, 4:8, :]
    w3_copies = coarse_send(1)
    wait_sent(u2_copies)

    wait_arrived(u2_copies)
    for f in range(2):
        g[15 * f] = g[15 * f] + kx[16 * f] * xr[3, f]
        dl[f] = kyf[f] * yr[3, f]
    add_rows(g, 0, 0)
    mid_put(1, restrict_fine(g, 0, 0, 0.5))
    b2_copies = rhs_send()

    pack_rows(px, 6, 1)
    def response_one(i):
        vb[i, :, IN, :] = (-S2) * w2[i]

    planes(1, 15, 7, response_one)

    def response_two(i):
        c, total = mid_sum(vb, i)
        xk[i] = 1.0 + (1.0 + ALPHA) * c + STEP * (w2[i] * total)

    planes(2, 14, 6, response_two)
    for x in range(8):
        fk[2, :, x : x + 1, :] = xk[4 + x, :, 3:4, :]
        fk[3, :, x : x + 1, :] = xk[4 + x, :, 12:13, :]
    fk[0] = xk[3, :, 4:12, :]
    fk[1] = xk[12, :, 4:12, :]
    coarse_wait(w3_copies, 1, cw)
    weight = cw[...]
    y = jnp.ones_like(weight)
    psi = y
    for k in range(3):
        inner = slice(k, 12 - k)
        y = y[1:-1] - coarse_operator(weight[inner] * y, mob[inner], lap[k : 10 - k])
        psi = psi[1:-1] + y
    ce[0:4] = 1.0 - S3 * (weight[4:8] * psi[1:5])
    for f in range(2):
        xr[1, f] = xr[1, f] + xr[2, f] + xr[3, f]
        yr[1, f] = yr[1, f] + yr[2, f] + yr[3, f]
    mid_own(1, b2)
    wait_sent(b2_copies)
    d_copies = fine_send(d, 4, 0, 0, 0)
    far_copies = fine_send(mf, 5, 1) + corner_send(mf, 0)
    wait_arrived(b2_copies)
    rhs_place()

    def mid_one(i):
        va[i, :, IN, :] = w2[i] * b2[i, :, IN, :]

    planes(2, 14, 6, mid_one)

    def mid_two(i):
        c, total = mid_sum(va, i)
        step = ALPHA * c + STEP * (w2[i] * total)
        vb[i, :, IN, :] = step
        x2[i] = c + step

    planes(3, 13, 5, mid_two)

    def mid_three(i):
        c, total = mid_sum(vb, i)
        rr[i] = d2[i] * (BETA * c - GAMMA * va[i, :, IN, :]) + total

    planes(4, 12, 4, mid_three)
    coarse_block(rr, 2, 4, 0.5)
    b3_copies = coarse_send(2)
    for f in range(2):
        k = 5 + 5 * f
        ring[f] = x2[k, :, 4:12, :]
        for x in range(8):
            ring[2 + f, :, x : x + 1, :] = x2[4 + x, :, k : k + 1, :]
    ring_copies = [
        remote(ring.at[f], ringr.at[f + 1 - 2 * (f % 2)], xs.at[8 + f], xrs.at[8 + f], ox, oy)
        for f, (ox, oy) in enumerate(NEAR[:4])
    ]
    for c in ring_copies:
        c.start()

    part = jnp.zeros((1, 128), F32)
    partm = jnp.zeros((1, 128), F32)
    for x in range(4):
        part = part + jnp.sum(
            ce[x, 4:8, :] * cstage[2, 4 * x : 4 * x + 4, :], axis=0, keepdims=True
        )
        partm = partm + jnp.sum(cstage[0, 4 * x : 4 * x + 4, :], axis=0, keepdims=True)
    ar1[0, 0:1, :] = part
    ar1[0, 1:2, :] = partm
    sums = []
    for o in range(1, nx):
        sums.append(remote(ar1.at[0], ar1.at[o], as1.at[o], ar1s.at[o], o, 0))
        sums[-1].start()

    x1_copies = fine_send(px, 6, 1) + corner_send(px, 1)
    coarse_wait(b3_copies, 2, cb)
    rhs = cb[...]
    e = weight * rhs
    for k in range(3):
        inner = slice(k, 12 - k)
        e = e[1:-1] + weight[k + 1 : 11 - k] * (
            rhs[k + 1 : 11 - k] - coarse_operator(e, mob[inner], lap[k : 10 - k])
        )
    wait(sums)
    total = ar1[0]
    for o in range(1, nx):
        total = total + ar1[o]
    ar2[0] = total
    sums = []
    for o in range(1, ny):
        sums.append(remote(ar2.at[0], ar2.at[o], as2.at[o], ar2s.at[o], 0, o))
        sums[-1].start()

    wait(ring_copies)
    for f in range(2):
        x2[2 + 11 * f, :, 4:12, :] = ringr[f]
        row = 2 + 11 * f
        for x in range(8):
            x2[4 + x, :, row : row + 1, :] = ringr[2 + f, :, x : x + 1, :]
    ce[3:9] = e
    for x in range(6):
        for h in range(2):
            t2[x, pl.ds(h, 8, stride=2), :] = ce[3 + x, 2:10, :]
    for x in range(6):
        v = t2[x]
        both = jnp.stack([v, v], axis=0)
        for q in range(2):
            va[2 + 2 * x + q, :, IN, :] = x2[2 + 2 * x + q] + both

    def post_one(i):
        c, total = mid_sum(va, i)
        vb[i, :, IN, :] = w2[i] * (b2[i, :, IN, :] + total) - INV * c

    planes(3, 13, 5, post_one)

    def post_two(i):
        c, total = mid_sum(vb, i)
        done = va[i, :, IN, :] + (1.0 + ALPHA) * c + STEP * (w2[i] * total)
        base[i - 4] = done[:, 4:12, :]

    planes(4, 12, 4, post_two)
    for x in range(8):
        fstage[0, :, x : x + 1, :] = base[x, :, 0:1, :]
        fstage[1, :, x : x + 1, :] = base[x, :, 7:8, :]
    x_copies = [
        remote(base.at[0], frecv.at[1], xs.at[0], xrs.at[0], -1, 0),
        remote(base.at[7], frecv.at[0], xs.at[1], xrs.at[1], 1, 0),
        remote(fstage.at[0], frecv.at[3], xs.at[2], xrs.at[2], 0, -1),
        remote(fstage.at[1], frecv.at[2], xs.at[3], xrs.at[3], 0, 1),
    ]
    for k, (dx, dy) in enumerate(NEAR[4:]):
        x, y = 7 * (k // 2), 7 * (k % 2)
        for t in range(2):
            bcs[k, t : t + 1, :] = base[x, t, y : y + 1, :]
        x_copies.append(
            remote(bcs.at[k], bcr.at[3 - k], xs.at[4 + k], xrs.at[4 + k], dx, dy)
        )
    for c in x_copies:
        c.start()

    wait(d_copies)
    wait(far_copies)

    def corners(f):
        return ((0, 1), (2, 3), (0, 2), (1, 3))[f]

    for f in range(4):
        first, second = (xr.at[0, f], xr.at[5, f]) if f < 2 else (yr.at[0, f - 2], yr.at[5, f - 2])
        k01 = kx[16 * f] if f < 2 else kyf[f - 2]
        c = first[...]
        vf[f, :, IN, :] = c
        for row, k in zip((7, 24), corners(f)):
            for t in range(4):
                vf[f, t, row : row + 1, :] = crn[0, k, t : t + 1, :]
        ktf[f, :, IN, :] = 0.5 * (c + vf[f, :, HI, :])
        ktf[f, :, 7:8, :] = 0.5 * (vf[f, :, 7:8, :] + vf[f, :, 8:9, :])
        k12 = 0.5 * (c + second[...])
        after = 0.5 * (c + fine_next(c))
        k12f[f] = k12
        kzf[f] = after
        wf[f] = INV / (
            S1 + k01 + k12 + ktf[f, :, IN, :] + ktf[f, :, LO, :] + after + fine_before(after)
        )

    wait(sums)
    total = ar2[0]
    for o in range(1, ny):
        total = total + ar2[o]
    cells = 16.0 * 128.0 * nx * ny
    sum_f = jnp.sum(total[0:1, :], axis=1, keepdims=True)
    sum_m = jnp.sum(total[1:2, :], axis=1, keepdims=True)
    kappa = 0.8 * (sum_f / cells) / (S3 + 5.0 * (sum_m / cells))

    for x in range(8):
        v = base[x] + kappa * xk[4 + x, :, 4:12, :]
        pout[8 * x : 8 * x + 8, 0:128] = v[0]
        pout[8 * x : 8 * x + 8, 128:256] = v[1]
    wait(x_copies[:4])
    for f in range(4):
        v = frecv[f] + kappa * fk[f]
        pout[64 + 8 * f : 72 + 8 * f, 0:128] = v[0]
        pout[64 + 8 * f : 72 + 8 * f, 128:256] = v[1]
    pout[...] = exact_dot(pout[:, 0:256], pmat[...])

    wait_sent(x1_copies)
    for j in range(8):
        for t in range(4):
            v = pout[8 * j : 8 * j + 8, 128 * t : 128 * t + 128]
            for q in range(2):
                for h in range(2):
                    rows = pl.ds(8 + h, 8, stride=2)
                    px[2 * j + 1 + q, t, rows, :] = px[2 * j + 1 + q, t, rows, :] + v
    for f in range(4):
        first = xr.at[1, f] if f < 2 else yr.at[1, f - 2]
        for t in range(4):
            lanes = slice(128 * t, 128 * t + 128)
            v = pout[64 + 8 * f : 72 + 8 * f, lanes]
            for h in range(2):
                rows = pl.ds(h, 8, stride=2)
                vf[f, t, pl.ds(8 + h, 8, stride=2), :] = first[t, rows, :] + v
    pack_rows(px, 1)
    for f in range(2):
        d[15 * f] = d[15 * f] + kx[16 * f] * vf[f, :, IN, :]
        dl[f] = kyf[f] * vf[2 + f, :, IN, :]
    add_rows(d, 0, 0)

    def fourth_sum(i):
        c, total = fine_sum(px, i)
        u[i + 1, :, IN, :] = w[i] * (d[i] + total) - INV * c

    planes(0, 16, 4, fourth_sum)

    def last_sum(i):
        c, total = fine_sum(u, i)
        g[i] = px[i + 1, :, IN, :] + (1.0 + ALPHA) * c + STEP * (w[i] * total)

    planes(0, 16, 4, last_sum)

    wait_arrived(x1_copies)
    wait(x_copies[4:])
    for k in range(4):
        x, y = 3 + 9 * (k // 2), 3 + 9 * (k % 2)
        for t in range(2):
            pcor[k : k + 1, 128 * t : 128 * t + 128] = (
                bcr[k, t : t + 1, :] + kappa * xk[x, t, y : y + 1, :]
            )
    pcor[...] = exact_dot(pcor[:, 0:256], pmat[...])
    for f in range(4):
        second = xr.at[6, f] if f < 2 else yr.at[6, f - 2]
        for t in range(4):
            lanes = slice(128 * t, 128 * t + 128)
            v = pout[64 + 8 * f : 72 + 8 * f, lanes]
            for h in range(2):
                rows = pl.ds(h, 8, stride=2)
                v2f[f, t, rows, :] = second[t, rows, :] + v
            for row, k in zip((7, 24), corners(f)):
                vf[f, t, row : row + 1, :] = crn[1, k, t : t + 1, :] + pcor[k : k + 1, lanes]
    for f in range(4):
        if f < 2:
            k01, inside, rhs_f = kx[16 * f], px[1 + 15 * f, :, IN, :], xr[4, f]
        else:
            k01, inside, rhs_f = kyf[f - 2], ys[1, f - 2], yr[4, f - 2]
        c = vf[f, :, IN, :]
        z = kzf[f]
        total = k01 * inside + k12f[f] * v2f[f]
        total = total + ktf[f, :, LO, :] * vf[f, :, LO, :] + ktf[f, :, IN, :] * vf[f, :, HI, :]
        total = total + z * fine_next(c) + fine_before(z * c)
        uf[f] = wf[f] * (rhs_f + total) - INV * c

    for f in range(2):
        g[15 * f] = g[15 * f] + gxf[f] * uf[f]
        dl[f] = gyf[f] * uf[2 + f]
    add_rows(g, 0, 0)
    for i in range(16):
        for t in range(4):
            out[i, :, 128 * t : 128 * t + 128] = g[i, t]


def solution(mesh):
    nx, ny = mesh.shape["gx"], mesh.shape["gy"]

    def local(p, d, m):
        vm = lambda *s: pltpu.VMEM(s, F32)
        sem = lambda *s: pltpu.SemaphoreType.DMA(s)
        plane = (16, 4, 16, 128)
        face = (4, 16, 128)
        scratch = [
            vm(18, 4, 32, 128), vm(18, 4, 32, 128), vm(18, 4, 32, 128), vm(18, 4, 32, 128),
            vm(*plane), vm(*plane), vm(*plane), vm(*plane),
            vm(17, 4, 16, 128), vm(16, 4, 32, 128), vm(*plane),
            vm(7, 2, *face), vm(7, 2, *face), vm(7, 2, *face),
            vm(2, *face), vm(2, *face), vm(2, *face), vm(2, *face), vm(64, 512),
            pltpu.VMEM((512, 256), BF16), pltpu.VMEM((256, 512), BF16), vm(96, 512),
            vm(2, 8, 2, 8, 128), vm(2, 2, 4, 2, 8, 128), vm(2, 2, 4, 2, 8, 128),
            vm(2, 2, 4, 2, 8, 128), vm(2, 2, 2, 2, 2, 8, 128),
            vm(16, 2, 32, 128), vm(16, 2, 32, 128), vm(16, 2, 16, 128), vm(16, 2, 16, 128),
            vm(17, 2, 16, 128), vm(16, 2, 32, 128), vm(16, 2, 16, 128),
            vm(16, 2, 32, 128), vm(16, 2, 32, 128), vm(16, 2, 16, 128), vm(16, 2, 16, 128),
            vm(16, 2, 16, 128),
            vm(3, 16, 128), vm(3, 8, 16, 128), vm(12, 16, 128), vm(12, 16, 128), vm(12, 16, 128),
            vm(12, 16, 128), vm(6, 16, 128),
            vm(8, 2, 8, 128), vm(2, 2, 8, 128), vm(4, 2, 8, 128), vm(4, 2, 8, 128),
            vm(nx, 2, 128), vm(ny, 2, 128),
            vm(2, 4, 4, 128), vm(2, 4, 4, 128), vm(4, 4, 32, 128), vm(4, *face), vm(4, 4, 32, 128),
            vm(4, *face), vm(4, *face), vm(4, *face), vm(4, *face), vm(4, 2, 128), vm(4, 2, 128),
            vm(2, 2, 2, 8, 128), vm(2, 2, 2, 8, 128), vm(2, 2, 2, 8, 128), vm(2, 2, 2, 8, 128),
            vm(4, 2, 8, 128), vm(4, 2, 8, 128), vm(8, 512),
            sem(3, 4), sem(9, 4), sem(9, 4), sem(2, 8), sem(2, 8), sem(3, 8), sem(3, 8),
            sem(12), sem(12), sem(nx), sem(nx), sem(ny), sem(ny),
        ]
        return pl.pallas_call(
            functools.partial(kernel, nx, ny),
            out_shape=jax.ShapeDtypeStruct((16, 16, 512), F32),
            in_specs=[pl.BlockSpec(memory_space=pl.ANY)] * 3,
            out_specs=pl.BlockSpec(memory_space=pltpu.VMEM),
            scratch_shapes=scratch,
            compiler_params=pltpu.CompilerParams(
                collective_id=0, has_side_effects=True, vmem_limit_bytes=30 * 1024 * 1024
            ),
        )(*[pltpu.with_memory_space_constraint(a, pltpu.HBM) for a in (p, d, m)])

    spec = P("gx", "gy", None)
    return jax.shard_map(
        local, mesh=mesh, in_specs=(spec, spec, spec), out_specs=spec, check_vma=False
    )
```

```python
import functools

import jax
import jax.numpy as jnp
from jax import lax
from jax.experimental import pallas as pl
from jax.experimental.pallas import tpu as pltpu
from jax.sharding import PartitionSpec as P

MESH = pl.DeviceIdType.MESH
F32 = jnp.float32
BF16 = jnp.bfloat16

S1 = 0.05
S2 = 0.2
S3 = 0.8
MIDPOINT = (2.0 + 0.3) / 2
HALFWIDTH = (2.0 - 0.3) / 2
SIGMA = MIDPOINT / HALFWIDTH
P1 = 1.0 / SIGMA
P2 = 1.0 / (2.0 * SIGMA - P1)
CA = P2 * P1
CB = 2.0 * P2 / HALFWIDTH
INV = 1.0 / MIDPOINT
ALPHA = CA + CB * (MIDPOINT - 1.0)
STEP = CB * MIDPOINT
BETA = 1.0 / CB - 1.0
GAMMA = CA / CB
NEAR = [(-1, 0), (1, 0), (0, -1), (0, 1), (-1, -1), (-1, 1), (1, -1), (1, 1)]


def thirds(x):
    high = x.astype(BF16)
    rest = x - high.astype(F32)
    middle = rest.astype(BF16)
    low = (rest - middle.astype(F32)).astype(BF16)
    return high, middle, low


def exact_dot(x, matrix):
    total = None
    for part in thirds(x):
        term = jnp.dot(part, matrix, preferred_element_type=F32)
        total = term if total is None else total + term
    return total


def weighted_sum(f):
    q = pltpu.roll(f, 1, 2) + pltpu.roll(f, f.shape[2] - 1, 2)
    face = 0.5 * f + 0.125 * q
    edge = 0.125 * f + 0.0625 * q
    rows = f.shape[1]
    a = 0.5 * q + (pltpu.roll(face, 1, 1) + pltpu.roll(face, rows - 1, 1))
    b = face + (pltpu.roll(edge, 1, 1) + pltpu.roll(edge, rows - 1, 1))
    return a[1:-1] + (b[:-2] + b[2:])


def coarse_operator(v, mob, mob_sum):
    c = v[1:-1]
    m = mob[1:-1]
    return S3 * c + 0.5 * (
        5.0 * m * c - m * weighted_sum(v) + c * mob_sum - weighted_sum(mob * v)
    )


def fine_next(v):
    turned = pltpu.roll(v, 127, 2)
    lane = lax.broadcasted_iota(jnp.int32, v.shape, 2)
    return jnp.where(lane == 127, jnp.concatenate([turned[1:], turned[:1]], axis=0), turned)


def fine_before(v):
    turned = pltpu.roll(v, 1, 2)
    lane = lax.broadcasted_iota(jnp.int32, v.shape, 2)
    return jnp.where(lane == 0, jnp.concatenate([turned[3:], turned[:3]], axis=0), turned)


def mid_next(v):
    return jnp.concatenate([v[1:], pltpu.roll(v[:1], 127, 2)], axis=0)


def mid_before(v):
    return jnp.concatenate([pltpu.roll(v[1:], 1, 2), v[:1]], axis=0)


def kernel(
    nx, ny,
    p_hbm, d_hbm, m_hbm, out,
    px, mf, u, u2, d, g, dg, w, kx, ky, kz,
    xr, ys, yr, kyf, gyf, gxf, dl, rs, tmat, pmat, pout,
    mid_b, mid_stage, mid_rx, mid_ry, mid_rc, b2, m2, w2, d2, kx2, ky2, kz2,
    va, vb, rr, x2, xk,
    cstage, crecv, cm, cw, cb, ce, t2,
    base, fstage, frecv, fk,
    ar1, ar2,
    cst, crn, vf, v2f, ktf, k12f, kzf, wf, uf, bcs, bcr,
    nst, nrx, nry, nrc, ring, ringr, pcor,
    in_sem, fs, fr, ms, mr, cs, cr, xs, xrs, as1, ar1s, as2, ar2s,
):
    gx = lax.axis_index("gx")
    gy = lax.axis_index("gy")
    IN = slice(8, 24)
    LO = slice(7, 23)
    HI = slice(9, 25)

    def device(ox, oy):
        return (lax.rem(gx + (ox % nx), nx), lax.rem(gy + (oy % ny), ny))

    peers = {(o, 0) for o in range(1, nx)} | {(0, o) for o in range(1, ny)}
    peers |= {(dx % nx, dy % ny) for dx, dy in NEAR}
    peers = sorted(peers - {(0, 0)})

    loads = []
    for n, (src, dst) in enumerate(
        ((m_hbm, mf.at[1:17, :, IN, :]), (p_hbm, px.at[1:17, :, IN, :]), (d_hbm, d))
    ):
        loads.append(
            [
                pltpu.make_async_copy(
                    src.at[:, :, 128 * t : 128 * t + 128], dst.at[:, t], in_sem.at[n, t]
                )
                for t in range(4)
            ]
        )
        for c in loads[-1]:
            c.start()
    barrier = pltpu.get_barrier_semaphore()
    for ox, oy in peers:
        pl.semaphore_signal(barrier, inc=1, device_id=device(ox, oy), device_id_type=MESH)

    def remote(src, dst, ssem, rsem, ox, oy):
        return pltpu.make_async_remote_copy(
            src_ref=src, dst_ref=dst, send_sem=ssem, recv_sem=rsem,
            device_id=device(ox, oy), device_id_type=MESH,
        )

    def planes(start, stop, width, body):
        def several(j, carry):
            for q in range(width):
                body(start + width * j + q)
            return carry

        lax.fori_loop(0, (stop - start) // width, several, 0)

    zeros = jnp.zeros((4, 8, 128), F32)
    rims = (mf, px, u, u2)
    for a in rims:
        for plane in (0, 17):
            a[plane, :, 8:16, :] = zeros
            a[plane, :, 16:24, :] = zeros

    def clear(i):
        for a in rims:
            a[i + 1, :, 0:8, :] = zeros
            a[i + 1, :, 24:32, :] = zeros
        ky[i, :, 0:8, :] = zeros

    planes(0, 16, 2, clear)

    zi = lax.broadcasted_iota(jnp.int32, tmat.shape, 0)
    ci = lax.broadcasted_iota(jnp.int32, tmat.shape, 1)
    hit = (zi >> 1) == (((ci & 127) << 1) + (ci >> 7))
    tmat[...] = jnp.where(hit, 1.0, 0.0).astype(BF16)
    zi = lax.broadcasted_iota(jnp.int32, pmat.shape, 1)
    ci = lax.broadcasted_iota(jnp.int32, pmat.shape, 0)
    hit = (zi >> 1) == (((ci & 127) << 1) + (ci >> 7))
    pmat[...] = jnp.where(hit, 1.0, 0.0).astype(BF16)

    def pack_rows(arr, n, layer=0, off=1, row=8):
        low, high = row + layer, row + 15 - layer
        for x in range(16):
            ys[n, 0, :, x : x + 1, :] = arr[x + off, :, low : low + 1, :]
            ys[n, 1, :, x : x + 1, :] = arr[x + off, :, high : high + 1, :]

    def fine_send(arr, n, layer=0, off=1, row=8):
        rows = slice(row, row + 16)
        low, high = arr.at[off + layer, :, rows, :], arr.at[off + 15 - layer, :, rows, :]
        copies = [
            remote(low, xr.at[n, 1], fs.at[n, 0], fr.at[n, 0], -1, 0),
            remote(high, xr.at[n, 0], fs.at[n, 1], fr.at[n, 1], 1, 0),
            remote(ys.at[n, 0], yr.at[n, 1], fs.at[n, 2], fr.at[n, 2], 0, -1),
            remote(ys.at[n, 1], yr.at[n, 0], fs.at[n, 3], fr.at[n, 3], 0, 1),
        ]
        for c in copies:
            c.start()
        return copies

    def wait(copies):
        for c in copies:
            c.wait()

    def wait_sent(copies):
        for c in copies:
            c.wait_send()

    def wait_arrived(copies):
        for c in copies:
            c.wait_recv()

    def corner_send(arr, n):
        copies = []
        for k, (dx, dy) in enumerate(NEAR[4:]):
            x, y = 1 + 15 * (k // 2), 8 + 15 * (k % 2)
            for t in range(4):
                cst[n, k, t : t + 1, :] = arr[x, t, y : y + 1, :]
            copies.append(
                remote(cst.at[n, k], crn.at[n, 3 - k], fs.at[7 + n, k], fr.at[7 + n, k], dx, dy)
            )
            copies[-1].start()
        return copies

    def restrict_fine(arr, off, row, scale):
        for j in range(8):
            for t in range(4):
                total = None
                for q in range(2):
                    for h in range(2):
                        part = arr[2 * j + q + off, t, pl.ds(row + h, 8, stride=2), :]
                        total = part if total is None else total + part
                rs[8 * j : 8 * j + 8, 128 * t : 128 * t + 128] = total * scale
        return exact_dot(rs[...], tmat[...])

    def mid_put(n, got):
        blocks = []
        for x in range(8):
            rows = got[8 * x : 8 * x + 8]
            v = jnp.stack([rows[:, :128], rows[:, 128:]], axis=0)
            mid_b[n, x] = v
            blocks.append(v)
        return blocks

    def mid_fold(n, blocks):
        low = lax.broadcasted_iota(jnp.int32, (2, 8, 128), 1) < 4
        for t in range(4):
            a, b = blocks[2 * t], blocks[2 * t + 1]
            mid_stage[n, 0, t] = jnp.where(low, a, pltpu.roll(b, 4, 1))
            mid_stage[n, 1, t] = jnp.where(low, pltpu.roll(a, 4, 1), b)

    def rhs_send():
        for q in range(2):
            for k in range(4):
                for j in range(2):
                    nst[j, q, :, 2 * k : 2 * k + 2, :] = mid_b[
                        1, 4 * q + k, :, 6 * j : 6 * j + 2, :
                    ]
        copies = [
            remote(mid_b.at[1, 0:2], nrx.at[1], ms.at[1, 0], mr.at[1, 0], -1, 0),
            remote(mid_b.at[1, 6:8], nrx.at[0], ms.at[1, 1], mr.at[1, 1], 1, 0),
            remote(nst.at[0], nry.at[1], ms.at[1, 2], mr.at[1, 2], 0, -1),
            remote(nst.at[1], nry.at[0], ms.at[1, 3], mr.at[1, 3], 0, 1),
        ]
        k = 4
        for i, dx in enumerate((-1, 1)):
            for j, dy in enumerate((-1, 1)):
                copies.append(
                    remote(
                        nst.at[j, i], nrc.at[1 - i, 1 - j], ms.at[1, k], mr.at[1, k], dx, dy
                    )
                )
                k += 1
        for c in copies:
            c.start()
        return copies

    def rhs_place():
        for i in range(2):
            for x in range(2):
                plane = 2 + 10 * i + x
                b2[plane, :, 12:20, :] = nrx[i, x]
                at = 4 - 4 * i + 2 * x
                for j in range(2):
                    row = 10 + 10 * j
                    b2[plane, :, row : row + 2, :] = nrc[i, j, :, at : at + 2, :]
        for j in range(2):
            row = 10 + 10 * j
            for q in range(2):
                for k in range(4):
                    b2[4 + 4 * q + k, :, row : row + 2, :] = nry[j, q, :, 2 * k : 2 * k + 2, :]

    def mid_send(n):
        copies = [
            remote(mid_b.at[n, 0:4], mid_rx.at[n, 1], ms.at[n, 0], mr.at[n, 0], -1, 0),
            remote(mid_b.at[n, 4:8], mid_rx.at[n, 0], ms.at[n, 1], mr.at[n, 1], 1, 0),
            remote(mid_stage.at[n, 0], mid_ry.at[n, 1], ms.at[n, 2], mr.at[n, 2], 0, -1),
            remote(mid_stage.at[n, 1], mid_ry.at[n, 0], ms.at[n, 3], mr.at[n, 3], 0, 1),
        ]
        k = 4
        for i, dx in enumerate((-1, 1)):
            for j, dy in enumerate((-1, 1)):
                copies.append(
                    remote(
                        mid_stage.at[n, j, 2 * i : 2 * i + 2], mid_rc.at[n, 1 - i, 1 - j],
                        ms.at[n, k], mr.at[n, k], dx, dy,
                    )
                )
                k += 1
        for c in copies:
            c.start()
        return copies

    def mid_place(n, ext):
        for i in range(2):
            for x in range(4):
                ext[12 * i + x, :, 12:20, :] = mid_rx[n, i, x]
            for t in range(4):
                for q in range(2):
                    ext[4 + 2 * t + q, :, 8 + 12 * i : 12 + 12 * i, :] = mid_ry[
                        n, i, t, :, 4 * q : 4 * q + 4, :
                    ]
            for j in range(2):
                for t in range(2):
                    for q in range(2):
                        ext[12 * i + 2 * t + q, :, 8 + 12 * j : 12 + 12 * j, :] = mid_rc[
                            n, i, j, t, :, 4 * q : 4 * q + 4, :
                        ]

    def mid_own(n, ext):
        for x in range(8):
            ext[4 + x, :, 12:20, :] = mid_b[n, x]

    def coarse_block(arr, n, row, scale):
        for x in range(4):
            total = None
            for q in range(2):
                for t in range(2):
                    for h in range(2):
                        part = arr[4 + 2 * x + q, t, pl.ds(row + h, 4, stride=2), :]
                        total = part if total is None else total + part
            cstage[n, 4 * x : 4 * x + 4, :] = total * scale

    def coarse_send(n):
        copies = []
        for k, (dx, dy) in enumerate(NEAR):
            copies.append(
                remote(cstage.at[n], crecv.at[n, k], cs.at[n, k], cr.at[n, k], dx, dy)
            )
            copies[-1].start()
        return copies

    def coarse_wait(copies, n, ext):
        def place(dx, dy, block):
            for x in range(4):
                ext[4 * dx + 4 + x, 4 * dy + 4 : 4 * dy + 8, :] = block[4 * x : 4 * x + 4, :]

        place(0, 0, cstage.at[n])
        wait(copies)
        for k, (dx, dy) in enumerate(NEAR):
            place(-dx, -dy, crecv.at[n, k])

    def fine_sum(arr, i):
        c = arr[i + 1, :, IN, :]
        z = kz[i]
        total = kx[i] * arr[i, :, IN, :] + kx[i + 1] * arr[i + 2, :, IN, :]
        total = total + ky[i, :, LO, :] * arr[i + 1, :, LO, :]
        total = total + ky[i, :, IN, :] * arr[i + 1, :, HI, :]
        return c, total + z * fine_next(c) + fine_before(z * c)

    def mid_sum(arr, i):
        c = arr[i, :, IN, :]
        z = kz2[i]
        total = kx2[i] * arr[i - 1, :, IN, :] + kx2[i + 1] * arr[i + 1, :, IN, :]
        total = total + ky2[i, :, LO, :] * arr[i, :, LO, :]
        total = total + ky2[i, :, IN, :] * arr[i, :, HI, :]
        return c, total + z * mid_next(c) + mid_before(z * c)

    def add_rows(arr, off, row):
        for x in range(16):
            for f in range(2):
                k = row + 15 * f
                arr[x + off, :, k : k + 1, :] = (
                    arr[x + off, :, k : k + 1, :] + dl[f, :, x : x + 1, :]
                )

    wait(loads[0])
    pack_rows(mf, 0)
    mid_fold(0, mid_put(0, restrict_fine(mf, 1, 8, 0.125)))
    wait(loads[1])
    pack_rows(px, 1)
    wait(loads[2])
    pl.semaphore_wait(barrier, len(peers))
    m_copies = fine_send(mf, 0)
    p_copies = fine_send(px, 1)

    def coefficients(i):
        c = mf[i + 1, :, IN, :]
        below = 0.5 * (c + mf[i, :, IN, :])
        above = c + mf[i + 2, :, IN, :]
        left = c + mf[i + 1, :, LO, :]
        right = 0.5 * (c + mf[i + 1, :, HI, :])
        after = 0.5 * (c + fine_next(c))
        before = c + fine_before(c)
        kx[i] = below
        ky[i, :, IN, :] = right
        kz[i] = after
        dg[i] = (S1 + below + right + after) + 0.5 * (above + left + before)

    planes(0, 16, 4, coefficients)
    kx[16] = 0.5 * mf[16, :, IN, :]

    def first_sum(i):
        c, total = fine_sum(px, i)
        g[i] = d[i] + total

    planes(0, 16, 4, first_sum)
    pack_rows(d, 4, 0, 0, 0)
    pack_rows(mf, 5, 1)
    wait_sent(m_copies)
    wait_sent(p_copies)
    m2_copies = mid_send(0)

    wait_arrived(m_copies)
    for f in range(2):
        face = 0.5 * xr[0, f]
        kx[16 * f] = kx[16 * f] + face
        dg[15 * f] = dg[15 * f] + face
        face = 0.5 * yr[0, f]
        kyf[f] = 0.5 * ys[0, f] + face
        dl[f] = face
    add_rows(dg, 0, 0)
    wait_arrived(p_copies)
    for f in range(2):
        g[15 * f] = g[15 * f] + kx[16 * f] * xr[1, f]
        dl[f] = kyf[f] * yr[1, f]
    add_rows(g, 0, 0)

    def first_step(i):
        weight = INV / dg[i]
        w[i] = weight
        u[i + 1, :, IN, :] = weight * g[i] - INV * px[i + 1, :, IN, :]

    planes(0, 16, 8, first_step)
    pack_rows(u, 2)
    u_copies = fine_send(u, 2)

    def second_sum(i):
        c, total = fine_sum(u, i)
        u2[i + 1, :, IN, :] = ALPHA * c + STEP * (w[i] * total)

    planes(0, 16, 4, second_sum)
    wait_sent(u_copies)
    for x in range(16):
        for f in range(2):
            gyf[f, :, x : x + 1, :] = w[x, :, 15 * f : 15 * f + 1, :]
    for f in range(2):
        gyf[f] = STEP * (gyf[f] * kyf[f])
        gxf[f] = STEP * (w[15 * f] * kx[16 * f])
    mid_own(0, m2)
    wait(m2_copies)
    mid_place(0, m2)
    coarse_block(m2, 0, 12, 0.125)
    m3_copies = coarse_send(0)

    wait_arrived(u_copies)
    for f in range(2):
        k = 1 + 15 * f
        u2[k, :, IN, :] = u2[k, :, IN, :] + gxf[f] * xr[2, f]
        dl[f] = gyf[f] * yr[2, f]
    add_rows(u2, 1, 8)
    pack_rows(u2, 3)
    u2_copies = fine_send(u2, 3)

    def third_sum(i):
        c, total = fine_sum(u2, i)
        before = u[i + 1, :, IN, :]
        g[i] = dg[i] * (BETA * c - GAMMA * before) + total
        px[i + 1, :, IN, :] = px[i + 1, :, IN, :] + before + c

    planes(0, 16, 4, third_sum)
    wait_sent(u2_copies)

    def mid_coefficients(i):
        c = m2[i, :, IN, :]
        below = 0.5 * (c + m2[i - 1, :, IN, :])
        above = 0.5 * (c + m2[i + 1, :, IN, :])
        left = c + m2[i, :, LO, :]
        right = 0.5 * (c + m2[i, :, HI, :])
        after = 0.5 * (c + mid_next(c))
        before = c + mid_before(c)
        kx2[i] = below
        kx2[i + 1] = above
        ky2[i, :, IN, :] = right
        kz2[i] = after
        diagonal = (S2 + below + above + right + after) + 0.5 * (left + before)
        d2[i] = diagonal
        w2[i] = INV / diagonal

    planes(1, 15, 7, mid_coefficients)
    coarse_wait(m3_copies, 0, cm)
    mob = cm[...]
    lap = weighted_sum(mob)
    cw[1:11] = 0.8 / (S3 + 0.5 * (5.0 * mob[1:-1] + lap))
    for x in range(4):
        cstage[1, 4 * x : 4 * x + 4, :] = cw[4 + x, 4:8, :]
    w3_copies = coarse_send(1)

    wait_arrived(u2_copies)
    for f in range(2):
        g[15 * f] = g[15 * f] + kx[16 * f] * xr[3, f]
        dl[f] = kyf[f] * yr[3, f]
    add_rows(g, 0, 0)
    mid_put(1, restrict_fine(g, 0, 0, 0.5))
    b2_copies = rhs_send()

    pack_rows(px, 6, 1)
    def response_one(i):
        vb[i, :, IN, :] = (-S2) * w2[i]

    planes(1, 15, 7, response_one)

    def response_two(i):
        c, total = mid_sum(vb, i)
        xk[i] = 1.0 + (1.0 + ALPHA) * c + STEP * (w2[i] * total)

    planes(2, 14, 6, response_two)
    for x in range(8):
        fk[2, :, x : x + 1, :] = xk[4 + x, :, 3:4, :]
        fk[3, :, x : x + 1, :] = xk[4 + x, :, 12:13, :]
    fk[0] = xk[3, :, 4:12, :]
    fk[1] = xk[12, :, 4:12, :]
    coarse_wait(w3_copies, 1, cw)
    weight = cw[...]
    y = jnp.ones_like(weight)
    psi = y
    for k in range(3):
        inner = slice(k, 12 - k)
        y = y[1:-1] - coarse_operator(weight[inner] * y, mob[inner], lap[k : 10 - k])
        psi = psi[1:-1] + y
    ce[0:4] = 1.0 - S3 * (weight[4:8] * psi[1:5])
    for f in range(2):
        xr[1, f] = xr[1, f] + xr[2, f] + xr[3, f]
        yr[1, f] = yr[1, f] + yr[2, f] + yr[3, f]
    mid_own(1, b2)
    wait_sent(b2_copies)
    x1_copies = fine_send(px, 6, 1) + corner_send(px, 1)
    wait_arrived(b2_copies)
    rhs_place()

    def mid_one(i):
        va[i, :, IN, :] = w2[i] * b2[i, :, IN, :]

    planes(2, 14, 6, mid_one)

    def mid_two(i):
        c, total = mid_sum(va, i)
        step = ALPHA * c + STEP * (w2[i] * total)
        vb[i, :, IN, :] = step
        x2[i] = c + step

    planes(3, 13, 5, mid_two)

    def mid_three(i):
        c, total = mid_sum(vb, i)
        rr[i] = d2[i] * (BETA * c - GAMMA * va[i, :, IN, :]) + total

    planes(4, 12, 4, mid_three)
    coarse_block(rr, 2, 4, 0.5)
    b3_copies = coarse_send(2)
    for f in range(2):
        k = 5 + 5 * f
        ring[f] = x2[k, :, 4:12, :]
        for x in range(8):
            ring[2 + f, :, x : x + 1, :] = x2[4 + x, :, k : k + 1, :]
    ring_copies = [
        remote(ring.at[f], ringr.at[f + 1 - 2 * (f % 2)], xs.at[8 + f], xrs.at[8 + f], ox, oy)
        for f, (ox, oy) in enumerate(NEAR[:4])
    ]
    for c in ring_copies:
        c.start()

    part = jnp.zeros((1, 128), F32)
    partm = jnp.zeros((1, 128), F32)
    for x in range(4):
        part = part + jnp.sum(
            ce[x, 4:8, :] * cstage[2, 4 * x : 4 * x + 4, :], axis=0, keepdims=True
        )
        partm = partm + jnp.sum(cstage[0, 4 * x : 4 * x + 4, :], axis=0, keepdims=True)
    ar1[0, 0:1, :] = part
    ar1[0, 1:2, :] = partm
    sums = []
    for o in range(1, nx):
        sums.append(remote(ar1.at[0], ar1.at[o], as1.at[o], ar1s.at[o], o, 0))
        sums[-1].start()

    d_copies = fine_send(d, 4, 0, 0, 0)
    far_copies = fine_send(mf, 5, 1) + corner_send(mf, 0)
    coarse_wait(b3_copies, 2, cb)
    rhs = cb[...]
    e = weight * rhs
    for k in range(3):
        inner = slice(k, 12 - k)
        e = e[1:-1] + weight[k + 1 : 11 - k] * (
            rhs[k + 1 : 11 - k] - coarse_operator(e, mob[inner], lap[k : 10 - k])
        )
    wait(sums)
    total = ar1[0]
    for o in range(1, nx):
        total = total + ar1[o]
    ar2[0] = total
    sums = []
    for o in range(1, ny):
        sums.append(remote(ar2.at[0], ar2.at[o], as2.at[o], ar2s.at[o], 0, o))
        sums[-1].start()

    wait(ring_copies)
    for f in range(2):
        x2[2 + 11 * f, :, 4:12, :] = ringr[f]
        row = 2 + 11 * f
        for x in range(8):
            x2[4 + x, :, row : row + 1, :] = ringr[2 + f, :, x : x + 1, :]
    ce[3:9] = e
    for x in range(6):
        for h in range(2):
            t2[x, pl.ds(h, 8, stride=2), :] = ce[3 + x, 2:10, :]
    for x in range(6):
        v = t2[x]
        both = jnp.stack([v, v], axis=0)
        for q in range(2):
            va[2 + 2 * x + q, :, IN, :] = x2[2 + 2 * x + q] + both

    def post_one(i):
        c, total = mid_sum(va, i)
        vb[i, :, IN, :] = w2[i] * (b2[i, :, IN, :] + total) - INV * c

    planes(3, 13, 5, post_one)

    def post_two(i):
        c, total = mid_sum(vb, i)
        done = va[i, :, IN, :] + (1.0 + ALPHA) * c + STEP * (w2[i] * total)
        base[i - 4] = done[:, 4:12, :]

    planes(4, 12, 4, post_two)
    for x in range(8):
        fstage[0, :, x : x + 1, :] = base[x, :, 0:1, :]
        fstage[1, :, x : x + 1, :] = base[x, :, 7:8, :]
    x_copies = [
        remote(base.at[0], frecv.at[1], xs.at[0], xrs.at[0], -1, 0),
        remote(base.at[7], frecv.at[0], xs.at[1], xrs.at[1], 1, 0),
        remote(fstage.at[0], frecv.at[3], xs.at[2], xrs.at[2], 0, -1),
        remote(fstage.at[1], frecv.at[2], xs.at[3], xrs.at[3], 0, 1),
    ]
    for k, (dx, dy) in enumerate(NEAR[4:]):
        x, y = 7 * (k // 2), 7 * (k % 2)
        for t in range(2):
            bcs[k, t : t + 1, :] = base[x, t, y : y + 1, :]
        x_copies.append(
            remote(bcs.at[k], bcr.at[3 - k], xs.at[4 + k], xrs.at[4 + k], dx, dy)
        )
    for c in x_copies:
        c.start()

    wait(d_copies)
    wait(far_copies)

    def corners(f):
        return ((0, 1), (2, 3), (0, 2), (1, 3))[f]

    for f in range(4):
        first, second = (xr.at[0, f], xr.at[5, f]) if f < 2 else (yr.at[0, f - 2], yr.at[5, f - 2])
        k01 = kx[16 * f] if f < 2 else kyf[f - 2]
        c = first[...]
        vf[f, :, IN, :] = c
        for row, k in zip((7, 24), corners(f)):
            for t in range(4):
                vf[f, t, row : row + 1, :] = crn[0, k, t : t + 1, :]
        ktf[f, :, IN, :] = 0.5 * (c + vf[f, :, HI, :])
        ktf[f, :, 7:8, :] = 0.5 * (vf[f, :, 7:8, :] + vf[f, :, 8:9, :])
        k12 = 0.5 * (c + second[...])
        after = 0.5 * (c + fine_next(c))
        k12f[f] = k12
        kzf[f] = after
        wf[f] = INV / (
            S1 + k01 + k12 + ktf[f, :, IN, :] + ktf[f, :, LO, :] + after + fine_before(after)
        )

    wait(sums)
    total = ar2[0]
    for o in range(1, ny):
        total = total + ar2[o]
    cells = 16.0 * 128.0 * nx * ny
    sum_f = jnp.sum(total[0:1, :], axis=1, keepdims=True)
    sum_m = jnp.sum(total[1:2, :], axis=1, keepdims=True)
    kappa = 0.8 * (sum_f / cells) / (S3 + 5.0 * (sum_m / cells))

    for x in range(8):
        v = base[x] + kappa * xk[4 + x, :, 4:12, :]
        pout[8 * x : 8 * x + 8, 0:128] = v[0]
        pout[8 * x : 8 * x + 8, 128:256] = v[1]
    wait(x_copies[:4])
    for f in range(4):
        v = frecv[f] + kappa * fk[f]
        pout[64 + 8 * f : 72 + 8 * f, 0:128] = v[0]
        pout[64 + 8 * f : 72 + 8 * f, 128:256] = v[1]
    pout[...] = exact_dot(pout[:, 0:256], pmat[...])

    wait_sent(x1_copies)
    for j in range(8):
        for t in range(4):
            v = pout[8 * j : 8 * j + 8, 128 * t : 128 * t + 128]
            for q in range(2):
                for h in range(2):
                    rows = pl.ds(8 + h, 8, stride=2)
                    px[2 * j + 1 + q, t, rows, :] = px[2 * j + 1 + q, t, rows, :] + v
    for f in range(4):
        first = xr.at[1, f] if f < 2 else yr.at[1, f - 2]
        for t in range(4):
            lanes = slice(128 * t, 128 * t + 128)
            v = pout[64 + 8 * f : 72 + 8 * f, lanes]
            for h in range(2):
                rows = pl.ds(h, 8, stride=2)
                vf[f, t, pl.ds(8 + h, 8, stride=2), :] = first[t, rows, :] + v
    pack_rows(px, 1)
    for f in range(2):
        d[15 * f] = d[15 * f] + kx[16 * f] * vf[f, :, IN, :]
        dl[f] = kyf[f] * vf[2 + f, :, IN, :]
    add_rows(d, 0, 0)

    def fourth_sum(i):
        c, total = fine_sum(px, i)
        u[i + 1, :, IN, :] = w[i] * (d[i] + total) - INV * c

    planes(0, 16, 8, fourth_sum)

    def last_sum(i):
        c, total = fine_sum(u, i)
        g[i] = px[i + 1, :, IN, :] + (1.0 + ALPHA) * c + STEP * (w[i] * total)

    planes(0, 16, 8, last_sum)

    wait_arrived(x1_copies)
    wait(x_copies[4:])
    for k in range(4):
        x, y = 3 + 9 * (k // 2), 3 + 9 * (k % 2)
        for t in range(2):
            pcor[k : k + 1, 128 * t : 128 * t + 128] = (
                bcr[k, t : t + 1, :] + kappa * xk[x, t, y : y + 1, :]
            )
    pcor[...] = exact_dot(pcor[:, 0:256], pmat[...])
    for f in range(4):
        second = xr.at[6, f] if f < 2 else yr.at[6, f - 2]
        for t in range(4):
            lanes = slice(128 * t, 128 * t + 128)
            v = pout[64 + 8 * f : 72 + 8 * f, lanes]
            for h in range(2):
                rows = pl.ds(h, 8, stride=2)
                v2f[f, t, rows, :] = second[t, rows, :] + v
            for row, k in zip((7, 24), corners(f)):
                vf[f, t, row : row + 1, :] = crn[1, k, t : t + 1, :] + pcor[k : k + 1, lanes]
    for f in range(4):
        if f < 2:
            k01, inside, rhs_f = kx[16 * f], px[1 + 15 * f, :, IN, :], xr[4, f]
        else:
            k01, inside, rhs_f = kyf[f - 2], ys[1, f - 2], yr[4, f - 2]
        c = vf[f, :, IN, :]
        z = kzf[f]
        total = k01 * inside + k12f[f] * v2f[f]
        total = total + ktf[f, :, LO, :] * vf[f, :, LO, :] + ktf[f, :, IN, :] * vf[f, :, HI, :]
        total = total + z * fine_next(c) + fine_before(z * c)
        uf[f] = wf[f] * (rhs_f + total) - INV * c

    for f in range(2):
        g[15 * f] = g[15 * f] + gxf[f] * uf[f]
        dl[f] = gyf[f] * uf[2 + f]
    add_rows(g, 0, 0)
    for i in range(16):
        for t in range(4):
            out[i, :, 128 * t : 128 * t + 128] = g[i, t]


def solution(mesh):
    nx, ny = mesh.shape["gx"], mesh.shape["gy"]

    def local(p, d, m):
        vm = lambda *s: pltpu.VMEM(s, F32)
        sem = lambda *s: pltpu.SemaphoreType.DMA(s)
        plane = (16, 4, 16, 128)
        face = (4, 16, 128)
        scratch = [
            vm(18, 4, 32, 128), vm(18, 4, 32, 128), vm(18, 4, 32, 128), vm(18, 4, 32, 128),
            vm(*plane), vm(*plane), vm(*plane), vm(*plane),
            vm(17, 4, 16, 128), vm(16, 4, 32, 128), vm(*plane),
            vm(7, 2, *face), vm(7, 2, *face), vm(7, 2, *face),
            vm(2, *face), vm(2, *face), vm(2, *face), vm(2, *face), vm(64, 512),
            pltpu.VMEM((512, 256), BF16), pltpu.VMEM((256, 512), BF16), vm(96, 512),
            vm(2, 8, 2, 8, 128), vm(2, 2, 4, 2, 8, 128), vm(2, 2, 4, 2, 8, 128),
            vm(2, 2, 4, 2, 8, 128), vm(2, 2, 2, 2, 2, 8, 128),
            vm(16, 2, 32, 128), vm(16, 2, 32, 128), vm(16, 2, 16, 128), vm(16, 2, 16, 128),
            vm(17, 2, 16, 128), vm(16, 2, 32, 128), vm(16, 2, 16, 128),
            vm(16, 2, 32, 128), vm(16, 2, 32, 128), vm(16, 2, 16, 128), vm(16, 2, 16, 128),
            vm(16, 2, 16, 128),
            vm(3, 16, 128), vm(3, 8, 16, 128), vm(12, 16, 128), vm(12, 16, 128), vm(12, 16, 128),
            vm(12, 16, 128), vm(6, 16, 128),
            vm(8, 2, 8, 128), vm(2, 2, 8, 128), vm(4, 2, 8, 128), vm(4, 2, 8, 128),
            vm(nx, 2, 128), vm(ny, 2, 128),
            vm(2, 4, 4, 128), vm(2, 4, 4, 128), vm(4, 4, 32, 128), vm(4, *face), vm(4, 4, 32, 128),
            vm(4, *face), vm(4, *face), vm(4, *face), vm(4, *face), vm(4, 2, 128), vm(4, 2, 128),
            vm(2, 2, 2, 8, 128), vm(2, 2, 2, 8, 128), vm(2, 2, 2, 8, 128), vm(2, 2, 2, 8, 128),
            vm(4, 2, 8, 128), vm(4, 2, 8, 128), vm(8, 512),
            sem(3, 4), sem(9, 4), sem(9, 4), sem(2, 8), sem(2, 8), sem(3, 8), sem(3, 8),
            sem(12), sem(12), sem(nx), sem(nx), sem(ny), sem(ny),
        ]
        return pl.pallas_call(
            functools.partial(kernel, nx, ny),
            out_shape=jax.ShapeDtypeStruct((16, 16, 512), F32),
            in_specs=[pl.BlockSpec(memory_space=pl.ANY)] * 3,
            out_specs=pl.BlockSpec(memory_space=pltpu.VMEM),
            scratch_shapes=scratch,
            compiler_params=pltpu.CompilerParams(
                collective_id=0, has_side_effects=True, vmem_limit_bytes=30 * 1024 * 1024
            ),
        )(*[pltpu.with_memory_space_constraint(a, pltpu.HBM) for a in (p, d, m)])

    spec = P("gx", "gy", None)
    return jax.shard_map(
        local, mesh=mesh, in_specs=(spec, spec, spec), out_specs=spec, check_vma=False
    )
```

```python
import functools

import jax
import jax.numpy as jnp
from jax import lax
from jax.experimental import pallas as pl
from jax.experimental.pallas import tpu as pltpu
from jax.sharding import PartitionSpec as P

MESH = pl.DeviceIdType.MESH
F32 = jnp.float32
BF16 = jnp.bfloat16

S1 = 0.05
S2 = 0.2
S3 = 0.8
MIDPOINT = (2.0 + 0.3) / 2
HALFWIDTH = (2.0 - 0.3) / 2
SIGMA = MIDPOINT / HALFWIDTH
P1 = 1.0 / SIGMA
P2 = 1.0 / (2.0 * SIGMA - P1)
CA = P2 * P1
CB = 2.0 * P2 / HALFWIDTH
INV = 1.0 / MIDPOINT
ALPHA = CA + CB * (MIDPOINT - 1.0)
STEP = CB * MIDPOINT
BETA = 1.0 / CB - 1.0
GAMMA = CA / CB
NEAR = [(-1, 0), (1, 0), (0, -1), (0, 1), (-1, -1), (-1, 1), (1, -1), (1, 1)]


def thirds(x):
    high = x.astype(BF16)
    rest = x - high.astype(F32)
    middle = rest.astype(BF16)
    low = (rest - middle.astype(F32)).astype(BF16)
    return high, middle, low


def exact_dot(x, matrix):
    total = None
    for part in thirds(x):
        term = jnp.dot(part, matrix, preferred_element_type=F32)
        total = term if total is None else total + term
    return total


def weighted_sum(f):
    q = pltpu.roll(f, 1, 2) + pltpu.roll(f, f.shape[2] - 1, 2)
    face = 0.5 * f + 0.125 * q
    edge = 0.125 * f + 0.0625 * q
    rows = f.shape[1]
    a = 0.5 * q + (pltpu.roll(face, 1, 1) + pltpu.roll(face, rows - 1, 1))
    b = face + (pltpu.roll(edge, 1, 1) + pltpu.roll(edge, rows - 1, 1))
    return a[1:-1] + (b[:-2] + b[2:])


def coarse_operator(v, mob, mob_sum):
    c = v[1:-1]
    m = mob[1:-1]
    return S3 * c + 0.5 * (
        5.0 * m * c - m * weighted_sum(v) + c * mob_sum - weighted_sum(mob * v)
    )


def fine_next(v):
    turned = pltpu.roll(v, 127, 2)
    lane = lax.broadcasted_iota(jnp.int32, v.shape, 2)
    return jnp.where(lane == 127, jnp.concatenate([turned[1:], turned[:1]], axis=0), turned)


def fine_before(v):
    turned = pltpu.roll(v, 1, 2)
    lane = lax.broadcasted_iota(jnp.int32, v.shape, 2)
    return jnp.where(lane == 0, jnp.concatenate([turned[3:], turned[:3]], axis=0), turned)


def mid_next(v):
    return jnp.concatenate([v[1:], pltpu.roll(v[:1], 127, 2)], axis=0)


def mid_before(v):
    return jnp.concatenate([pltpu.roll(v[1:], 1, 2), v[:1]], axis=0)


def kernel(
    nx, ny,
    p_hbm, d_hbm, m_hbm, out,
    px, mf, u, u2, d, g, dg, w, kx, ky, kz,
    xr, ys, yr, kyf, gyf, gxf, dl, rs, tmat, pmat, pout,
    mid_b, mid_stage, mid_rx, mid_ry, mid_rc, b2, m2, w2, d2, kx2, ky2, kz2,
    va, vb, rr, x2, xk,
    cstage, crecv, cm, cw, cb, ce, t2,
    base, fstage, frecv, fk,
    ar1, ar2,
    cst, crn, vf, v2f, ktf, k12f, kzf, wf, uf, bcs, bcr,
    nst, nrx, nry, nrc, ring, ringr, pcor,
    in_sem, fs, fr, ms, mr, cs, cr, xs, xrs, as1, ar1s, as2, ar2s,
):
    gx = lax.axis_index("gx")
    gy = lax.axis_index("gy")
    IN = slice(8, 24)
    LO = slice(7, 23)
    HI = slice(9, 25)

    def device(ox, oy):
        return (lax.rem(gx + (ox % nx), nx), lax.rem(gy + (oy % ny), ny))

    peers = {(o, 0) for o in range(1, nx)} | {(0, o) for o in range(1, ny)}
    peers |= {(dx % nx, dy % ny) for dx, dy in NEAR}
    peers = sorted(peers - {(0, 0)})

    loads = []
    for n, (src, dst) in enumerate(
        ((m_hbm, mf.at[1:17, :, IN, :]), (p_hbm, px.at[1:17, :, IN, :]), (d_hbm, d))
    ):
        loads.append(
            [
                pltpu.make_async_copy(
                    src.at[:, :, 128 * t : 128 * t + 128], dst.at[:, t], in_sem.at[n, t]
                )
                for t in range(4)
            ]
        )
        for c in loads[-1]:
            c.start()
    barrier = pltpu.get_barrier_semaphore()
    for ox, oy in peers:
        pl.semaphore_signal(barrier, inc=1, device_id=device(ox, oy), device_id_type=MESH)

    def remote(src, dst, ssem, rsem, ox, oy):
        return pltpu.make_async_remote_copy(
            src_ref=src, dst_ref=dst, send_sem=ssem, recv_sem=rsem,
            device_id=device(ox, oy), device_id_type=MESH,
        )

    def planes(start, stop, width, body):
        def several(j, carry):
            for q in range(width):
                body(start + width * j + q)
            return carry

        lax.fori_loop(0, (stop - start) // width, several, 0)

    zeros = jnp.zeros((4, 8, 128), F32)
    rims = (mf, px, u, u2)
    for a in rims:
        for plane in (0, 17):
            a[plane, :, 8:16, :] = zeros
            a[plane, :, 16:24, :] = zeros

    def clear(i):
        for a in rims:
            a[i + 1, :, 0:8, :] = zeros
            a[i + 1, :, 24:32, :] = zeros
        ky[i, :, 0:8, :] = zeros

    planes(0, 16, 2, clear)

    zi = lax.broadcasted_iota(jnp.int32, tmat.shape, 0)
    ci = lax.broadcasted_iota(jnp.int32, tmat.shape, 1)
    hit = (zi >> 1) == (((ci & 127) << 1) + (ci >> 7))
    tmat[...] = jnp.where(hit, 1.0, 0.0).astype(BF16)
    zi = lax.broadcasted_iota(jnp.int32, pmat.shape, 1)
    ci = lax.broadcasted_iota(jnp.int32, pmat.shape, 0)
    hit = (zi >> 1) == (((ci & 127) << 1) + (ci >> 7))
    pmat[...] = jnp.where(hit, 1.0, 0.0).astype(BF16)

    def pack_rows(arr, n, layer=0, off=1, row=8):
        low, high = row + layer, row + 15 - layer
        for x in range(16):
            ys[n, 0, :, x : x + 1, :] = arr[x + off, :, low : low + 1, :]
            ys[n, 1, :, x : x + 1, :] = arr[x + off, :, high : high + 1, :]

    def fine_send(arr, n, layer=0, off=1, row=8):
        rows = slice(row, row + 16)
        low, high = arr.at[off + layer, :, rows, :], arr.at[off + 15 - layer, :, rows, :]
        copies = [
            remote(low, xr.at[n, 1], fs.at[n, 0], fr.at[n, 0], -1, 0),
            remote(high, xr.at[n, 0], fs.at[n, 1], fr.at[n, 1], 1, 0),
            remote(ys.at[n, 0], yr.at[n, 1], fs.at[n, 2], fr.at[n, 2], 0, -1),
            remote(ys.at[n, 1], yr.at[n, 0], fs.at[n, 3], fr.at[n, 3], 0, 1),
        ]
        for c in copies:
            c.start()
        return copies

    def wait(copies):
        for c in copies:
            c.wait()

    def wait_sent(copies):
        for c in copies:
            c.wait_send()

    def wait_arrived(copies):
        for c in copies:
            c.wait_recv()

    def corner_send(arr, n):
        copies = []
        for k, (dx, dy) in enumerate(NEAR[4:]):
            x, y = 1 + 15 * (k // 2), 8 + 15 * (k % 2)
            for t in range(4):
                cst[n, k, t : t + 1, :] = arr[x, t, y : y + 1, :]
            copies.append(
                remote(cst.at[n, k], crn.at[n, 3 - k], fs.at[7 + n, k], fr.at[7 + n, k], dx, dy)
            )
            copies[-1].start()
        return copies

    def restrict_fine(arr, off, row, scale):
        for j in range(8):
            for t in range(4):
                total = None
                for q in range(2):
                    for h in range(2):
                        part = arr[2 * j + q + off, t, pl.ds(row + h, 8, stride=2), :]
                        total = part if total is None else total + part
                rs[8 * j : 8 * j + 8, 128 * t : 128 * t + 128] = total * scale
        return exact_dot(rs[...], tmat[...])

    def mid_put(n, got):
        blocks = []
        for x in range(8):
            rows = got[8 * x : 8 * x + 8]
            v = jnp.stack([rows[:, :128], rows[:, 128:]], axis=0)
            mid_b[n, x] = v
            blocks.append(v)
        return blocks

    def mid_fold(n, blocks):
        low = lax.broadcasted_iota(jnp.int32, (2, 8, 128), 1) < 4
        for t in range(4):
            a, b = blocks[2 * t], blocks[2 * t + 1]
            mid_stage[n, 0, t] = jnp.where(low, a, pltpu.roll(b, 4, 1))
            mid_stage[n, 1, t] = jnp.where(low, pltpu.roll(a, 4, 1), b)

    def rhs_send():
        for q in range(2):
            for k in range(4):
                for j in range(2):
                    nst[j, q, :, 2 * k : 2 * k + 2, :] = mid_b[
                        1, 4 * q + k, :, 6 * j : 6 * j + 2, :
                    ]
        copies = [
            remote(mid_b.at[1, 0:2], nrx.at[1], ms.at[1, 0], mr.at[1, 0], -1, 0),
            remote(mid_b.at[1, 6:8], nrx.at[0], ms.at[1, 1], mr.at[1, 1], 1, 0),
            remote(nst.at[0], nry.at[1], ms.at[1, 2], mr.at[1, 2], 0, -1),
            remote(nst.at[1], nry.at[0], ms.at[1, 3], mr.at[1, 3], 0, 1),
        ]
        k = 4
        for i, dx in enumerate((-1, 1)):
            for j, dy in enumerate((-1, 1)):
                copies.append(
                    remote(
                        nst.at[j, i], nrc.at[1 - i, 1 - j], ms.at[1, k], mr.at[1, k], dx, dy
                    )
                )
                k += 1
        for c in copies:
            c.start()
        return copies

    def rhs_place():
        for i in range(2):
            for x in range(2):
                plane = 2 + 10 * i + x
                b2[plane, :, 12:20, :] = nrx[i, x]
                at = 4 - 4 * i + 2 * x
                for j in range(2):
                    row = 10 + 10 * j
                    b2[plane, :, row : row + 2, :] = nrc[i, j, :, at : at + 2, :]
        for j in range(2):
            row = 10 + 10 * j
            for q in range(2):
                for k in range(4):
                    b2[4 + 4 * q + k, :, row : row + 2, :] = nry[j, q, :, 2 * k : 2 * k + 2, :]

    def mid_send(n):
        copies = [
            remote(mid_b.at[n, 0:4], mid_rx.at[n, 1], ms.at[n, 0], mr.at[n, 0], -1, 0),
            remote(mid_b.at[n, 4:8], mid_rx.at[n, 0], ms.at[n, 1], mr.at[n, 1], 1, 0),
            remote(mid_stage.at[n, 0], mid_ry.at[n, 1], ms.at[n, 2], mr.at[n, 2], 0, -1),
            remote(mid_stage.at[n, 1], mid_ry.at[n, 0], ms.at[n, 3], mr.at[n, 3], 0, 1),
        ]
        k = 4
        for i, dx in enumerate((-1, 1)):
            for j, dy in enumerate((-1, 1)):
                copies.append(
                    remote(
                        mid_stage.at[n, j, 2 * i : 2 * i + 2], mid_rc.at[n, 1 - i, 1 - j],
                        ms.at[n, k], mr.at[n, k], dx, dy,
                    )
                )
                k += 1
        for c in copies:
            c.start()
        return copies

    def mid_place(n, ext):
        for i in range(2):
            for x in range(4):
                ext[12 * i + x, :, 12:20, :] = mid_rx[n, i, x]
            for t in range(4):
                for q in range(2):
                    ext[4 + 2 * t + q, :, 8 + 12 * i : 12 + 12 * i, :] = mid_ry[
                        n, i, t, :, 4 * q : 4 * q + 4, :
                    ]
            for j in range(2):
                for t in range(2):
                    for q in range(2):
                        ext[12 * i + 2 * t + q, :, 8 + 12 * j : 12 + 12 * j, :] = mid_rc[
                            n, i, j, t, :, 4 * q : 4 * q + 4, :
                        ]

    def mid_own(n, ext):
        for x in range(8):
            ext[4 + x, :, 12:20, :] = mid_b[n, x]

    def coarse_block(arr, n, row, scale):
        for x in range(4):
            total = None
            for q in range(2):
                for t in range(2):
                    for h in range(2):
                        part = arr[4 + 2 * x + q, t, pl.ds(row + h, 4, stride=2), :]
                        total = part if total is None else total + part
            cstage[n, 4 * x : 4 * x + 4, :] = total * scale

    def coarse_send(n):
        copies = []
        for k, (dx, dy) in enumerate(NEAR):
            copies.append(
                remote(cstage.at[n], crecv.at[n, k], cs.at[n, k], cr.at[n, k], dx, dy)
            )
            copies[-1].start()
        return copies

    def coarse_wait(copies, n, ext):
        def place(dx, dy, block):
            for x in range(4):
                ext[4 * dx + 4 + x, 4 * dy + 4 : 4 * dy + 8, :] = block[4 * x : 4 * x + 4, :]

        place(0, 0, cstage.at[n])
        wait(copies)
        for k, (dx, dy) in enumerate(NEAR):
            place(-dx, -dy, crecv.at[n, k])

    def fine_sum(arr, i):
        c = arr[i + 1, :, IN, :]
        z = kz[i]
        total = kx[i] * arr[i, :, IN, :] + kx[i + 1] * arr[i + 2, :, IN, :]
        total = total + ky[i, :, LO, :] * arr[i + 1, :, LO, :]
        total = total + ky[i, :, IN, :] * arr[i + 1, :, HI, :]
        return c, total + z * fine_next(c) + fine_before(z * c)

    def mid_sum(arr, i):
        c = arr[i, :, IN, :]
        z = kz2[i]
        total = kx2[i] * arr[i - 1, :, IN, :] + kx2[i + 1] * arr[i + 1, :, IN, :]
        total = total + ky2[i, :, LO, :] * arr[i, :, LO, :]
        total = total + ky2[i, :, IN, :] * arr[i, :, HI, :]
        return c, total + z * mid_next(c) + mid_before(z * c)

    def add_rows(arr, off, row):
        for x in range(16):
            for f in range(2):
                k = row + 15 * f
                arr[x + off, :, k : k + 1, :] = (
                    arr[x + off, :, k : k + 1, :] + dl[f, :, x : x + 1, :]
                )

    wait(loads[0])
    pack_rows(mf, 0)
    mid_fold(0, mid_put(0, restrict_fine(mf, 1, 8, 0.125)))
    wait(loads[1])
    pack_rows(px, 1)
    wait(loads[2])
    pl.semaphore_wait(barrier, len(peers))
    m_copies = fine_send(mf, 0)
    p_copies = fine_send(px, 1)

    def coefficients(i):
        c = mf[i + 1, :, IN, :]
        below = 0.5 * (c + mf[i, :, IN, :])
        above = c + mf[i + 2, :, IN, :]
        left = c + mf[i + 1, :, LO, :]
        right = 0.5 * (c + mf[i + 1, :, HI, :])
        after = 0.5 * (c + fine_next(c))
        before = c + fine_before(c)
        kx[i] = below
        ky[i, :, IN, :] = right
        kz[i] = after
        dg[i] = (S1 + below + right + after) + 0.5 * (above + left + before)

    planes(0, 16, 4, coefficients)
    kx[16] = 0.5 * mf[16, :, IN, :]

    def first_sum(i):
        c, total = fine_sum(px, i)
        g[i] = d[i] + total

    planes(0, 16, 4, first_sum)
    pack_rows(d, 4, 0, 0, 0)
    pack_rows(mf, 5, 1)
    wait_sent(m_copies)
    wait_sent(p_copies)
    m2_copies = mid_send(0)

    wait_arrived(m_copies)
    for f in range(2):
        face = 0.5 * xr[0, f]
        kx[16 * f] = kx[16 * f] + face
        dg[15 * f] = dg[15 * f] + face
        face = 0.5 * yr[0, f]
        kyf[f] = 0.5 * ys[0, f] + face
        dl[f] = face
    add_rows(dg, 0, 0)
    wait_arrived(p_copies)
    for f in range(2):
        g[15 * f] = g[15 * f] + kx[16 * f] * xr[1, f]
        dl[f] = kyf[f] * yr[1, f]
    add_rows(g, 0, 0)

    def first_step(i):
        weight = INV / dg[i]
        w[i] = weight
        u[i + 1, :, IN, :] = weight * g[i] - INV * px[i + 1, :, IN, :]

    planes(0, 16, 8, first_step)
    pack_rows(u, 2)
    u_copies = fine_send(u, 2)

    def second_sum(i):
        c, total = fine_sum(u, i)
        u2[i + 1, :, IN, :] = ALPHA * c + STEP * (w[i] * total)

    planes(0, 16, 4, second_sum)
    wait_sent(u_copies)
    for x in range(16):
        for f in range(2):
            gyf[f, :, x : x + 1, :] = w[x, :, 15 * f : 15 * f + 1, :]
    for f in range(2):
        gyf[f] = STEP * (gyf[f] * kyf[f])
        gxf[f] = STEP * (w[15 * f] * kx[16 * f])
    mid_own(0, m2)
    wait(m2_copies)
    mid_place(0, m2)
    coarse_block(m2, 0, 12, 0.125)
    m3_copies = coarse_send(0)

    wait_arrived(u_copies)
    for f in range(2):
        k = 1 + 15 * f
        u2[k, :, IN, :] = u2[k, :, IN, :] + gxf[f] * xr[2, f]
        dl[f] = gyf[f] * yr[2, f]
    add_rows(u2, 1, 8)
    pack_rows(u2, 3)
    u2_copies = fine_send(u2, 3)

    def third_sum(i):
        c, total = fine_sum(u2, i)
        before = u[i + 1, :, IN, :]
        g[i] = dg[i] * (BETA * c - GAMMA * before) + total
        px[i + 1, :, IN, :] = px[i + 1, :, IN, :] + before + c

    planes(0, 16, 4, third_sum)
    wait_sent(u2_copies)

    def mid_coefficients(i):
        c = m2[i, :, IN, :]
        below = 0.5 * (c + m2[i - 1, :, IN, :])
        above = 0.5 * (c + m2[i + 1, :, IN, :])
        left = c + m2[i, :, LO, :]
        right = 0.5 * (c + m2[i, :, HI, :])
        after = 0.5 * (c + mid_next(c))
        before = c + mid_before(c)
        kx2[i] = below
        kx2[i + 1] = above
        ky2[i, :, IN, :] = right
        kz2[i] = after
        diagonal = (S2 + below + above + right + after) + 0.5 * (left + before)
        d2[i] = diagonal
        w2[i] = INV / diagonal

    planes(1, 15, 7, mid_coefficients)
    coarse_wait(m3_copies, 0, cm)
    mob = cm[...]
    lap = weighted_sum(mob)
    cw[1:11] = 0.8 / (S3 + 0.5 * (5.0 * mob[1:-1] + lap))
    for x in range(4):
        cstage[1, 4 * x : 4 * x + 4, :] = cw[4 + x, 4:8, :]
    w3_copies = coarse_send(1)

    wait_arrived(u2_copies)
    for f in range(2):
        g[15 * f] = g[15 * f] + kx[16 * f] * xr[3, f]
        dl[f] = kyf[f] * yr[3, f]
    add_rows(g, 0, 0)
    mid_put(1, restrict_fine(g, 0, 0, 0.5))
    b2_copies = rhs_send()

    pack_rows(px, 6, 1)
    def response_one(i):
        vb[i, :, IN, :] = (-S2) * w2[i]

    planes(1, 15, 7, response_one)

    def response_two(i):
        c, total = mid_sum(vb, i)
        xk[i] = 1.0 + (1.0 + ALPHA) * c + STEP * (w2[i] * total)

    planes(2, 14, 6, response_two)
    for x in range(8):
        fk[2, :, x : x + 1, :] = xk[4 + x, :, 3:4, :]
        fk[3, :, x : x + 1, :] = xk[4 + x, :, 12:13, :]
    fk[0] = xk[3, :, 4:12, :]
    fk[1] = xk[12, :, 4:12, :]
    coarse_wait(w3_copies, 1, cw)
    weight = cw[...]
    y = jnp.ones_like(weight)
    psi = y
    for k in range(3):
        inner = slice(k, 12 - k)
        y = y[1:-1] - coarse_operator(weight[inner] * y, mob[inner], lap[k : 10 - k])
        psi = psi[1:-1] + y
    ce[0:4] = 1.0 - S3 * (weight[4:8] * psi[1:5])
    for f in range(2):
        xr[1, f] = xr[1, f] + xr[2, f] + xr[3, f]
        yr[1, f] = yr[1, f] + yr[2, f] + yr[3, f]
    mid_own(1, b2)
    wait_sent(b2_copies)
    x1_copies = fine_send(px, 6, 1) + corner_send(px, 1)
    wait_arrived(b2_copies)
    rhs_place()

    def mid_one(i):
        va[i, :, IN, :] = w2[i] * b2[i, :, IN, :]

    planes(2, 14, 6, mid_one)

    def mid_two(i):
        c, total = mid_sum(va, i)
        step = ALPHA * c + STEP * (w2[i] * total)
        vb[i, :, IN, :] = step
        x2[i] = c + step

    planes(3, 13, 5, mid_two)

    def mid_three(i):
        c, total = mid_sum(vb, i)
        rr[i] = d2[i] * (BETA * c - GAMMA * va[i, :, IN, :]) + total

    planes(4, 12, 4, mid_three)
    coarse_block(rr, 2, 4, 0.5)
    b3_copies = coarse_send(2)
    for f in range(2):
        k = 5 + 5 * f
        ring[f] = x2[k, :, 4:12, :]
        for x in range(8):
            ring[2 + f, :, x : x + 1, :] = x2[4 + x, :, k : k + 1, :]
    ring_copies = [
        remote(ring.at[f], ringr.at[f + 1 - 2 * (f % 2)], xs.at[8 + f], xrs.at[8 + f], ox, oy)
        for f, (ox, oy) in enumerate(NEAR[:4])
    ]
    for c in ring_copies:
        c.start()

    part = jnp.zeros((1, 128), F32)
    partm = jnp.zeros((1, 128), F32)
    for x in range(4):
        part = part + jnp.sum(
            ce[x, 4:8, :] * cstage[2, 4 * x : 4 * x + 4, :], axis=0, keepdims=True
        )
        partm = partm + jnp.sum(cstage[0, 4 * x : 4 * x + 4, :], axis=0, keepdims=True)
    ar1[0, 0:1, :] = part
    ar1[0, 1:2, :] = partm
    sums = []
    for o in range(1, nx):
        sums.append(remote(ar1.at[0], ar1.at[o], as1.at[o], ar1s.at[o], o, 0))
        sums[-1].start()

    d_copies = fine_send(d, 4, 0, 0, 0)
    far_copies = fine_send(mf, 5, 1) + corner_send(mf, 0)
    coarse_wait(b3_copies, 2, cb)
    rhs = cb[...]
    e = weight * rhs
    for k in range(3):
        inner = slice(k, 12 - k)
        e = e[1:-1] + weight[k + 1 : 11 - k] * (
            rhs[k + 1 : 11 - k] - coarse_operator(e, mob[inner], lap[k : 10 - k])
        )
    wait(sums)
    total = ar1[0]
    for o in range(1, nx):
        total = total + ar1[o]
    ar2[0] = total
    sums = []
    for o in range(1, ny):
        sums.append(remote(ar2.at[0], ar2.at[o], as2.at[o], ar2s.at[o], 0, o))
        sums[-1].start()

    wait(ring_copies)
    for f in range(2):
        x2[2 + 11 * f, :, 4:12, :] = ringr[f]
        row = 2 + 11 * f
        for x in range(8):
            x2[4 + x, :, row : row + 1, :] = ringr[2 + f, :, x : x + 1, :]
    ce[3:9] = e
    for x in range(6):
        for h in range(2):
            t2[x, pl.ds(h, 8, stride=2), :] = ce[3 + x, 2:10, :]
    for x in range(6):
        v = t2[x]
        both = jnp.stack([v, v], axis=0)
        for q in range(2):
            va[2 + 2 * x + q, :, IN, :] = x2[2 + 2 * x + q] + both

    def post_one(i):
        c, total = mid_sum(va, i)
        vb[i, :, IN, :] = w2[i] * (b2[i, :, IN, :] + total) - INV * c

    planes(3, 13, 5, post_one)

    def post_two(i):
        c, total = mid_sum(vb, i)
        done = va[i, :, IN, :] + (1.0 + ALPHA) * c + STEP * (w2[i] * total)
        base[i - 4] = done[:, 4:12, :]

    planes(4, 12, 4, post_two)
    for x in range(8):
        fstage[0, :, x : x + 1, :] = base[x, :, 0:1, :]
        fstage[1, :, x : x + 1, :] = base[x, :, 7:8, :]
    x_copies = [
        remote(base.at[0], frecv.at[1], xs.at[0], xrs.at[0], -1, 0),
        remote(base.at[7], frecv.at[0], xs.at[1], xrs.at[1], 1, 0),
        remote(fstage.at[0], frecv.at[3], xs.at[2], xrs.at[2], 0, -1),
        remote(fstage.at[1], frecv.at[2], xs.at[3], xrs.at[3], 0, 1),
    ]
    for k, (dx, dy) in enumerate(NEAR[4:]):
        x, y = 7 * (k // 2), 7 * (k % 2)
        for t in range(2):
            bcs[k, t : t + 1, :] = base[x, t, y : y + 1, :]
        x_copies.append(
            remote(bcs.at[k], bcr.at[3 - k], xs.at[4 + k], xrs.at[4 + k], dx, dy)
        )
    for c in x_copies:
        c.start()

    wait(d_copies)
    wait(far_copies)

    def corners(f):
        return ((0, 1), (2, 3), (0, 2), (1, 3))[f]

    for f in range(4):
        first, second = (xr.at[0, f], xr.at[5, f]) if f < 2 else (yr.at[0, f - 2], yr.at[5, f - 2])
        k01 = kx[16 * f] if f < 2 else kyf[f - 2]
        c = first[...]
        vf[f, :, IN, :] = c
        for row, k in zip((7, 24), corners(f)):
            for t in range(4):
                vf[f, t, row : row + 1, :] = crn[0, k, t : t + 1, :]
        ktf[f, :, IN, :] = 0.5 * (c + vf[f, :, HI, :])
        ktf[f, :, 7:8, :] = 0.5 * (vf[f, :, 7:8, :] + vf[f, :, 8:9, :])
        k12 = 0.5 * (c + second[...])
        after = 0.5 * (c + fine_next(c))
        k12f[f] = k12
        kzf[f] = after
        wf[f] = INV / (
            S1 + k01 + k12 + ktf[f, :, IN, :] + ktf[f, :, LO, :] + after + fine_before(after)
        )

    wait(sums)
    total = ar2[0]
    for o in range(1, ny):
        total = total + ar2[o]
    cells = 16.0 * 128.0 * nx * ny
    sum_f = jnp.sum(total[0:1, :], axis=1, keepdims=True)
    sum_m = jnp.sum(total[1:2, :], axis=1, keepdims=True)
    kappa = 0.8 * (sum_f / cells) / (S3 + 5.0 * (sum_m / cells))

    for x in range(8):
        v = base[x] + kappa * xk[4 + x, :, 4:12, :]
        pout[8 * x : 8 * x + 8, 0:128] = v[0]
        pout[8 * x : 8 * x + 8, 128:256] = v[1]
    wait(x_copies[:4])
    for f in range(4):
        v = frecv[f] + kappa * fk[f]
        pout[64 + 8 * f : 72 + 8 * f, 0:128] = v[0]
        pout[64 + 8 * f : 72 + 8 * f, 128:256] = v[1]
    pout[...] = exact_dot(pout[:, 0:256], pmat[...])

    wait_sent(x1_copies)
    for j in range(8):
        for t in range(4):
            v = pout[8 * j : 8 * j + 8, 128 * t : 128 * t + 128]
            for q in range(2):
                for h in range(2):
                    rows = pl.ds(8 + h, 8, stride=2)
                    px[2 * j + 1 + q, t, rows, :] = px[2 * j + 1 + q, t, rows, :] + v
    for f in range(4):
        first = xr.at[1, f] if f < 2 else yr.at[1, f - 2]
        for t in range(4):
            lanes = slice(128 * t, 128 * t + 128)
            v = pout[64 + 8 * f : 72 + 8 * f, lanes]
            for h in range(2):
                rows = pl.ds(h, 8, stride=2)
                vf[f, t, pl.ds(8 + h, 8, stride=2), :] = first[t, rows, :] + v
    pack_rows(px, 1)
    for f in range(2):
        d[15 * f] = d[15 * f] + kx[16 * f] * vf[f, :, IN, :]
        dl[f] = kyf[f] * vf[2 + f, :, IN, :]
    add_rows(d, 0, 0)

    def fourth_sum(i):
        c, total = fine_sum(px, i)
        u[i + 1, :, IN, :] = w[i] * (d[i] + total) - INV * c

    planes(0, 16, 8, fourth_sum)

    def last_sum(i):
        c, total = fine_sum(u, i)
        done = px[i + 1, :, IN, :] + (1.0 + ALPHA) * c + STEP * (w[i] * total)
        for t in range(4):
            out[i, :, 128 * t : 128 * t + 128] = done[t]

    planes(0, 16, 8, last_sum)

    wait_arrived(x1_copies)
    wait(x_copies[4:])
    for k in range(4):
        x, y = 3 + 9 * (k // 2), 3 + 9 * (k % 2)
        for t in range(2):
            pcor[k : k + 1, 128 * t : 128 * t + 128] = (
                bcr[k, t : t + 1, :] + kappa * xk[x, t, y : y + 1, :]
            )
    pcor[...] = exact_dot(pcor[:, 0:256], pmat[...])
    for f in range(4):
        second = xr.at[6, f] if f < 2 else yr.at[6, f - 2]
        for t in range(4):
            lanes = slice(128 * t, 128 * t + 128)
            v = pout[64 + 8 * f : 72 + 8 * f, lanes]
            for h in range(2):
                rows = pl.ds(h, 8, stride=2)
                v2f[f, t, rows, :] = second[t, rows, :] + v
            for row, k in zip((7, 24), corners(f)):
                vf[f, t, row : row + 1, :] = crn[1, k, t : t + 1, :] + pcor[k : k + 1, lanes]
    for f in range(4):
        if f < 2:
            k01, inside, rhs_f = kx[16 * f], px[1 + 15 * f, :, IN, :], xr[4, f]
        else:
            k01, inside, rhs_f = kyf[f - 2], ys[1, f - 2], yr[4, f - 2]
        c = vf[f, :, IN, :]
        z = kzf[f]
        total = k01 * inside + k12f[f] * v2f[f]
        total = total + ktf[f, :, LO, :] * vf[f, :, LO, :] + ktf[f, :, IN, :] * vf[f, :, HI, :]
        total = total + z * fine_next(c) + fine_before(z * c)
        uf[f] = wf[f] * (rhs_f + total) - INV * c

    for f in range(2):
        face = gxf[f] * uf[f]
        dl[f] = gyf[f] * uf[2 + f]
        for t in range(4):
            lanes = slice(128 * t, 128 * t + 128)
            out[15 * f, :, lanes] = out[15 * f, :, lanes] + face[t]
    for x in range(16):
        for f in range(2):
            for t in range(4):
                lanes = slice(128 * t, 128 * t + 128)
                k = 15 * f
                out[x, k : k + 1, lanes] = out[x, k : k + 1, lanes] + dl[f, t, x : x + 1, :]


def solution(mesh):
    nx, ny = mesh.shape["gx"], mesh.shape["gy"]

    def local(p, d, m):
        vm = lambda *s: pltpu.VMEM(s, F32)
        sem = lambda *s: pltpu.SemaphoreType.DMA(s)
        plane = (16, 4, 16, 128)
        face = (4, 16, 128)
        scratch = [
            vm(18, 4, 32, 128), vm(18, 4, 32, 128), vm(18, 4, 32, 128), vm(18, 4, 32, 128),
            vm(*plane), vm(*plane), vm(*plane), vm(*plane),
            vm(17, 4, 16, 128), vm(16, 4, 32, 128), vm(*plane),
            vm(7, 2, *face), vm(7, 2, *face), vm(7, 2, *face),
            vm(2, *face), vm(2, *face), vm(2, *face), vm(2, *face), vm(64, 512),
            pltpu.VMEM((512, 256), BF16), pltpu.VMEM((256, 512), BF16), vm(96, 512),
            vm(2, 8, 2, 8, 128), vm(2, 2, 4, 2, 8, 128), vm(2, 2, 4, 2, 8, 128),
            vm(2, 2, 4, 2, 8, 128), vm(2, 2, 2, 2, 2, 8, 128),
            vm(16, 2, 32, 128), vm(16, 2, 32, 128), vm(16, 2, 16, 128), vm(16, 2, 16, 128),
            vm(17, 2, 16, 128), vm(16, 2, 32, 128), vm(16, 2, 16, 128),
            vm(16, 2, 32, 128), vm(16, 2, 32, 128), vm(16, 2, 16, 128), vm(16, 2, 16, 128),
            vm(16, 2, 16, 128),
            vm(3, 16, 128), vm(3, 8, 16, 128), vm(12, 16, 128), vm(12, 16, 128), vm(12, 16, 128),
            vm(12, 16, 128), vm(6, 16, 128),
            vm(8, 2, 8, 128), vm(2, 2, 8, 128), vm(4, 2, 8, 128), vm(4, 2, 8, 128),
            vm(nx, 2, 128), vm(ny, 2, 128),
            vm(2, 4, 4, 128), vm(2, 4, 4, 128), vm(4, 4, 32, 128), vm(4, *face), vm(4, 4, 32, 128),
            vm(4, *face), vm(4, *face), vm(4, *face), vm(4, *face), vm(4, 2, 128), vm(4, 2, 128),
            vm(2, 2, 2, 8, 128), vm(2, 2, 2, 8, 128), vm(2, 2, 2, 8, 128), vm(2, 2, 2, 8, 128),
            vm(4, 2, 8, 128), vm(4, 2, 8, 128), vm(8, 512),
            sem(3, 4), sem(9, 4), sem(9, 4), sem(2, 8), sem(2, 8), sem(3, 8), sem(3, 8),
            sem(12), sem(12), sem(nx), sem(nx), sem(ny), sem(ny),
        ]
        return pl.pallas_call(
            functools.partial(kernel, nx, ny),
            out_shape=jax.ShapeDtypeStruct((16, 16, 512), F32),
            in_specs=[pl.BlockSpec(memory_space=pl.ANY)] * 3,
            out_specs=pl.BlockSpec(memory_space=pltpu.VMEM),
            scratch_shapes=scratch,
            compiler_params=pltpu.CompilerParams(
                collective_id=0, has_side_effects=True, vmem_limit_bytes=30 * 1024 * 1024
            ),
        )(*[pltpu.with_memory_space_constraint(a, pltpu.HBM) for a in (p, d, m)])

    spec = P("gx", "gy", None)
    return jax.shard_map(
        local, mesh=mesh, in_specs=(spec, spec, spec), out_specs=spec, check_vma=False
    )
```

```python
import functools

import jax
import jax.numpy as jnp
from jax import lax
from jax.experimental import pallas as pl
from jax.experimental.pallas import tpu as pltpu
from jax.sharding import PartitionSpec as P

MESH = pl.DeviceIdType.MESH
F32 = jnp.float32
BF16 = jnp.bfloat16

S1 = 0.05
S2 = 0.2
S3 = 0.8
MIDPOINT = (2.0 + 0.3) / 2
HALFWIDTH = (2.0 - 0.3) / 2
SIGMA = MIDPOINT / HALFWIDTH
P1 = 1.0 / SIGMA
P2 = 1.0 / (2.0 * SIGMA - P1)
CA = P2 * P1
CB = 2.0 * P2 / HALFWIDTH
INV = 1.0 / MIDPOINT
ALPHA = CA + CB * (MIDPOINT - 1.0)
STEP = CB * MIDPOINT
BETA = 1.0 / CB - 1.0
GAMMA = CA / CB
NEAR = [(-1, 0), (1, 0), (0, -1), (0, 1), (-1, -1), (-1, 1), (1, -1), (1, 1)]


def thirds(x):
    high = x.astype(BF16)
    rest = x - high.astype(F32)
    middle = rest.astype(BF16)
    low = (rest - middle.astype(F32)).astype(BF16)
    return high, middle, low


def exact_dot(x, matrix):
    total = None
    for part in thirds(x):
        term = jnp.dot(part, matrix, preferred_element_type=F32)
        total = term if total is None else total + term
    return total


def weighted_sum(f):
    q = pltpu.roll(f, 1, 2) + pltpu.roll(f, f.shape[2] - 1, 2)
    face = 0.5 * f + 0.125 * q
    edge = 0.125 * f + 0.0625 * q
    rows = f.shape[1]
    a = 0.5 * q + (pltpu.roll(face, 1, 1) + pltpu.roll(face, rows - 1, 1))
    b = face + (pltpu.roll(edge, 1, 1) + pltpu.roll(edge, rows - 1, 1))
    return a[1:-1] + (b[:-2] + b[2:])


def coarse_operator(v, mob, mob_sum):
    c = v[1:-1]
    m = mob[1:-1]
    return S3 * c + 0.5 * (
        5.0 * m * c - m * weighted_sum(v) + c * mob_sum - weighted_sum(mob * v)
    )


def fine_next(v):
    turned = pltpu.roll(v, 127, 2)
    lane = lax.broadcasted_iota(jnp.int32, v.shape, 2)
    return jnp.where(lane == 127, jnp.concatenate([turned[1:], turned[:1]], axis=0), turned)


def fine_before(v):
    turned = pltpu.roll(v, 1, 2)
    lane = lax.broadcasted_iota(jnp.int32, v.shape, 2)
    return jnp.where(lane == 0, jnp.concatenate([turned[3:], turned[:3]], axis=0), turned)


def mid_next(v):
    return jnp.concatenate([v[1:], pltpu.roll(v[:1], 127, 2)], axis=0)


def mid_before(v):
    return jnp.concatenate([pltpu.roll(v[1:], 1, 2), v[:1]], axis=0)


def kernel(
    nx, ny,
    p_hbm, d_hbm, m_hbm, out,
    px, mf, u, u2, d, g, dg, w, kx, ky, kz,
    xr, ys, yr, kyf, gyf, gxf, dl, rs, tmat, pmat, pout,
    mid_b, mid_stage, mid_rx, mid_ry, mid_rc, b2, m2, w2, d2, kx2, ky2, kz2,
    va, vb, rr, x2, xk,
    cstage, crecv, cm, cw, cb, ce, t2,
    base, fstage, frecv, fk,
    ar1, ar2,
    cst, crn, vf, v2f, ktf, k12f, kzf, wf, uf, bcs, bcr,
    nst, nrx, nry, nrc, ring, ringr, pcor,
    in_sem, fs, fr, ms, mr, cs, cr, xs, xrs, as1, ar1s, as2, ar2s,
):
    gx = lax.axis_index("gx")
    gy = lax.axis_index("gy")
    IN = slice(8, 24)
    LO = slice(7, 23)
    HI = slice(9, 25)

    def device(ox, oy):
        return (lax.rem(gx + (ox % nx), nx), lax.rem(gy + (oy % ny), ny))

    peers = {(o, 0) for o in range(1, nx)} | {(0, o) for o in range(1, ny)}
    peers |= {(dx % nx, dy % ny) for dx, dy in NEAR}
    peers = sorted(peers - {(0, 0)})

    loads = []
    for n, (src, dst) in enumerate(
        ((m_hbm, mf.at[1:17, :, IN, :]), (p_hbm, px.at[1:17, :, IN, :]), (d_hbm, d))
    ):
        loads.append(
            [
                pltpu.make_async_copy(
                    src.at[:, :, 128 * t : 128 * t + 128], dst.at[:, t], in_sem.at[n, t]
                )
                for t in range(4)
            ]
        )
        for c in loads[-1]:
            c.start()
    barrier = pltpu.get_barrier_semaphore()
    for ox, oy in peers:
        pl.semaphore_signal(barrier, inc=1, device_id=device(ox, oy), device_id_type=MESH)

    def remote(src, dst, ssem, rsem, ox, oy):
        return pltpu.make_async_remote_copy(
            src_ref=src, dst_ref=dst, send_sem=ssem, recv_sem=rsem,
            device_id=device(ox, oy), device_id_type=MESH,
        )

    def planes(start, stop, width, body):
        def several(j, carry):
            for q in range(width):
                body(start + width * j + q)
            return carry

        lax.fori_loop(0, (stop - start) // width, several, 0)

    zeros = jnp.zeros((4, 8, 128), F32)
    rims = (mf, px, u, u2)
    for a in rims:
        for plane in (0, 17):
            a[plane, :, 8:16, :] = zeros
            a[plane, :, 16:24, :] = zeros

    def clear(i):
        for a in rims:
            a[i + 1, :, 0:8, :] = zeros
            a[i + 1, :, 24:32, :] = zeros
        ky[i, :, 0:8, :] = zeros

    planes(0, 16, 2, clear)

    zi = lax.broadcasted_iota(jnp.int32, tmat.shape, 0)
    ci = lax.broadcasted_iota(jnp.int32, tmat.shape, 1)
    hit = (zi >> 1) == (((ci & 127) << 1) + (ci >> 7))
    tmat[...] = jnp.where(hit, 1.0, 0.0).astype(BF16)
    zi = lax.broadcasted_iota(jnp.int32, pmat.shape, 1)
    ci = lax.broadcasted_iota(jnp.int32, pmat.shape, 0)
    hit = (zi >> 1) == (((ci & 127) << 1) + (ci >> 7))
    pmat[...] = jnp.where(hit, 1.0, 0.0).astype(BF16)

    def pack_rows(arr, n, layer=0, off=1, row=8):
        low, high = row + layer, row + 15 - layer
        for x in range(16):
            ys[n, 0, :, x : x + 1, :] = arr[x + off, :, low : low + 1, :]
            ys[n, 1, :, x : x + 1, :] = arr[x + off, :, high : high + 1, :]

    def fine_send(arr, n, layer=0, off=1, row=8):
        rows = slice(row, row + 16)
        low, high = arr.at[off + layer, :, rows, :], arr.at[off + 15 - layer, :, rows, :]
        copies = [
            remote(low, xr.at[n, 1], fs.at[n, 0], fr.at[n, 0], -1, 0),
            remote(high, xr.at[n, 0], fs.at[n, 1], fr.at[n, 1], 1, 0),
            remote(ys.at[n, 0], yr.at[n, 1], fs.at[n, 2], fr.at[n, 2], 0, -1),
            remote(ys.at[n, 1], yr.at[n, 0], fs.at[n, 3], fr.at[n, 3], 0, 1),
        ]
        for c in copies:
            c.start()
        return copies

    def wait(copies):
        for c in copies:
            c.wait()

    def wait_sent(copies):
        for c in copies:
            c.wait_send()

    def wait_arrived(copies):
        for c in copies:
            c.wait_recv()

    def corner_send(arr, n):
        copies = []
        for k, (dx, dy) in enumerate(NEAR[4:]):
            x, y = 1 + 15 * (k // 2), 8 + 15 * (k % 2)
            for t in range(4):
                cst[n, k, t : t + 1, :] = arr[x, t, y : y + 1, :]
            copies.append(
                remote(cst.at[n, k], crn.at[n, 3 - k], fs.at[7 + n, k], fr.at[7 + n, k], dx, dy)
            )
            copies[-1].start()
        return copies

    def restrict_fine(arr, off, row, scale):
        for j in range(8):
            for t in range(4):
                total = None
                for q in range(2):
                    for h in range(2):
                        part = arr[2 * j + q + off, t, pl.ds(row + h, 8, stride=2), :]
                        total = part if total is None else total + part
                rs[8 * j : 8 * j + 8, 128 * t : 128 * t + 128] = total * scale
        return exact_dot(rs[...], tmat[...])

    def mid_put(n, got):
        blocks = []
        for x in range(8):
            rows = got[8 * x : 8 * x + 8]
            v = jnp.stack([rows[:, :128], rows[:, 128:]], axis=0)
            mid_b[n, x] = v
            blocks.append(v)
        return blocks

    def mid_fold(n, blocks):
        low = lax.broadcasted_iota(jnp.int32, (2, 8, 128), 1) < 4
        for t in range(4):
            a, b = blocks[2 * t], blocks[2 * t + 1]
            mid_stage[n, 0, t] = jnp.where(low, a, pltpu.roll(b, 4, 1))
            mid_stage[n, 1, t] = jnp.where(low, pltpu.roll(a, 4, 1), b)

    def rhs_send():
        for q in range(2):
            for k in range(4):
                for j in range(2):
                    nst[j, q, :, 2 * k : 2 * k + 2, :] = mid_b[
                        1, 4 * q + k, :, 6 * j : 6 * j + 2, :
                    ]
        copies = [
            remote(mid_b.at[1, 0:2], nrx.at[1], ms.at[1, 0], mr.at[1, 0], -1, 0),
            remote(mid_b.at[1, 6:8], nrx.at[0], ms.at[1, 1], mr.at[1, 1], 1, 0),
            remote(nst.at[0], nry.at[1], ms.at[1, 2], mr.at[1, 2], 0, -1),
            remote(nst.at[1], nry.at[0], ms.at[1, 3], mr.at[1, 3], 0, 1),
        ]
        k = 4
        for i, dx in enumerate((-1, 1)):
            for j, dy in enumerate((-1, 1)):
                copies.append(
                    remote(
                        nst.at[j, i], nrc.at[1 - i, 1 - j], ms.at[1, k], mr.at[1, k], dx, dy
                    )
                )
                k += 1
        for c in copies:
            c.start()
        return copies

    def rhs_place():
        for i in range(2):
            for x in range(2):
                plane = 2 + 10 * i + x
                b2[plane, :, 12:20, :] = nrx[i, x]
                at = 4 - 4 * i + 2 * x
                for j in range(2):
                    row = 10 + 10 * j
                    b2[plane, :, row : row + 2, :] = nrc[i, j, :, at : at + 2, :]
        for j in range(2):
            row = 10 + 10 * j
            for q in range(2):
                for k in range(4):
                    b2[4 + 4 * q + k, :, row : row + 2, :] = nry[j, q, :, 2 * k : 2 * k + 2, :]

    def mid_send(n):
        copies = [
            remote(mid_b.at[n, 0:3], mid_rx.at[n, 1, 0:3], ms.at[n, 0], mr.at[n, 0], -1, 0),
            remote(mid_b.at[n, 5:8], mid_rx.at[n, 0, 1:4], ms.at[n, 1], mr.at[n, 1], 1, 0),
            remote(mid_stage.at[n, 0], mid_ry.at[n, 1], ms.at[n, 2], mr.at[n, 2], 0, -1),
            remote(mid_stage.at[n, 1], mid_ry.at[n, 0], ms.at[n, 3], mr.at[n, 3], 0, 1),
        ]
        k = 4
        for i, dx in enumerate((-1, 1)):
            for j, dy in enumerate((-1, 1)):
                copies.append(
                    remote(
                        mid_stage.at[n, j, 2 * i : 2 * i + 2], mid_rc.at[n, 1 - i, 1 - j],
                        ms.at[n, k], mr.at[n, k], dx, dy,
                    )
                )
                k += 1
        for c in copies:
            c.start()
        return copies

    def mid_place(n, ext):
        for i in range(2):
            for x in range(1 - i, 4 - i):
                ext[12 * i + x, :, 12:20, :] = mid_rx[n, i, x]
            for t in range(4):
                for q in range(2):
                    ext[4 + 2 * t + q, :, 8 + 12 * i : 12 + 12 * i, :] = mid_ry[
                        n, i, t, :, 4 * q : 4 * q + 4, :
                    ]
            for j in range(2):
                for t in range(2):
                    for q in range(2):
                        ext[12 * i + 2 * t + q, :, 8 + 12 * j : 12 + 12 * j, :] = mid_rc[
                            n, i, j, t, :, 4 * q : 4 * q + 4, :
                        ]

    def mid_own(n, ext):
        for x in range(8):
            ext[4 + x, :, 12:20, :] = mid_b[n, x]

    def coarse_block(arr, n, row, scale):
        for x in range(4):
            total = None
            for q in range(2):
                for t in range(2):
                    for h in range(2):
                        part = arr[4 + 2 * x + q, t, pl.ds(row + h, 4, stride=2), :]
                        total = part if total is None else total + part
            cstage[n, 4 * x : 4 * x + 4, :] = total * scale

    def coarse_send(n):
        copies = []
        for k, (dx, dy) in enumerate(NEAR):
            copies.append(
                remote(cstage.at[n], crecv.at[n, k], cs.at[n, k], cr.at[n, k], dx, dy)
            )
            copies[-1].start()
        return copies

    def coarse_wait(copies, n, ext):
        def place(dx, dy, block):
            for x in range(4):
                ext[4 * dx + 4 + x, 4 * dy + 4 : 4 * dy + 8, :] = block[4 * x : 4 * x + 4, :]

        place(0, 0, cstage.at[n])
        wait(copies)
        for k, (dx, dy) in enumerate(NEAR):
            place(-dx, -dy, crecv.at[n, k])

    def fine_sum(arr, i):
        c = arr[i + 1, :, IN, :]
        z = kz[i]
        total = kx[i] * arr[i, :, IN, :] + kx[i + 1] * arr[i + 2, :, IN, :]
        total = total + ky[i, :, LO, :] * arr[i + 1, :, LO, :]
        total = total + ky[i, :, IN, :] * arr[i + 1, :, HI, :]
        return c, total + z * fine_next(c) + fine_before(z * c)

    def mid_sum(arr, i):
        c = arr[i, :, IN, :]
        z = kz2[i]
        total = kx2[i] * arr[i - 1, :, IN, :] + kx2[i + 1] * arr[i + 1, :, IN, :]
        total = total + ky2[i, :, LO, :] * arr[i, :, LO, :]
        total = total + ky2[i, :, IN, :] * arr[i, :, HI, :]
        return c, total + z * mid_next(c) + mid_before(z * c)

    def add_rows(arr, off, row):
        for x in range(16):
            for f in range(2):
                k = row + 15 * f
                arr[x + off, :, k : k + 1, :] = (
                    arr[x + off, :, k : k + 1, :] + dl[f, :, x : x + 1, :]
                )

    wait(loads[0])
    pack_rows(mf, 0)
    mid_fold(0, mid_put(0, restrict_fine(mf, 1, 8, 0.125)))
    wait(loads[1])
    pack_rows(px, 1)
    wait(loads[2])
    pl.semaphore_wait(barrier, len(peers))
    m_copies = fine_send(mf, 0)
    p_copies = fine_send(px, 1)

    def coefficients(i):
        c = mf[i + 1, :, IN, :]
        below = 0.5 * (c + mf[i, :, IN, :])
        above = c + mf[i + 2, :, IN, :]
        left = c + mf[i + 1, :, LO, :]
        right = 0.5 * (c + mf[i + 1, :, HI, :])
        after = 0.5 * (c + fine_next(c))
        before = c + fine_before(c)
        kx[i] = below
        ky[i, :, IN, :] = right
        kz[i] = after
        dg[i] = (S1 + below + right + after) + 0.5 * (above + left + before)

    planes(0, 16, 4, coefficients)
    kx[16] = 0.5 * mf[16, :, IN, :]

    def first_sum(i):
        c, total = fine_sum(px, i)
        g[i] = d[i] + total

    planes(0, 16, 4, first_sum)
    pack_rows(d, 4, 0, 0, 0)
    pack_rows(mf, 5, 1)
    wait_sent(m_copies)
    wait_sent(p_copies)
    m2_copies = mid_send(0)

    wait_arrived(m_copies)
    for f in range(2):
        face = 0.5 * xr[0, f]
        kx[16 * f] = kx[16 * f] + face
        dg[15 * f] = dg[15 * f] + face
        face = 0.5 * yr[0, f]
        kyf[f] = 0.5 * ys[0, f] + face
        dl[f] = face
    add_rows(dg, 0, 0)
    wait_arrived(p_copies)
    for f in range(2):
        g[15 * f] = g[15 * f] + kx[16 * f] * xr[1, f]
        dl[f] = kyf[f] * yr[1, f]
    add_rows(g, 0, 0)

    def first_step(i):
        weight = INV / dg[i]
        w[i] = weight
        u[i + 1, :, IN, :] = weight * g[i] - INV * px[i + 1, :, IN, :]

    planes(0, 16, 8, first_step)
    pack_rows(u, 2)
    u_copies = fine_send(u, 2)

    def second_sum(i):
        c, total = fine_sum(u, i)
        u2[i + 1, :, IN, :] = ALPHA * c + STEP * (w[i] * total)

    planes(0, 16, 4, second_sum)
    wait_sent(u_copies)
    for x in range(16):
        for f in range(2):
            gyf[f, :, x : x + 1, :] = w[x, :, 15 * f : 15 * f + 1, :]
    for f in range(2):
        gyf[f] = STEP * (gyf[f] * kyf[f])
        gxf[f] = STEP * (w[15 * f] * kx[16 * f])
    mid_own(0, m2)
    wait(m2_copies)
    mid_place(0, m2)
    coarse_block(m2, 0, 12, 0.125)
    m3_copies = coarse_send(0)

    wait_arrived(u_copies)
    for f in range(2):
        k = 1 + 15 * f
        u2[k, :, IN, :] = u2[k, :, IN, :] + gxf[f] * xr[2, f]
        dl[f] = gyf[f] * yr[2, f]
    add_rows(u2, 1, 8)
    pack_rows(u2, 3)
    u2_copies = fine_send(u2, 3)

    def third_sum(i):
        c, total = fine_sum(u2, i)
        before = u[i + 1, :, IN, :]
        g[i] = dg[i] * (BETA * c - GAMMA * before) + total
        px[i + 1, :, IN, :] = px[i + 1, :, IN, :] + before + c

    planes(0, 16, 4, third_sum)
    wait_sent(u2_copies)

    def mid_coefficients(i):
        c = m2[i, :, IN, :]
        below = 0.5 * (c + m2[i - 1, :, IN, :])
        above = 0.5 * (c + m2[i + 1, :, IN, :])
        left = c + m2[i, :, LO, :]
        right = 0.5 * (c + m2[i, :, HI, :])
        after = 0.5 * (c + mid_next(c))
        before = c + mid_before(c)
        kx2[i] = below
        kx2[i + 1] = above
        ky2[i, :, IN, :] = right
        kz2[i] = after
        diagonal = (S2 + below + above + right + after) + 0.5 * (left + before)
        d2[i] = diagonal
        w2[i] = INV / diagonal

    planes(2, 14, 6, mid_coefficients)
    coarse_wait(m3_copies, 0, cm)
    mob = cm[...]
    lap = weighted_sum(mob)
    cw[1:11] = 0.8 / (S3 + 0.5 * (5.0 * mob[1:-1] + lap))
    for x in range(4):
        cstage[1, 4 * x : 4 * x + 4, :] = cw[4 + x, 4:8, :]
    w3_copies = coarse_send(1)

    wait_arrived(u2_copies)
    for f in range(2):
        g[15 * f] = g[15 * f] + kx[16 * f] * xr[3, f]
        dl[f] = kyf[f] * yr[3, f]
    add_rows(g, 0, 0)
    mid_put(1, restrict_fine(g, 0, 0, 0.5))
    b2_copies = rhs_send()

    pack_rows(px, 6, 1)
    def response_one(i):
        vb[i, :, IN, :] = (-S2) * w2[i]

    planes(2, 14, 6, response_one)

    def response_two(i):
        c, total = mid_sum(vb, i)
        xk[i] = 1.0 + (1.0 + ALPHA) * c + STEP * (w2[i] * total)

    planes(3, 13, 5, response_two)
    for x in range(8):
        fk[2, :, x : x + 1, :] = xk[4 + x, :, 3:4, :]
        fk[3, :, x : x + 1, :] = xk[4 + x, :, 12:13, :]
    fk[0] = xk[3, :, 4:12, :]
    fk[1] = xk[12, :, 4:12, :]
    coarse_wait(w3_copies, 1, cw)
    weight = cw[...]
    y = jnp.ones_like(weight)
    psi = y
    for k in range(3):
        inner = slice(k, 12 - k)
        y = y[1:-1] - coarse_operator(weight[inner] * y, mob[inner], lap[k : 10 - k])
        psi = psi[1:-1] + y
    ce[0:4] = 1.0 - S3 * (weight[4:8] * psi[1:5])
    for f in range(2):
        xr[1, f] = xr[1, f] + xr[2, f] + xr[3, f]
        yr[1, f] = yr[1, f] + yr[2, f] + yr[3, f]
    mid_own(1, b2)
    wait_sent(b2_copies)
    x1_copies = fine_send(px, 6, 1) + corner_send(px, 1)
    wait_arrived(b2_copies)
    rhs_place()

    def mid_one(i):
        va[i, :, IN, :] = w2[i] * b2[i, :, IN, :]

    planes(2, 14, 6, mid_one)

    def mid_two(i):
        c, total = mid_sum(va, i)
        step = ALPHA * c + STEP * (w2[i] * total)
        vb[i, :, IN, :] = step
        x2[i] = c + step

    planes(3, 13, 5, mid_two)

    def mid_three(i):
        c, total = mid_sum(vb, i)
        rr[i] = d2[i] * (BETA * c - GAMMA * va[i, :, IN, :]) + total

    planes(4, 12, 4, mid_three)
    coarse_block(rr, 2, 4, 0.5)
    b3_copies = coarse_send(2)
    part = jnp.zeros((1, 128), F32)
    partm = jnp.zeros((1, 128), F32)
    for x in range(4):
        part = part + jnp.sum(
            ce[x, 4:8, :] * cstage[2, 4 * x : 4 * x + 4, :], axis=0, keepdims=True
        )
        partm = partm + jnp.sum(cstage[0, 4 * x : 4 * x + 4, :], axis=0, keepdims=True)
    ar1[0, 0:1, :] = part
    ar1[0, 1:2, :] = partm
    sums = []
    for o in range(1, nx):
        sums.append(remote(ar1.at[0], ar1.at[o], as1.at[o], ar1s.at[o], o, 0))
        sums[-1].start()

    for f in range(2):
        k = 5 + 5 * f
        ring[f] = x2[k, :, 4:12, :]
        for x in range(8):
            ring[2 + f, :, x : x + 1, :] = x2[4 + x, :, k : k + 1, :]
    ring_copies = [
        remote(ring.at[f], ringr.at[f + 1 - 2 * (f % 2)], xs.at[8 + f], xrs.at[8 + f], ox, oy)
        for f, (ox, oy) in enumerate(NEAR[:4])
    ]
    for c in ring_copies:
        c.start()

    d_copies = fine_send(d, 4, 0, 0, 0)
    far_copies = fine_send(mf, 5, 1) + corner_send(mf, 0)
    coarse_wait(b3_copies, 2, cb)
    rhs = cb[...]
    e = weight * rhs
    for k in range(3):
        inner = slice(k, 12 - k)
        e = e[1:-1] + weight[k + 1 : 11 - k] * (
            rhs[k + 1 : 11 - k] - coarse_operator(e, mob[inner], lap[k : 10 - k])
        )
    wait(sums)
    total = ar1[0]
    for o in range(1, nx):
        total = total + ar1[o]
    ar2[0] = total
    sums = []
    for o in range(1, ny):
        sums.append(remote(ar2.at[0], ar2.at[o], as2.at[o], ar2s.at[o], 0, o))
        sums[-1].start()

    wait(ring_copies)
    for f in range(2):
        x2[2 + 11 * f, :, 4:12, :] = ringr[f]
        row = 2 + 11 * f
        for x in range(8):
            x2[4 + x, :, row : row + 1, :] = ringr[2 + f, :, x : x + 1, :]
    ce[3:9] = e
    for x in range(6):
        for h in range(2):
            t2[x, pl.ds(h, 8, stride=2), :] = ce[3 + x, 2:10, :]
    for x in range(6):
        v = t2[x]
        both = jnp.stack([v, v], axis=0)
        for q in range(2):
            va[2 + 2 * x + q, :, IN, :] = x2[2 + 2 * x + q] + both

    def post_one(i):
        c, total = mid_sum(va, i)
        vb[i, :, IN, :] = w2[i] * (b2[i, :, IN, :] + total) - INV * c

    planes(3, 13, 5, post_one)

    def post_two(i):
        c, total = mid_sum(vb, i)
        done = va[i, :, IN, :] + (1.0 + ALPHA) * c + STEP * (w2[i] * total)
        base[i - 4] = done[:, 4:12, :]

    planes(4, 12, 4, post_two)
    for x in range(8):
        fstage[0, :, x : x + 1, :] = base[x, :, 0:1, :]
        fstage[1, :, x : x + 1, :] = base[x, :, 7:8, :]
    x_copies = [
        remote(base.at[0], frecv.at[1], xs.at[0], xrs.at[0], -1, 0),
        remote(base.at[7], frecv.at[0], xs.at[1], xrs.at[1], 1, 0),
        remote(fstage.at[0], frecv.at[3], xs.at[2], xrs.at[2], 0, -1),
        remote(fstage.at[1], frecv.at[2], xs.at[3], xrs.at[3], 0, 1),
    ]
    for k, (dx, dy) in enumerate(NEAR[4:]):
        x, y = 7 * (k // 2), 7 * (k % 2)
        for t in range(2):
            bcs[k, t : t + 1, :] = base[x, t, y : y + 1, :]
        x_copies.append(
            remote(bcs.at[k], bcr.at[3 - k], xs.at[4 + k], xrs.at[4 + k], dx, dy)
        )
    for c in x_copies:
        c.start()

    wait(d_copies)
    wait(far_copies)

    def corners(f):
        return ((0, 1), (2, 3), (0, 2), (1, 3))[f]

    for f in range(4):
        first, second = (xr.at[0, f], xr.at[5, f]) if f < 2 else (yr.at[0, f - 2], yr.at[5, f - 2])
        k01 = kx[16 * f] if f < 2 else kyf[f - 2]
        c = first[...]
        vf[f, :, IN, :] = c
        for row, k in zip((7, 24), corners(f)):
            for t in range(4):
                vf[f, t, row : row + 1, :] = crn[0, k, t : t + 1, :]
        ktf[f, :, IN, :] = 0.5 * (c + vf[f, :, HI, :])
        ktf[f, :, 7:8, :] = 0.5 * (vf[f, :, 7:8, :] + vf[f, :, 8:9, :])
        k12 = 0.5 * (c + second[...])
        after = 0.5 * (c + fine_next(c))
        k12f[f] = k12
        kzf[f] = after
        wf[f] = INV / (
            S1 + k01 + k12 + ktf[f, :, IN, :] + ktf[f, :, LO, :] + after + fine_before(after)
        )

    wait(sums)
    total = ar2[0]
    for o in range(1, ny):
        total = total + ar2[o]
    cells = 16.0 * 128.0 * nx * ny
    sum_f = jnp.sum(total[0:1, :], axis=1, keepdims=True)
    sum_m = jnp.sum(total[1:2, :], axis=1, keepdims=True)
    kappa = 0.8 * (sum_f / cells) / (S3 + 5.0 * (sum_m / cells))

    for x in range(8):
        v = base[x] + kappa * xk[4 + x, :, 4:12, :]
        pout[8 * x : 8 * x + 8, 0:128] = v[0]
        pout[8 * x : 8 * x + 8, 128:256] = v[1]
    wait(x_copies[:4])
    for f in range(4):
        v = frecv[f] + kappa * fk[f]
        pout[64 + 8 * f : 72 + 8 * f, 0:128] = v[0]
        pout[64 + 8 * f : 72 + 8 * f, 128:256] = v[1]
    pout[...] = exact_dot(pout[:, 0:256], pmat[...])

    wait_sent(x1_copies)
    for j in range(8):
        for t in range(4):
            v = pout[8 * j : 8 * j + 8, 128 * t : 128 * t + 128]
            for q in range(2):
                for h in range(2):
                    rows = pl.ds(8 + h, 8, stride=2)
                    px[2 * j + 1 + q, t, rows, :] = px[2 * j + 1 + q, t, rows, :] + v
    for f in range(4):
        first = xr.at[1, f] if f < 2 else yr.at[1, f - 2]
        for t in range(4):
            lanes = slice(128 * t, 128 * t + 128)
            v = pout[64 + 8 * f : 72 + 8 * f, lanes]
            for h in range(2):
                rows = pl.ds(h, 8, stride=2)
                vf[f, t, pl.ds(8 + h, 8, stride=2), :] = first[t, rows, :] + v
    pack_rows(px, 1)
    for f in range(2):
        d[15 * f] = d[15 * f] + kx[16 * f] * vf[f, :, IN, :]
        dl[f] = kyf[f] * vf[2 + f, :, IN, :]
    add_rows(d, 0, 0)

    def fourth_sum(i):
        c, total = fine_sum(px, i)
        u[i + 1, :, IN, :] = w[i] * (d[i] + total) - INV * c

    planes(0, 16, 8, fourth_sum)

    def last_sum(i):
        c, total = fine_sum(u, i)
        done = px[i + 1, :, IN, :] + (1.0 + ALPHA) * c + STEP * (w[i] * total)
        for t in range(4):
            out[i, :, 128 * t : 128 * t + 128] = done[t]

    planes(0, 16, 8, last_sum)

    wait_arrived(x1_copies)
    wait(x_copies[4:])
    for k in range(4):
        x, y = 3 + 9 * (k // 2), 3 + 9 * (k % 2)
        for t in range(2):
            pcor[k : k + 1, 128 * t : 128 * t + 128] = (
                bcr[k, t : t + 1, :] + kappa * xk[x, t, y : y + 1, :]
            )
    pcor[...] = exact_dot(pcor[:, 0:256], pmat[...])
    for f in range(4):
        second = xr.at[6, f] if f < 2 else yr.at[6, f - 2]
        for t in range(4):
            lanes = slice(128 * t, 128 * t + 128)
            v = pout[64 + 8 * f : 72 + 8 * f, lanes]
            for h in range(2):
                rows = pl.ds(h, 8, stride=2)
                v2f[f, t, rows, :] = second[t, rows, :] + v
            for row, k in zip((7, 24), corners(f)):
                vf[f, t, row : row + 1, :] = crn[1, k, t : t + 1, :] + pcor[k : k + 1, lanes]
    for f in range(4):
        if f < 2:
            k01, inside, rhs_f = kx[16 * f], px[1 + 15 * f, :, IN, :], xr[4, f]
        else:
            k01, inside, rhs_f = kyf[f - 2], ys[1, f - 2], yr[4, f - 2]
        c = vf[f, :, IN, :]
        z = kzf[f]
        total = k01 * inside + k12f[f] * v2f[f]
        total = total + ktf[f, :, LO, :] * vf[f, :, LO, :] + ktf[f, :, IN, :] * vf[f, :, HI, :]
        total = total + z * fine_next(c) + fine_before(z * c)
        uf[f] = wf[f] * (rhs_f + total) - INV * c

    for f in range(2):
        face = gxf[f] * uf[f]
        dl[f] = gyf[f] * uf[2 + f]
        for t in range(4):
            lanes = slice(128 * t, 128 * t + 128)
            out[15 * f, :, lanes] = out[15 * f, :, lanes] + face[t]
    for x in range(16):
        for f in range(2):
            for t in range(4):
                lanes = slice(128 * t, 128 * t + 128)
                k = 15 * f
                out[x, k : k + 1, lanes] = out[x, k : k + 1, lanes] + dl[f, t, x : x + 1, :]


def solution(mesh):
    nx, ny = mesh.shape["gx"], mesh.shape["gy"]

    def local(p, d, m):
        vm = lambda *s: pltpu.VMEM(s, F32)
        sem = lambda *s: pltpu.SemaphoreType.DMA(s)
        plane = (16, 4, 16, 128)
        face = (4, 16, 128)
        scratch = [
            vm(18, 4, 32, 128), vm(18, 4, 32, 128), vm(18, 4, 32, 128), vm(18, 4, 32, 128),
            vm(*plane), vm(*plane), vm(*plane), vm(*plane),
            vm(17, 4, 16, 128), vm(16, 4, 32, 128), vm(*plane),
            vm(7, 2, *face), vm(7, 2, *face), vm(7, 2, *face),
            vm(2, *face), vm(2, *face), vm(2, *face), vm(2, *face), vm(64, 512),
            pltpu.VMEM((512, 256), BF16), pltpu.VMEM((256, 512), BF16), vm(96, 512),
            vm(2, 8, 2, 8, 128), vm(2, 2, 4, 2, 8, 128), vm(2, 2, 4, 2, 8, 128),
            vm(2, 2, 4, 2, 8, 128), vm(2, 2, 2, 2, 2, 8, 128),
            vm(16, 2, 32, 128), vm(16, 2, 32, 128), vm(16, 2, 16, 128), vm(16, 2, 16, 128),
            vm(17, 2, 16, 128), vm(16, 2, 32, 128), vm(16, 2, 16, 128),
            vm(16, 2, 32, 128), vm(16, 2, 32, 128), vm(16, 2, 16, 128), vm(16, 2, 16, 128),
            vm(16, 2, 16, 128),
            vm(3, 16, 128), vm(3, 8, 16, 128), vm(12, 16, 128), vm(12, 16, 128), vm(12, 16, 128),
            vm(12, 16, 128), vm(6, 16, 128),
            vm(8, 2, 8, 128), vm(2, 2, 8, 128), vm(4, 2, 8, 128), vm(4, 2, 8, 128),
            vm(nx, 2, 128), vm(ny, 2, 128),
            vm(2, 4, 4, 128), vm(2, 4, 4, 128), vm(4, 4, 32, 128), vm(4, *face), vm(4, 4, 32, 128),
            vm(4, *face), vm(4, *face), vm(4, *face), vm(4, *face), vm(4, 2, 128), vm(4, 2, 128),
            vm(2, 2, 2, 8, 128), vm(2, 2, 2, 8, 128), vm(2, 2, 2, 8, 128), vm(2, 2, 2, 8, 128),
            vm(4, 2, 8, 128), vm(4, 2, 8, 128), vm(8, 512),
            sem(3, 4), sem(9, 4), sem(9, 4), sem(2, 8), sem(2, 8), sem(3, 8), sem(3, 8),
            sem(12), sem(12), sem(nx), sem(nx), sem(ny), sem(ny),
        ]
        return pl.pallas_call(
            functools.partial(kernel, nx, ny),
            out_shape=jax.ShapeDtypeStruct((16, 16, 512), F32),
            in_specs=[pl.BlockSpec(memory_space=pl.ANY)] * 3,
            out_specs=pl.BlockSpec(memory_space=pltpu.VMEM),
            scratch_shapes=scratch,
            compiler_params=pltpu.CompilerParams(
                collective_id=0, has_side_effects=True, vmem_limit_bytes=30 * 1024 * 1024
            ),
        )(*[pltpu.with_memory_space_constraint(a, pltpu.HBM) for a in (p, d, m)])

    spec = P("gx", "gy", None)
    return jax.shard_map(
        local, mesh=mesh, in_specs=(spec, spec, spec), out_specs=spec, check_vma=False
    )
```

```python
import functools

import jax
import jax.numpy as jnp
from jax import lax
from jax.experimental import pallas as pl
from jax.experimental.pallas import tpu as pltpu
from jax.sharding import PartitionSpec as P

MESH = pl.DeviceIdType.MESH
F32 = jnp.float32
BF16 = jnp.bfloat16

S1 = 0.05
S2 = 0.2
S3 = 0.8
MIDPOINT = (2.0 + 0.3) / 2
HALFWIDTH = (2.0 - 0.3) / 2
SIGMA = MIDPOINT / HALFWIDTH
P1 = 1.0 / SIGMA
P2 = 1.0 / (2.0 * SIGMA - P1)
CA = P2 * P1
CB = 2.0 * P2 / HALFWIDTH
INV = 1.0 / MIDPOINT
ALPHA = CA + CB * (MIDPOINT - 1.0)
STEP = CB * MIDPOINT
BETA = 1.0 / CB - 1.0
GAMMA = CA / CB
NEAR = [(-1, 0), (1, 0), (0, -1), (0, 1), (-1, -1), (-1, 1), (1, -1), (1, 1)]


def thirds(x):
    high = x.astype(BF16)
    rest = x - high.astype(F32)
    middle = rest.astype(BF16)
    low = (rest - middle.astype(F32)).astype(BF16)
    return high, middle, low


def exact_dot(x, matrix):
    total = None
    for part in thirds(x):
        term = jnp.dot(part, matrix, preferred_element_type=F32)
        total = term if total is None else total + term
    return total


def weighted_sum(f):
    q = pltpu.roll(f, 1, 2) + pltpu.roll(f, f.shape[2] - 1, 2)
    face = 0.5 * f + 0.125 * q
    edge = 0.125 * f + 0.0625 * q
    rows = f.shape[1]
    a = 0.5 * q + (pltpu.roll(face, 1, 1) + pltpu.roll(face, rows - 1, 1))
    b = face + (pltpu.roll(edge, 1, 1) + pltpu.roll(edge, rows - 1, 1))
    return a[1:-1] + (b[:-2] + b[2:])


def coarse_operator(v, mob, mob_sum):
    c = v[1:-1]
    m = mob[1:-1]
    return S3 * c + 0.5 * (
        5.0 * m * c - m * weighted_sum(v) + c * mob_sum - weighted_sum(mob * v)
    )


def fine_next(v):
    turned = pltpu.roll(v, 127, 2)
    lane = lax.broadcasted_iota(jnp.int32, v.shape, 2)
    return jnp.where(lane == 127, jnp.concatenate([turned[1:], turned[:1]], axis=0), turned)


def fine_before(v):
    turned = pltpu.roll(v, 1, 2)
    lane = lax.broadcasted_iota(jnp.int32, v.shape, 2)
    return jnp.where(lane == 0, jnp.concatenate([turned[3:], turned[:3]], axis=0), turned)


def mid_next(v):
    return jnp.concatenate([v[1:], pltpu.roll(v[:1], 127, 2)], axis=0)


def mid_before(v):
    return jnp.concatenate([pltpu.roll(v[1:], 1, 2), v[:1]], axis=0)


def kernel(
    nx, ny,
    p_hbm, d_hbm, m_hbm, out,
    px, mf, u, u2, d, g, dg, w, kx, ky, kz,
    xr, ys, yr, kyf, gyf, gxf, dl, rs, tmat, pmat, pout,
    mid_b, mid_stage, mid_rx, mid_ry, mid_rc, b2, m2, w2, d2, kx2, ky2, kz2,
    va, vb, rr, x2, xk,
    cstage, crecv, cm, cw, cb, ce, t2,
    base, fstage, frecv, fk,
    ar1, ar2,
    cst, crn, vf, v2f, ktf, k12f, kzf, wf, uf, bcs, bcr,
    nst, nrx, nry, nrc, ring, ringr, pcor,
    in_sem, fs, fr, ms, mr, cs, cr, xs, xrs, as1, ar1s, as2, ar2s,
):
    gx = lax.axis_index("gx")
    gy = lax.axis_index("gy")
    IN = slice(8, 24)
    LO = slice(7, 23)
    HI = slice(9, 25)

    def device(ox, oy):
        return (lax.rem(gx + (ox % nx), nx), lax.rem(gy + (oy % ny), ny))

    peers = {(o, 0) for o in range(1, nx)} | {(0, o) for o in range(1, ny)}
    peers |= {(dx % nx, dy % ny) for dx, dy in NEAR}
    peers = sorted(peers - {(0, 0)})

    loads = []
    for n, (src, dst) in enumerate(
        ((m_hbm, mf.at[1:17, :, IN, :]), (p_hbm, px.at[1:17, :, IN, :]), (d_hbm, d))
    ):
        loads.append(
            [
                pltpu.make_async_copy(
                    src.at[:, :, 128 * t : 128 * t + 128], dst.at[:, t], in_sem.at[n, t]
                )
                for t in range(4)
            ]
        )
        for c in loads[-1]:
            c.start()
    barrier = pltpu.get_barrier_semaphore()
    for ox, oy in peers:
        pl.semaphore_signal(barrier, inc=1, device_id=device(ox, oy), device_id_type=MESH)

    def remote(src, dst, ssem, rsem, ox, oy):
        return pltpu.make_async_remote_copy(
            src_ref=src, dst_ref=dst, send_sem=ssem, recv_sem=rsem,
            device_id=device(ox, oy), device_id_type=MESH,
        )

    def planes(start, stop, width, body):
        def several(j, carry):
            for q in range(width):
                body(start + width * j + q)
            return carry

        lax.fori_loop(0, (stop - start) // width, several, 0)

    zeros = jnp.zeros((4, 8, 128), F32)
    rims = (mf, px, u, u2)
    for a in rims:
        for plane in (0, 17):
            a[plane, :, 8:16, :] = zeros
            a[plane, :, 16:24, :] = zeros

    def clear(i):
        for a in rims:
            a[i + 1, :, 0:8, :] = zeros
            a[i + 1, :, 24:32, :] = zeros
        ky[i, :, 0:8, :] = zeros

    planes(0, 16, 2, clear)

    zi = lax.broadcasted_iota(jnp.int32, tmat.shape, 0)
    ci = lax.broadcasted_iota(jnp.int32, tmat.shape, 1)
    hit = (zi >> 1) == (((ci & 127) << 1) + (ci >> 7))
    tmat[...] = jnp.where(hit, 1.0, 0.0).astype(BF16)
    zi = lax.broadcasted_iota(jnp.int32, pmat.shape, 1)
    ci = lax.broadcasted_iota(jnp.int32, pmat.shape, 0)
    hit = (zi >> 1) == (((ci & 127) << 1) + (ci >> 7))
    pmat[...] = jnp.where(hit, 1.0, 0.0).astype(BF16)

    def pack_rows(arr, n, layer=0, off=1, row=8):
        low, high = row + layer, row + 15 - layer
        for x in range(16):
            ys[n, 0, :, x : x + 1, :] = arr[x + off, :, low : low + 1, :]
            ys[n, 1, :, x : x + 1, :] = arr[x + off, :, high : high + 1, :]

    def fine_send(arr, n, layer=0, off=1, row=8):
        rows = slice(row, row + 16)
        low, high = arr.at[off + layer, :, rows, :], arr.at[off + 15 - layer, :, rows, :]
        copies = [
            remote(low, xr.at[n, 1], fs.at[n, 0], fr.at[n, 0], -1, 0),
            remote(high, xr.at[n, 0], fs.at[n, 1], fr.at[n, 1], 1, 0),
            remote(ys.at[n, 0], yr.at[n, 1], fs.at[n, 2], fr.at[n, 2], 0, -1),
            remote(ys.at[n, 1], yr.at[n, 0], fs.at[n, 3], fr.at[n, 3], 0, 1),
        ]
        for c in copies:
            c.start()
        return copies

    def wait(copies):
        for c in copies:
            c.wait()

    def wait_sent(copies):
        for c in copies:
            c.wait_send()

    def wait_arrived(copies):
        for c in copies:
            c.wait_recv()

    def corner_send(arr, n):
        copies = []
        for k, (dx, dy) in enumerate(NEAR[4:]):
            x, y = 1 + 15 * (k // 2), 8 + 15 * (k % 2)
            for t in range(4):
                cst[n, k, t : t + 1, :] = arr[x, t, y : y + 1, :]
            copies.append(
                remote(cst.at[n, k], crn.at[n, 3 - k], fs.at[7 + n, k], fr.at[7 + n, k], dx, dy)
            )
            copies[-1].start()
        return copies

    def restrict_fine(arr, off, row, scale):
        for j in range(8):
            for t in range(4):
                total = None
                for q in range(2):
                    for h in range(2):
                        part = arr[2 * j + q + off, t, pl.ds(row + h, 8, stride=2), :]
                        total = part if total is None else total + part
                rs[8 * j : 8 * j + 8, 128 * t : 128 * t + 128] = total * scale
        return exact_dot(rs[...], tmat[...])

    def mid_put(n, got):
        blocks = []
        for x in range(8):
            rows = got[8 * x : 8 * x + 8]
            v = jnp.stack([rows[:, :128], rows[:, 128:]], axis=0)
            mid_b[n, x] = v
            blocks.append(v)
        return blocks

    def mid_fold(n, blocks):
        low = lax.broadcasted_iota(jnp.int32, (2, 8, 128), 1) < 4
        for t in range(4):
            a, b = blocks[2 * t], blocks[2 * t + 1]
            mid_stage[n, 0, t] = jnp.where(low, a, pltpu.roll(b, 4, 1))
            mid_stage[n, 1, t] = jnp.where(low, pltpu.roll(a, 4, 1), b)

    def rhs_send():
        for q in range(2):
            for k in range(4):
                for j in range(2):
                    nst[j, q, :, 2 * k : 2 * k + 2, :] = mid_b[
                        1, 4 * q + k, :, 6 * j : 6 * j + 2, :
                    ]
        copies = [
            remote(mid_b.at[1, 0:2], nrx.at[1], ms.at[1, 0], mr.at[1, 0], -1, 0),
            remote(mid_b.at[1, 6:8], nrx.at[0], ms.at[1, 1], mr.at[1, 1], 1, 0),
            remote(nst.at[0], nry.at[1], ms.at[1, 2], mr.at[1, 2], 0, -1),
            remote(nst.at[1], nry.at[0], ms.at[1, 3], mr.at[1, 3], 0, 1),
        ]
        k = 4
        for i, dx in enumerate((-1, 1)):
            for j, dy in enumerate((-1, 1)):
                copies.append(
                    remote(
                        nst.at[j, i], nrc.at[1 - i, 1 - j], ms.at[1, k], mr.at[1, k], dx, dy
                    )
                )
                k += 1
        for c in copies:
            c.start()
        return copies

    def rhs_place():
        for i in range(2):
            for x in range(2):
                plane = 2 + 10 * i + x
                b2[plane, :, 12:20, :] = nrx[i, x]
                at = 4 - 4 * i + 2 * x
                for j in range(2):
                    row = 10 + 10 * j
                    b2[plane, :, row : row + 2, :] = nrc[i, j, :, at : at + 2, :]
        for j in range(2):
            row = 10 + 10 * j
            for q in range(2):
                for k in range(4):
                    b2[4 + 4 * q + k, :, row : row + 2, :] = nry[j, q, :, 2 * k : 2 * k + 2, :]

    def mid_send(n):
        copies = [
            remote(mid_b.at[n, 0:3], mid_rx.at[n, 1, 0:3], ms.at[n, 0], mr.at[n, 0], -1, 0),
            remote(mid_b.at[n, 5:8], mid_rx.at[n, 0, 1:4], ms.at[n, 1], mr.at[n, 1], 1, 0),
            remote(mid_stage.at[n, 0], mid_ry.at[n, 1], ms.at[n, 2], mr.at[n, 2], 0, -1),
            remote(mid_stage.at[n, 1], mid_ry.at[n, 0], ms.at[n, 3], mr.at[n, 3], 0, 1),
        ]
        k = 4
        for i, dx in enumerate((-1, 1)):
            for j, dy in enumerate((-1, 1)):
                copies.append(
                    remote(
                        mid_stage.at[n, j, 2 * i : 2 * i + 2], mid_rc.at[n, 1 - i, 1 - j],
                        ms.at[n, k], mr.at[n, k], dx, dy,
                    )
                )
                k += 1
        for c in copies:
            c.start()
        return copies

    def mid_place(n, ext):
        for i in range(2):
            for x in range(1 - i, 4 - i):
                ext[12 * i + x, :, 12:20, :] = mid_rx[n, i, x]
            for t in range(4):
                for q in range(2):
                    ext[4 + 2 * t + q, :, 8 + 12 * i : 12 + 12 * i, :] = mid_ry[
                        n, i, t, :, 4 * q : 4 * q + 4, :
                    ]
            for j in range(2):
                for t in range(2):
                    for q in range(2):
                        ext[12 * i + 2 * t + q, :, 8 + 12 * j : 12 + 12 * j, :] = mid_rc[
                            n, i, j, t, :, 4 * q : 4 * q + 4, :
                        ]

    def mid_own(n, ext):
        for x in range(8):
            ext[4 + x, :, 12:20, :] = mid_b[n, x]

    def coarse_block(arr, n, row, scale):
        for x in range(4):
            total = None
            for q in range(2):
                for t in range(2):
                    for h in range(2):
                        part = arr[4 + 2 * x + q, t, pl.ds(row + h, 4, stride=2), :]
                        total = part if total is None else total + part
            cstage[n, 4 * x : 4 * x + 4, :] = total * scale

    def coarse_send(n):
        copies = []
        for k, (dx, dy) in enumerate(NEAR):
            copies.append(
                remote(cstage.at[n], crecv.at[n, k], cs.at[n, k], cr.at[n, k], dx, dy)
            )
            copies[-1].start()
        return copies

    def coarse_wait(copies, n, ext):
        def place(dx, dy, block):
            for x in range(4):
                ext[4 * dx + 4 + x, 4 * dy + 4 : 4 * dy + 8, :] = block[4 * x : 4 * x + 4, :]

        place(0, 0, cstage.at[n])
        wait(copies)
        for k, (dx, dy) in enumerate(NEAR):
            place(-dx, -dy, crecv.at[n, k])

    def fine_sum(arr, i):
        c = arr[i + 1, :, IN, :]
        z = kz[i]
        total = kx[i] * arr[i, :, IN, :] + kx[i + 1] * arr[i + 2, :, IN, :]
        total = total + ky[i, :, LO, :] * arr[i + 1, :, LO, :]
        total = total + ky[i, :, IN, :] * arr[i + 1, :, HI, :]
        return c, total + z * fine_next(c) + fine_before(z * c)

    def mid_sum(arr, i):
        c = arr[i, :, IN, :]
        z = kz2[i]
        total = kx2[i] * arr[i - 1, :, IN, :] + kx2[i + 1] * arr[i + 1, :, IN, :]
        total = total + ky2[i, :, LO, :] * arr[i, :, LO, :]
        total = total + ky2[i, :, IN, :] * arr[i, :, HI, :]
        return c, total + z * mid_next(c) + mid_before(z * c)

    def add_rows(arr, off, row):
        for x in range(16):
            for f in range(2):
                k = row + 15 * f
                arr[x + off, :, k : k + 1, :] = (
                    arr[x + off, :, k : k + 1, :] + dl[f, :, x : x + 1, :]
                )

    wait(loads[0])
    pack_rows(mf, 0)
    mid_fold(0, mid_put(0, restrict_fine(mf, 1, 8, 0.125)))
    wait(loads[1])
    pack_rows(px, 1)
    wait(loads[2])
    pl.semaphore_wait(barrier, len(peers))
    m_copies = fine_send(mf, 0)
    p_copies = fine_send(px, 1)

    def coefficients(i):
        c = mf[i + 1, :, IN, :]
        below = 0.5 * (c + mf[i, :, IN, :])
        above = c + mf[i + 2, :, IN, :]
        left = c + mf[i + 1, :, LO, :]
        right = 0.5 * (c + mf[i + 1, :, HI, :])
        after = 0.5 * (c + fine_next(c))
        before = c + fine_before(c)
        kx[i] = below
        ky[i, :, IN, :] = right
        kz[i] = after
        dg[i] = (S1 + below + right + after) + 0.5 * (above + left + before)

    planes(0, 16, 4, coefficients)
    kx[16] = 0.5 * mf[16, :, IN, :]

    def first_sum(i):
        c, total = fine_sum(px, i)
        g[i] = d[i] + total

    planes(0, 16, 8, first_sum)
    pack_rows(d, 4, 0, 0, 0)
    pack_rows(mf, 5, 1)
    wait_sent(m_copies)
    wait_sent(p_copies)
    m2_copies = mid_send(0)

    wait_arrived(m_copies)
    for f in range(2):
        face = 0.5 * xr[0, f]
        kx[16 * f] = kx[16 * f] + face
        dg[15 * f] = dg[15 * f] + face
        face = 0.5 * yr[0, f]
        kyf[f] = 0.5 * ys[0, f] + face
        dl[f] = face
    add_rows(dg, 0, 0)
    wait_arrived(p_copies)
    for f in range(2):
        g[15 * f] = g[15 * f] + kx[16 * f] * xr[1, f]
        dl[f] = kyf[f] * yr[1, f]
    add_rows(g, 0, 0)

    def first_step(i):
        weight = INV / dg[i]
        w[i] = weight
        u[i + 1, :, IN, :] = weight * g[i] - INV * px[i + 1, :, IN, :]

    planes(0, 16, 8, first_step)
    pack_rows(u, 2)
    u_copies = fine_send(u, 2)

    def second_sum(i):
        c, total = fine_sum(u, i)
        u2[i + 1, :, IN, :] = ALPHA * c + STEP * (w[i] * total)

    planes(0, 16, 8, second_sum)
    wait_sent(u_copies)
    for x in range(16):
        for f in range(2):
            gyf[f, :, x : x + 1, :] = w[x, :, 15 * f : 15 * f + 1, :]
    for f in range(2):
        gyf[f] = STEP * (gyf[f] * kyf[f])
        gxf[f] = STEP * (w[15 * f] * kx[16 * f])
    mid_own(0, m2)
    wait(m2_copies)
    mid_place(0, m2)
    coarse_block(m2, 0, 12, 0.125)
    m3_copies = coarse_send(0)

    wait_arrived(u_copies)
    for f in range(2):
        k = 1 + 15 * f
        u2[k, :, IN, :] = u2[k, :, IN, :] + gxf[f] * xr[2, f]
        dl[f] = gyf[f] * yr[2, f]
    add_rows(u2, 1, 8)
    pack_rows(u2, 3)
    u2_copies = fine_send(u2, 3)

    def third_sum(i):
        c, total = fine_sum(u2, i)
        before = u[i + 1, :, IN, :]
        g[i] = dg[i] * (BETA * c - GAMMA * before) + total
        px[i + 1, :, IN, :] = px[i + 1, :, IN, :] + before + c

    planes(0, 16, 8, third_sum)
    wait_sent(u2_copies)

    def mid_coefficients(i):
        c = m2[i, :, IN, :]
        below = 0.5 * (c + m2[i - 1, :, IN, :])
        above = 0.5 * (c + m2[i + 1, :, IN, :])
        left = c + m2[i, :, LO, :]
        right = 0.5 * (c + m2[i, :, HI, :])
        after = 0.5 * (c + mid_next(c))
        before = c + mid_before(c)
        kx2[i] = below
        kx2[i + 1] = above
        ky2[i, :, IN, :] = right
        kz2[i] = after
        diagonal = (S2 + below + above + right + after) + 0.5 * (left + before)
        d2[i] = diagonal
        w2[i] = INV / diagonal

    planes(2, 14, 6, mid_coefficients)
    coarse_wait(m3_copies, 0, cm)
    mob = cm[...]
    lap = weighted_sum(mob)
    cw[1:11] = 0.8 / (S3 + 0.5 * (5.0 * mob[1:-1] + lap))
    for x in range(4):
        cstage[1, 4 * x : 4 * x + 4, :] = cw[4 + x, 4:8, :]
    w3_copies = coarse_send(1)

    wait_arrived(u2_copies)
    for f in range(2):
        g[15 * f] = g[15 * f] + kx[16 * f] * xr[3, f]
        dl[f] = kyf[f] * yr[3, f]
    add_rows(g, 0, 0)
    mid_put(1, restrict_fine(g, 0, 0, 0.5))
    b2_copies = rhs_send()

    pack_rows(px, 6, 1)
    def response_one(i):
        vb[i, :, IN, :] = (-S2) * w2[i]

    planes(2, 14, 6, response_one)

    def response_two(i):
        c, total = mid_sum(vb, i)
        xk[i] = 1.0 + (1.0 + ALPHA) * c + STEP * (w2[i] * total)

    planes(3, 13, 5, response_two)
    for x in range(8):
        fk[2, :, x : x + 1, :] = xk[4 + x, :, 3:4, :]
        fk[3, :, x : x + 1, :] = xk[4 + x, :, 12:13, :]
    fk[0] = xk[3, :, 4:12, :]
    fk[1] = xk[12, :, 4:12, :]
    coarse_wait(w3_copies, 1, cw)
    weight = cw[...]
    y = jnp.ones_like(weight)
    psi = y
    for k in range(3):
        inner = slice(k, 12 - k)
        y = y[1:-1] - coarse_operator(weight[inner] * y, mob[inner], lap[k : 10 - k])
        psi = psi[1:-1] + y
    ce[0:4] = 1.0 - S3 * (weight[4:8] * psi[1:5])
    for f in range(2):
        xr[1, f] = xr[1, f] + xr[2, f] + xr[3, f]
        yr[1, f] = yr[1, f] + yr[2, f] + yr[3, f]
    mid_own(1, b2)
    wait_sent(b2_copies)
    x1_copies = fine_send(px, 6, 1) + corner_send(px, 1)
    wait_arrived(b2_copies)
    rhs_place()

    def mid_one(i):
        va[i, :, IN, :] = w2[i] * b2[i, :, IN, :]

    planes(2, 14, 6, mid_one)

    def mid_two(i):
        c, total = mid_sum(va, i)
        step = ALPHA * c + STEP * (w2[i] * total)
        vb[i, :, IN, :] = step
        x2[i] = c + step

    planes(3, 13, 5, mid_two)

    def mid_three(i):
        c, total = mid_sum(vb, i)
        rr[i] = d2[i] * (BETA * c - GAMMA * va[i, :, IN, :]) + total

    planes(4, 12, 4, mid_three)
    coarse_block(rr, 2, 4, 0.5)
    b3_copies = coarse_send(2)
    part = jnp.zeros((1, 128), F32)
    partm = jnp.zeros((1, 128), F32)
    for x in range(4):
        part = part + jnp.sum(
            ce[x, 4:8, :] * cstage[2, 4 * x : 4 * x + 4, :], axis=0, keepdims=True
        )
        partm = partm + jnp.sum(cstage[0, 4 * x : 4 * x + 4, :], axis=0, keepdims=True)
    ar1[0, 0:1, :] = part
    ar1[0, 1:2, :] = partm
    sums = []
    for o in range(1, nx):
        sums.append(remote(ar1.at[0], ar1.at[o], as1.at[o], ar1s.at[o], o, 0))
        sums[-1].start()

    for f in range(2):
        k = 5 + 5 * f
        ring[f] = x2[k, :, 4:12, :]
        for x in range(8):
            ring[2 + f, :, x : x + 1, :] = x2[4 + x, :, k : k + 1, :]
    ring_copies = [
        remote(ring.at[f], ringr.at[f + 1 - 2 * (f % 2)], xs.at[8 + f], xrs.at[8 + f], ox, oy)
        for f, (ox, oy) in enumerate(NEAR[:4])
    ]
    for c in ring_copies:
        c.start()

    d_copies = fine_send(d, 4, 0, 0, 0)
    far_copies = fine_send(mf, 5, 1) + corner_send(mf, 0)
    coarse_wait(b3_copies, 2, cb)
    rhs = cb[...]
    e = weight * rhs
    for k in range(3):
        inner = slice(k, 12 - k)
        e = e[1:-1] + weight[k + 1 : 11 - k] * (
            rhs[k + 1 : 11 - k] - coarse_operator(e, mob[inner], lap[k : 10 - k])
        )
    wait(sums)
    total = ar1[0]
    for o in range(1, nx):
        total = total + ar1[o]
    ar2[0] = total
    sums = []
    for o in range(1, ny):
        sums.append(remote(ar2.at[0], ar2.at[o], as2.at[o], ar2s.at[o], 0, o))
        sums[-1].start()

    wait(ring_copies)
    for f in range(2):
        x2[2 + 11 * f, :, 4:12, :] = ringr[f]
        row = 2 + 11 * f
        for x in range(8):
            x2[4 + x, :, row : row + 1, :] = ringr[2 + f, :, x : x + 1, :]
    ce[3:9] = e
    for x in range(6):
        for h in range(2):
            t2[x, pl.ds(h, 8, stride=2), :] = ce[3 + x, 2:10, :]
    for x in range(6):
        v = t2[x]
        both = jnp.stack([v, v], axis=0)
        for q in range(2):
            va[2 + 2 * x + q, :, IN, :] = x2[2 + 2 * x + q] + both

    def post_one(i):
        c, total = mid_sum(va, i)
        vb[i, :, IN, :] = w2[i] * (b2[i, :, IN, :] + total) - INV * c

    planes(3, 13, 5, post_one)

    def post_two(i):
        c, total = mid_sum(vb, i)
        done = va[i, :, IN, :] + (1.0 + ALPHA) * c + STEP * (w2[i] * total)
        base[i - 4] = done[:, 4:12, :]

    planes(4, 12, 4, post_two)
    for x in range(8):
        fstage[0, :, x : x + 1, :] = base[x, :, 0:1, :]
        fstage[1, :, x : x + 1, :] = base[x, :, 7:8, :]
    x_copies = [
        remote(base.at[0], frecv.at[1], xs.at[0], xrs.at[0], -1, 0),
        remote(base.at[7], frecv.at[0], xs.at[1], xrs.at[1], 1, 0),
        remote(fstage.at[0], frecv.at[3], xs.at[2], xrs.at[2], 0, -1),
        remote(fstage.at[1], frecv.at[2], xs.at[3], xrs.at[3], 0, 1),
    ]
    for k, (dx, dy) in enumerate(NEAR[4:]):
        x, y = 7 * (k // 2), 7 * (k % 2)
        for t in range(2):
            bcs[k, t : t + 1, :] = base[x, t, y : y + 1, :]
        x_copies.append(
            remote(bcs.at[k], bcr.at[3 - k], xs.at[4 + k], xrs.at[4 + k], dx, dy)
        )
    for c in x_copies:
        c.start()

    wait(d_copies)
    wait(far_copies)

    def corners(f):
        return ((0, 1), (2, 3), (0, 2), (1, 3))[f]

    for f in range(4):
        first, second = (xr.at[0, f], xr.at[5, f]) if f < 2 else (yr.at[0, f - 2], yr.at[5, f - 2])
        k01 = kx[16 * f] if f < 2 else kyf[f - 2]
        c = first[...]
        vf[f, :, IN, :] = c
        for row, k in zip((7, 24), corners(f)):
            for t in range(4):
                vf[f, t, row : row + 1, :] = crn[0, k, t : t + 1, :]
        ktf[f, :, IN, :] = 0.5 * (c + vf[f, :, HI, :])
        ktf[f, :, 7:8, :] = 0.5 * (vf[f, :, 7:8, :] + vf[f, :, 8:9, :])
        k12 = 0.5 * (c + second[...])
        after = 0.5 * (c + fine_next(c))
        k12f[f] = k12
        kzf[f] = after
        wf[f] = INV / (
            S1 + k01 + k12 + ktf[f, :, IN, :] + ktf[f, :, LO, :] + after + fine_before(after)
        )

    wait(sums)
    total = ar2[0]
    for o in range(1, ny):
        total = total + ar2[o]
    cells = 16.0 * 128.0 * nx * ny
    sum_f = jnp.sum(total[0:1, :], axis=1, keepdims=True)
    sum_m = jnp.sum(total[1:2, :], axis=1, keepdims=True)
    kappa = 0.8 * (sum_f / cells) / (S3 + 5.0 * (sum_m / cells))

    for x in range(8):
        v = base[x] + kappa * xk[4 + x, :, 4:12, :]
        pout[8 * x : 8 * x + 8, 0:128] = v[0]
        pout[8 * x : 8 * x + 8, 128:256] = v[1]
    wait(x_copies[:4])
    for f in range(4):
        v = frecv[f] + kappa * fk[f]
        pout[64 + 8 * f : 72 + 8 * f, 0:128] = v[0]
        pout[64 + 8 * f : 72 + 8 * f, 128:256] = v[1]
    pout[...] = exact_dot(pout[:, 0:256], pmat[...])

    wait_sent(x1_copies)
    for j in range(8):
        for t in range(4):
            v = pout[8 * j : 8 * j + 8, 128 * t : 128 * t + 128]
            for q in range(2):
                for h in range(2):
                    rows = pl.ds(8 + h, 8, stride=2)
                    px[2 * j + 1 + q, t, rows, :] = px[2 * j + 1 + q, t, rows, :] + v
    for f in range(4):
        first = xr.at[1, f] if f < 2 else yr.at[1, f - 2]
        for t in range(4):
            lanes = slice(128 * t, 128 * t + 128)
            v = pout[64 + 8 * f : 72 + 8 * f, lanes]
            for h in range(2):
                rows = pl.ds(h, 8, stride=2)
                vf[f, t, pl.ds(8 + h, 8, stride=2), :] = first[t, rows, :] + v
    pack_rows(px, 1)
    for f in range(2):
        d[15 * f] = d[15 * f] + kx[16 * f] * vf[f, :, IN, :]
        dl[f] = kyf[f] * vf[2 + f, :, IN, :]
    add_rows(d, 0, 0)

    def fourth_sum(i):
        c, total = fine_sum(px, i)
        u[i + 1, :, IN, :] = w[i] * (d[i] + total) - INV * c

    planes(0, 16, 8, fourth_sum)

    def last_sum(i):
        c, total = fine_sum(u, i)
        done = px[i + 1, :, IN, :] + (1.0 + ALPHA) * c + STEP * (w[i] * total)
        for t in range(4):
            out[i, :, 128 * t : 128 * t + 128] = done[t]

    planes(0, 16, 8, last_sum)

    wait_arrived(x1_copies)
    wait(x_copies[4:])
    for k in range(4):
        x, y = 3 + 9 * (k // 2), 3 + 9 * (k % 2)
        for t in range(2):
            pcor[k : k + 1, 128 * t : 128 * t + 128] = (
                bcr[k, t : t + 1, :] + kappa * xk[x, t, y : y + 1, :]
            )
    pcor[...] = exact_dot(pcor[:, 0:256], pmat[...])
    for f in range(4):
        second = xr.at[6, f] if f < 2 else yr.at[6, f - 2]
        for t in range(4):
            lanes = slice(128 * t, 128 * t + 128)
            v = pout[64 + 8 * f : 72 + 8 * f, lanes]
            for h in range(2):
                rows = pl.ds(h, 8, stride=2)
                v2f[f, t, rows, :] = second[t, rows, :] + v
            for row, k in zip((7, 24), corners(f)):
                vf[f, t, row : row + 1, :] = crn[1, k, t : t + 1, :] + pcor[k : k + 1, lanes]
    for f in range(4):
        if f < 2:
            k01, inside, rhs_f = kx[16 * f], px[1 + 15 * f, :, IN, :], xr[4, f]
        else:
            k01, inside, rhs_f = kyf[f - 2], ys[1, f - 2], yr[4, f - 2]
        c = vf[f, :, IN, :]
        z = kzf[f]
        total = k01 * inside + k12f[f] * v2f[f]
        total = total + ktf[f, :, LO, :] * vf[f, :, LO, :] + ktf[f, :, IN, :] * vf[f, :, HI, :]
        total = total + z * fine_next(c) + fine_before(z * c)
        uf[f] = wf[f] * (rhs_f + total) - INV * c

    for f in range(2):
        face = gxf[f] * uf[f]
        dl[f] = gyf[f] * uf[2 + f]
        for t in range(4):
            lanes = slice(128 * t, 128 * t + 128)
            out[15 * f, :, lanes] = out[15 * f, :, lanes] + face[t]
    for x in range(16):
        for f in range(2):
            for t in range(4):
                lanes = slice(128 * t, 128 * t + 128)
                k = 15 * f
                out[x, k : k + 1, lanes] = out[x, k : k + 1, lanes] + dl[f, t, x : x + 1, :]


def solution(mesh):
    nx, ny = mesh.shape["gx"], mesh.shape["gy"]

    def local(p, d, m):
        vm = lambda *s: pltpu.VMEM(s, F32)
        sem = lambda *s: pltpu.SemaphoreType.DMA(s)
        plane = (16, 4, 16, 128)
        face = (4, 16, 128)
        scratch = [
            vm(18, 4, 32, 128), vm(18, 4, 32, 128), vm(18, 4, 32, 128), vm(18, 4, 32, 128),
            vm(*plane), vm(*plane), vm(*plane), vm(*plane),
            vm(17, 4, 16, 128), vm(16, 4, 32, 128), vm(*plane),
            vm(7, 2, *face), vm(7, 2, *face), vm(7, 2, *face),
            vm(2, *face), vm(2, *face), vm(2, *face), vm(2, *face), vm(64, 512),
            pltpu.VMEM((512, 256), BF16), pltpu.VMEM((256, 512), BF16), vm(96, 512),
            vm(2, 8, 2, 8, 128), vm(2, 2, 4, 2, 8, 128), vm(2, 2, 4, 2, 8, 128),
            vm(2, 2, 4, 2, 8, 128), vm(2, 2, 2, 2, 2, 8, 128),
            vm(16, 2, 32, 128), vm(16, 2, 32, 128), vm(16, 2, 16, 128), vm(16, 2, 16, 128),
            vm(17, 2, 16, 128), vm(16, 2, 32, 128), vm(16, 2, 16, 128),
            vm(16, 2, 32, 128), vm(16, 2, 32, 128), vm(16, 2, 16, 128), vm(16, 2, 16, 128),
            vm(16, 2, 16, 128),
            vm(3, 16, 128), vm(3, 8, 16, 128), vm(12, 16, 128), vm(12, 16, 128), vm(12, 16, 128),
            vm(12, 16, 128), vm(6, 16, 128),
            vm(8, 2, 8, 128), vm(2, 2, 8, 128), vm(4, 2, 8, 128), vm(4, 2, 8, 128),
            vm(nx, 2, 128), vm(ny, 2, 128),
            vm(2, 4, 4, 128), vm(2, 4, 4, 128), vm(4, 4, 32, 128), vm(4, *face), vm(4, 4, 32, 128),
            vm(4, *face), vm(4, *face), vm(4, *face), vm(4, *face), vm(4, 2, 128), vm(4, 2, 128),
            vm(2, 2, 2, 8, 128), vm(2, 2, 2, 8, 128), vm(2, 2, 2, 8, 128), vm(2, 2, 2, 8, 128),
            vm(4, 2, 8, 128), vm(4, 2, 8, 128), vm(8, 512),
            sem(3, 4), sem(9, 4), sem(9, 4), sem(2, 8), sem(2, 8), sem(3, 8), sem(3, 8),
            sem(12), sem(12), sem(nx), sem(nx), sem(ny), sem(ny),
        ]
        return pl.pallas_call(
            functools.partial(kernel, nx, ny),
            out_shape=jax.ShapeDtypeStruct((16, 16, 512), F32),
            in_specs=[pl.BlockSpec(memory_space=pl.ANY)] * 3,
            out_specs=pl.BlockSpec(memory_space=pltpu.VMEM),
            scratch_shapes=scratch,
            compiler_params=pltpu.CompilerParams(
                collective_id=0, has_side_effects=True, vmem_limit_bytes=30 * 1024 * 1024
            ),
        )(*[pltpu.with_memory_space_constraint(a, pltpu.HBM) for a in (p, d, m)])

    spec = P("gx", "gy", None)
    return jax.shard_map(
        local, mesh=mesh, in_specs=(spec, spec, spec), out_specs=spec, check_vma=False
    )
```
